128 devices in a mesh: rep: 4 (over y), shard: 32 (over x, z, core).
Axes of the slice: x: 4, y: 4, z: 4, core: 2. Of those that a mesh axis runs over, the one named last changes fastest.
Arguments:
- short_tokens: bfloat16 [256, 64, 768], P(('rep', 'shard')), may hold values from -6 to 6
- long_tokens: bfloat16 [256, 256, 768], P(('rep', 'shard')), may hold values from -6 to 6
- short_lengths: int32 [256], P(('rep', 'shard')), may hold values from 16 to 64
- long_lengths: int32 [256], P(('rep', 'shard')), may hold values from 65 to 256
- short_cotangent: bfloat16 [256, 64, 768], P(('rep', 'shard')), may hold values from -6 to 6
- long_cotangent: bfloat16 [256, 256, 768], P(('rep', 'shard')), may hold values from -6 to 6
- input_weight: bfloat16 [768, 2304], P('shard'), may hold values from -0.21875 to 0.21875
- query_bias: bfloat16 [768], P('shard'), may hold values from -3 to 3
- value_bias: bfloat16 [768], P('shard'), may hold values from -1.1953125 to 1.1953125
- output_weight: bfloat16 [768, 768], P('shard'), may hold values from -0.625 to 0.625
- output_bias: bfloat16 [768], P('shard'), may hold values from -1.1953125 to 1.1953125
- first_gain: bfloat16 [768], P('shard'), may hold values from 0.5 to 1.5
- first_shift: bfloat16 [768], P('shard'), may hold values from -1.1953125 to 1.1953125
- up_weight: bfloat16 [768, 3072], P('shard'), may hold values from -0.21875 to 0.21875
- up_bias: bfloat16 [3072], P('shard'), may hold values from -3 to 3
- down_weight: bfloat16 [3072, 768], P('shard'), may hold values from -0.109375 to 0.109375
- down_bias: bfloat16 [768], P('shard'), may hold values from -1.1953125 to 1.1953125
- second_gain: bfloat16 [768], P('shard'), may hold values from 0.5 to 1.5
- second_shift: bfloat16 [768], P('shard'), may hold values from -1.1953125 to 1.1953125
Outputs:
- short_out: bfloat16 [256, 64, 768], P(('rep', 'shard'))
- long_out: bfloat16 [256, 256, 768], P(('rep', 'shard'))
- short_grad: float32 [256, 64, 768], P(('rep', 'shard'))
- long_grad: float32 [256, 256, 768], P(('rep', 'shard'))
- grad_input_weight: float32 [768, 2304], P('shard')
- grad_query_bias: float32 [768], P('shard')
- grad_value_bias: float32 [768], P('shard')
- grad_output_weight: float32 [768, 768], P('shard')
- grad_output_bias: float32 [768], P('shard')
- grad_first_gain: float32 [768], P('shard')
- grad_first_shift: float32 [768], P('shard')
- grad_up_weight: float32 [768, 3072], P('shard')
- grad_up_bias: float32 [3072], P('shard')
- grad_down_weight: float32 [3072, 768], P('shard')
- grad_down_bias: float32 [768], P('shard')
- grad_second_gain: float32 [768], P('shard')
- grad_second_shift: float32 [768], P('shard')
The draws below stay inside these ranges and needn't reach their ends.
All inputs are finite; a program needn't handle non-finite values.
Results may differ from the reference program's by a relative error of at most 0.025.
Values may be sent and summed in bfloat16 or wider, within the bound.
No kernel may reach another device: no remote copies, remote signals or barrier semaphores. Data moves between devices by JAX's collectives and lax.ppermute only.
A program may use at most 192 MiB of HBM per device.

```python
import math
import jax
import jax.numpy as jnp
from jax import lax

D = 768
HEADS = 12
HEAD_DIM = 64
FF = 3072
SHORT_LEN = 64
LONG_LEN = 256
SHORT_PASSAGES = 256
LONG_PASSAGES = 256


def touch_ends(values, key, least, top_value):
    dims = values.shape
    place = [jax.random.randint(jax.random.fold_in(key, axis), (), 0, dims[axis]) for axis in range(len(dims))]
    values = values.at[tuple(place)].set(least)
    longest = dims.index(max(dims))
    place[longest] = (place[longest] + 1) % dims[longest]
    return values.at[tuple(place)].set(top_value)


def steps_of(rng, extent, cuts, low, high):
    gain, own = 1.0, jax.random.fold_in(rng, 6)
    for axis_at, shards_of in cuts:
        draws = jnp.exp(jax.random.uniform(jax.random.fold_in(own, axis_at), (shards_of,), jnp.float32, low / len(cuts), high / len(cuts)))
        gain = gain * jnp.repeat(draws, extent[axis_at] // shards_of).reshape([-1 if axis == axis_at else 1 for axis in range(len(extent))])
    return gain


def scatter_about(rng, shape, width, reach, shards=(), kind=jnp.bfloat16):
    array = jax.random.normal(rng, shape, jnp.float32) * width
    if len(shards) > 0:
        array = steps_of(rng, shape, shards, -0.22, 0.18) * array
    return jnp.clip(array, min=-reach, max=reach).astype(kind)


def setup_inputs(seed: int = 0) -> dict:
    streams_of = jax.random.split(jax.random.key(seed), 20)
    short_tokens = scatter_about(streams_of[0], (SHORT_PASSAGES, SHORT_LEN, D), 1.0, 6.0, ((0, 128),))
    long_tokens = scatter_about(streams_of[1], (LONG_PASSAGES, LONG_LEN, D), 1.0, 6.0, ((0, 128),))
    short_lengths = touch_ends(jax.random.randint(streams_of[2], (SHORT_PASSAGES,), SHORT_LEN // 4, SHORT_LEN + 1), jax.random.fold_in(streams_of[2], 1), SHORT_LEN // 4, SHORT_LEN).astype(jnp.int32)
    long_lengths = touch_ends(jax.random.randint(streams_of[3], (LONG_PASSAGES,), SHORT_LEN + 1, LONG_LEN + 1), jax.random.fold_in(streams_of[3], 1), SHORT_LEN + 1, LONG_LEN).astype(jnp.int32)
    short_cotangent = scatter_about(streams_of[4], (SHORT_PASSAGES, SHORT_LEN, D), 1.0, 6.0, ((0, 128),))
    long_cotangent = scatter_about(streams_of[5], (LONG_PASSAGES, LONG_LEN, D), 1.0, 6.0, ((0, 128),))
    input_weight = scatter_about(streams_of[6], (D, 3 * D), D ** -0.5, 0.21875, ((0, 32),))
    query_bias = scatter_about(streams_of[7], (D,), 0.5, 3.0, ((0, 32),))
    value_bias = scatter_about(streams_of[8], (D,), 0.2, 1.1953125, ((0, 32),))
    output_weight = scatter_about(streams_of[9], (D, D), (D // 8) ** -0.5, 0.625, ((0, 32),))
    output_bias = scatter_about(streams_of[10], (D,), 0.2, 1.1953125, ((0, 32),))
    first_gain = jnp.clip(1.0 + 0.1 * jax.random.normal(streams_of[11], (D,), jnp.float32), 0.5, 1.5).astype(jnp.bfloat16)
    first_shift = scatter_about(streams_of[12], (D,), 0.2, 1.1953125, ((0, 32),))
    up_weight = scatter_about(streams_of[13], (D, FF), D ** -0.5, 0.21875, ((0, 32),))
    up_bias = scatter_about(streams_of[14], (FF,), 0.5, 3.0, ((0, 32),))
    down_weight = scatter_about(streams_of[15], (FF, D), FF ** -0.5, 0.109375, ((0, 32),))
    down_bias = scatter_about(streams_of[16], (D,), 0.2, 1.1953125, ((0, 32),))
    second_gain = jnp.clip(1.0 + 0.1 * jax.random.normal(streams_of[17], (D,), jnp.float32), 0.5, 1.5).astype(jnp.bfloat16)
    second_shift = scatter_about(streams_of[18], (D,), 0.2, 1.1953125, ((0, 32),))
    return {"short_tokens": short_tokens, "long_tokens": long_tokens, "short_lengths": short_lengths, "long_lengths": long_lengths, "short_cotangent": short_cotangent, "long_cotangent": long_cotangent, "input_weight": input_weight, "query_bias": query_bias, "value_bias": value_bias, "output_weight": output_weight, "output_bias": output_bias, "first_gain": first_gain, "first_shift": first_shift, "up_weight": up_weight, "up_bias": up_bias, "down_weight": down_weight, "down_bias": down_bias, "second_gain": second_gain, "second_shift": second_shift}


@jax.custom_vjp
def low(v):
    return lax.optimization_barrier(v.astype(jnp.bfloat16)).astype(jnp.float32)

@jax.custom_vjp
def low_back(v):
    return v

def low_keep(v):
    return (low(v), None)

def low_pass(kept, grad):
    return (grad,)

def back_keep(v):
    return (v, None)

def back_low(kept, grad):
    return (low(grad),)
low.defvjp(low_keep, low_pass)
low_back.defvjp(back_keep, back_low)
EPSILON = 1e-06

def layer_norm(hidden, norm_gain, norm_shift):
    center = hidden - lax.optimization_barrier(jnp.mean(hidden, axis=-1, keepdims=True))
    spread = lax.optimization_barrier(jnp.mean(center * center, axis=-1, keepdims=True))
    return center * lax.rsqrt(spread + EPSILON) * norm_gain + norm_shift

def product(left_side, right_side):
    return jnp.einsum('bld,de->ble', left_side, right_side, precision=lax.Precision.HIGHEST)

def attention(query_rows, key_rows, value_rows, valid_mask):
    batch_size, seq_length, row_width = query_rows.shape
    split = (batch_size, seq_length, HEADS, HEAD_DIM)
    raw_scores = jnp.einsum('bqhd,bkhd->bhqk', query_rows.reshape(split), key_rows.reshape(split), precision=lax.Precision.HIGHEST)
    scores = low_back(raw_scores * HEAD_DIM ** (-0.5))
    masked = jnp.where(valid_mask[:, None, None, :], scores, -1000000000.0)
    probs = low(jax.nn.softmax(masked, axis=-1))
    context = jnp.einsum('bhqk,bkhd->bqhd', probs, value_rows.reshape(split), precision=lax.Precision.HIGHEST)
    return low(low_back(context.reshape(batch_size, seq_length, row_width)))

def block(params, tokens, lengths):
    input_weight, query_bias, value_bias, output_weight, output_bias, first_gain, first_shift, up_weight, up_bias, down_weight, down_bias, second_gain, second_shift = params
    batch_size, seq_length, row_width = tokens.shape
    valid_mask = lax.broadcasted_iota(jnp.int32, (batch_size, seq_length), 1) < lengths[:, None].astype(jnp.int32)
    in_bias = jnp.concatenate([query_bias, jnp.zeros((row_width,), jnp.float32), value_bias])
    projected = low(low_back(product(low(tokens), input_weight) + in_bias))
    context = attention(projected[..., :row_width], projected[..., row_width:2 * row_width], projected[..., 2 * row_width:], valid_mask)
    attended = low_back(product(context, output_weight) + output_bias)
    first_out = layer_norm(tokens + attended, first_gain, first_shift)
    up_pre = low_back(product(low(first_out), up_weight) + up_bias)
    hidden = low(jax.nn.gelu(up_pre, approximate=False))
    ffn_out = low_back(product(hidden, down_weight) + down_bias)
    normed = layer_norm(first_out + ffn_out, second_gain, second_shift)
    return normed * valid_mask[..., None].astype(jnp.float32)

def run_bucket(params, tokens, lengths):
    count = tokens.shape[0]
    group_size = math.gcd(count, max(1, 4096 // tokens.shape[1]))
    stacked = tokens.reshape((count // group_size, group_size) + tokens.shape[1:])
    grouped_lengths = lengths.reshape(count // group_size, group_size)
    checked = jax.checkpoint(block)

    def scan_step(carry, pair):
        return (carry, checked(params, pair[0], pair[1]))
    unused, outputs = lax.scan(scan_step, jnp.zeros((), jnp.int32), (stacked, grouped_lengths))
    return outputs.reshape(tokens.shape)

def reference(short_tokens, long_tokens, short_lengths, long_lengths, short_cotangent, long_cotangent, input_weight, query_bias, value_bias, output_weight, output_bias, first_gain, first_shift, up_weight, up_bias, down_weight, down_bias, second_gain, second_shift):
    params = tuple((weight.astype(jnp.float32) for weight in (input_weight, query_bias, value_bias, output_weight, output_bias, first_gain, first_shift, up_weight, up_bias, down_weight, down_bias, second_gain, second_shift)))

    def forward(weights, short_rows, long_rows):
        return (run_bucket(weights, short_rows, short_lengths), run_bucket(weights, long_rows, long_lengths))
    outputs, pullback = jax.vjp(forward, params, short_tokens.astype(jnp.float32), long_tokens.astype(jnp.float32))
    grads, short_grad, long_grad = pullback((short_cotangent.astype(jnp.float32), long_cotangent.astype(jnp.float32)))
    return (outputs[0].astype(jnp.bfloat16), outputs[1].astype(jnp.bfloat16), short_grad, long_grad, grads[0], grads[1], grads[2], grads[3], grads[4], grads[5], grads[6], grads[7], grads[8], grads[9], grads[10], grads[11], grads[12])
```

```python
import functools

import jax
import jax.numpy as jnp
from jax import lax
from jax.experimental import pallas as pl
from jax.experimental.pallas import tpu as pltpu
from jax.sharding import PartitionSpec as P

F32 = jnp.float32
BF16 = jnp.bfloat16
HEAD_DIM = 64
PAIR = 128
EPSILON = 1e-06
QB, VB, OB, G1, S1, DB, G2, S2 = range(8)
VMEM_LIMIT = 56 * 1024 * 1024
RING = 4
CHIPS = RING * RING
SHARDS = 2 * CHIPS


def nn(a, b):
    return lax.dot_general(a, b, (((1,), (0,)), ((), ())), preferred_element_type=F32)


def nt(a, b):
    return lax.dot_general(a, b, (((1,), (1,)), ((), ())), preferred_element_type=F32)


def tn(a, b):
    return lax.dot_general(a, b, (((0,), (0,)), ((), ())), preferred_element_type=F32)


def iota(shape, dim):
    return lax.broadcasted_iota(jnp.int32, shape, dim)


def row_of(ref, i):
    return ref[i : i + 1, :].astype(F32)


def whole(*shape):
    return pl.BlockSpec(shape, lambda g, *_: (0,) * len(shape))


def params():
    return pltpu.CompilerParams(vmem_limit_bytes=VMEM_LIMIT)


def cost(flops, moved):
    return pl.CostEstimate(flops=int(flops), bytes_accessed=int(moved), transcendentals=0)


def places(pos, x, z):
    along_x, along_z = (x - pos[0]) & (RING - 1), (z - pos[1]) & (RING - 1)
    return along_x * RING + along_z, along_z * RING + along_x


def deal(keep, give, pos, value, at, each):
    first = pos[2] == 0
    for x in range(RING):
        for z in range(RING):
            p0, p1 = places(pos, x, z)
            low = 2 * (x * RING + z) * each
            even, odd = value[low : low + each], value[low + each : low + 2 * each]
            keep[jnp.where(first, p0, p1), at] = jnp.where(first, even, odd)
            give[jnp.where(first, p1, p0), at] = jnp.where(first, odd, even)


def spread(owners, width):
    each = width // owners
    at = iota((owners, width), 1)
    low = iota((owners, width), 0) * each
    return (at >= low) & (at < low + each)


def column_rest(rows, width, each):
    at = iota((rows, width), 1)
    return at - (at // each) * each


def two_heads(pair):
    low_half = iota(pair.shape, 1) < HEAD_DIM
    zero = jnp.zeros_like(pair)
    return jnp.concatenate([jnp.where(low_half, pair, zero), jnp.where(low_half, zero, pair)], axis=0)


def own_lanes(stack):
    half = stack.shape[0] // 2
    return jnp.where(iota((half, stack.shape[1]), 1) < HEAD_DIM, stack[:half], stack[half:])


def normalized(hidden):
    center = hidden - jnp.mean(hidden, axis=-1, keepdims=True)
    spread_of = jnp.mean(center * center, axis=-1, keepdims=True)
    inverse = lax.rsqrt(spread_of + EPSILON)
    return center * inverse, inverse


def norm_back(scaled, unit, inverse):
    return inverse * (
        scaled
        - jnp.mean(scaled, axis=-1, keepdims=True)
        - unit * jnp.mean(scaled * unit, axis=-1, keepdims=True)
    )


def segments(dims):
    short_rows, long_count, long_length, _ = dims
    return [(0, short_rows, None)] + [
        (short_rows + i * long_length, long_length, i) for i in range(long_count)
    ]


def key_bias(slen, llen, short_length, rows, long_at):
    key = iota((rows, rows), 0)
    if long_at is not None:
        return jnp.where(key < llen[long_at], 0.0, -1e9).astype(F32)
    query = iota((rows, rows), 1)
    keep = jnp.zeros((rows, rows), jnp.bool_)
    for p in range(rows // short_length):
        low, high = p * short_length, (p + 1) * short_length
        keep = keep | ((key >= low) & (key < low + slen[p]) & (query >= low) & (query < high))
    return jnp.where(keep, 0.0, -1e9).astype(F32)


def valid_rows(slen, llen, dims):
    short_rows, long_count, long_length, short_length = dims
    parts = []
    at = iota((short_length, 1), 0)
    for p in range(short_rows // short_length):
        parts.append((at < slen[p]).astype(F32))
    at = iota((long_length, 1), 0)
    for p in range(long_count):
        parts.append((at < llen[p]).astype(F32))
    return jnp.concatenate(parts, axis=0)


def pack_body(wqkv, wo, wup, wdown, *rest):
    vectors, out = rest[:-1], rest[-1]
    each, width = wo.shape
    slabs = wqkv.shape[1] // width
    for j in range(slabs):
        out[j * each : (j + 1) * each] = wqkv[:, j * width : (j + 1) * width]
    out[slabs * each : (slabs + 1) * each] = wo[...]
    base = (slabs + 1) * each
    slabs = wup.shape[1] // width
    for j in range(slabs):
        out[base + j * each : base + (j + 1) * each] = wup[:, j * width : (j + 1) * width]
    base += slabs * each
    out[base : base + wdown.shape[0]] = wdown[...]
    base += wdown.shape[0]
    out[base:] = jnp.zeros((8, width), BF16)
    for i, v in enumerate(vectors[:-1]):
        out[base : base + 1, i * each : (i + 1) * each] = v[...]
    out[base + 1 : base + 2, : vectors[-1].shape[1]] = vectors[-1][...]


def pack(wqkv, wo, wup, wdown, vectors, ub):
    each, width = wo.shape
    rows = each * (wqkv.shape[1] // width + 1 + wup.shape[1] // width) + wdown.shape[0] + 8
    return pl.pallas_call(
        pack_body,
        out_shape=jax.ShapeDtypeStruct((rows, width), BF16),
        compiler_params=params(),
        name="pack",
    )(wqkv, wo, wup, wdown, *[v[None] for v in vectors], ub[None])


def attention_forward_body(
    dims, slen, llen, xs, xl, wq, wk, wv, wo_block, small,
    q_o, k_o, v_o, c_o, ps_o, pl_o, n_o, r_o, low_o, vecs_o, ub_o,
    x_all, total, wo_all,
):
    step = pl.program_id(0)
    short_rows, width = dims[0], x_all.shape[1]
    cols = q_o.shape[1]

    @pl.when(step == 0)
    def _():
        x_all[:short_rows, :] = xs[...]
        x_all[short_rows:, :] = xl[...]
        total[...] = jnp.zeros_like(total)
        wo_all[...] = wo_block[...].reshape(width, width)
        packed = small[...]
        each = width // SHARDS
        line = packed[:, 0, : 8 * each + 64]
        rest = column_rest(line.shape[1], width, each)
        mine = spread(SHARDS, width)
        for i in range(8):
            pick = (iota(rest.shape, 0) == rest + i * each).astype(BF16)
            row = jnp.sum(jnp.where(mine, nn(line, pick), 0.0), axis=0, keepdims=True)
            vecs_o[i : i + 1] = row.astype(BF16)
        inner = ub_o.shape[1]
        line = packed[:, 1, :128]
        pick = (iota((128, inner), 0) == column_rest(128, inner, inner // SHARDS)).astype(BF16)
        row = jnp.sum(jnp.where(spread(SHARDS, inner), nn(line, pick), 0.0), axis=0, keepdims=True)
        ub_o[...] = row.astype(BF16)

    x = x_all[...]
    at_cols = pl.ds(pl.multiple_of(step * cols, cols), cols)
    q_o[...] = (nn(x, wq[...].reshape(width, cols)) + vecs_o[QB : QB + 1, at_cols].astype(F32)).astype(BF16)
    k_o[...] = nn(x, wk[...].reshape(width, cols)).astype(BF16)
    v_o[...] = (nn(x, wv[...].reshape(width, cols)) + vecs_o[VB : VB + 1, at_cols].astype(F32)).astype(BF16)
    for first, rows, long_at in segments(dims):
        bias = key_bias(slen, llen, dims[3], rows, long_at)
        at = slice(first, first + rows)
        for pair in range(cols // PAIR):
            lanes = slice(pair * PAIR, (pair + 1) * PAIR)
            q = q_o[at, lanes] * jnp.asarray(HEAD_DIM**-0.5, BF16)
            scores = nt(two_heads(k_o[at, lanes]), q)
            probs = []
            for h in range(2):
                s = scores[h * rows : (h + 1) * rows] + bias
                e = jnp.exp(s - jnp.max(s, axis=0, keepdims=True))
                probs.append((e * (1.0 / jnp.sum(e, axis=0, keepdims=True))).astype(BF16))
            probs = jnp.concatenate(probs, axis=0)
            if long_at is None:
                ps_o[pair] = probs
            else:
                pl_o[long_at, pair] = probs
            c_o[at, lanes] = tn(two_heads(v_o[at, lanes]), probs).T.astype(BF16)
    total[...] += nn(c_o[...], wo_all[at_cols, :])

    @pl.when(step == pl.num_programs(0) - 1)
    def _():
        h = x_all[...].astype(F32) + (total[...] + row_of(vecs_o, OB))
        unit, inverse = normalized(h)
        n_o[...] = unit
        r_o[...] = inverse
        low_o[...] = (unit * row_of(vecs_o, G1) + row_of(vecs_o, S1)).astype(BF16)


def attention_forward(slen, llen, xs, xl, gathered, inner, dims):
    rows, width = xs.shape[0] + xl.shape[0], xs.shape[1]
    short_rows, long_count, long_length, _ = dims
    each = width // SHARDS
    step = 256
    steps, pairs = width // step, width // PAIR
    per = step // PAIR
    slab = lambda i: pl.BlockSpec((SHARDS, each, step), lambda g, *_: (0, i, g))
    cols = pl.BlockSpec((rows, step), lambda g, *_: (0, g))
    return pl.pallas_call(
        functools.partial(attention_forward_body, dims),
        grid_spec=pltpu.PrefetchScalarGridSpec(
            num_scalar_prefetch=2,
            grid=(steps,),
            in_specs=[
                whole(*xs.shape), whole(*xl.shape), slab(0), slab(1), slab(2),
                pl.BlockSpec((SHARDS, each, width), lambda g, *_: (0, 3, 0)),
                pl.BlockSpec((SHARDS, 8, width), lambda g, *_: (0, gathered.shape[1] // 8 - 1, 0)),
            ],
            out_specs=[
                cols, cols, cols, cols,
                pl.BlockSpec((per, 2 * short_rows, short_rows), lambda g, *_: (g, 0, 0)),
                pl.BlockSpec((long_count, per, 2 * long_length, long_length), lambda g, *_: (0, g, 0, 0)),
                whole(rows, width), whole(rows, 1), whole(rows, width), whole(8, width), whole(1, inner),
            ],
            scratch_shapes=[
                pltpu.VMEM((rows, width), BF16), pltpu.VMEM((rows, width), F32), pltpu.VMEM((width, width), BF16),
            ],
        ),
        out_shape=[
            *[jax.ShapeDtypeStruct((rows, width), BF16)] * 4,
            jax.ShapeDtypeStruct((pairs, 2 * short_rows, short_rows), BF16),
            jax.ShapeDtypeStruct((long_count, pairs, 2 * long_length, long_length), BF16),
            jax.ShapeDtypeStruct((rows, width), F32),
            jax.ShapeDtypeStruct((rows, 1), F32),
            jax.ShapeDtypeStruct((rows, width), BF16),
            jax.ShapeDtypeStruct((8, width), BF16),
            jax.ShapeDtypeStruct((1, inner), BF16),
        ],
        compiler_params=params(),
        cost_estimate=cost(8 * rows * width * width, 20e6),
        name="attention_forward",
    )(slen, llen, xs, xl, gathered, gathered, gathered, gathered, gathered)


def feed_forward_body(
    dims, half,
    slen, llen, pos, low, unit1, cot_s, cot_l, wup, ub, wdown, vecs,
    gelu_o, keep, give, gffn_o, gss_o, outs_o, outl_o, sums_o,
    hidden, total,
):
    step = pl.program_id(0)
    short_rows = dims[0]
    block, width = hidden.shape[2], low.shape[1]

    @pl.when(step < half)
    def _():
        pre = nn(low[...], wup[...].reshape(width, block)) + ub[...].astype(F32)
        cdf = 0.5 + 0.5 * lax.erf(pre * (0.5**0.5))
        density = jnp.exp(-0.5 * pre * pre) * (0.5 / jnp.pi) ** 0.5
        h = (pre * cdf).astype(BF16)
        gelu_o[...] = (cdf + pre * density).astype(BF16)
        hidden[step] = h
        part = nn(h, wdown[...].reshape(block, width))

        @pl.when(step == 0)
        def _():
            total[...] = part

        @pl.when(step > 0)
        def _():
            total[...] += part

    @pl.when(step == half - 1)
    def _():
        first = unit1[...] * row_of(vecs, G1) + row_of(vecs, S1)
        unit, inverse = normalized(first + (total[...] + row_of(vecs, DB)))
        valid = valid_rows(slen, llen, dims)
        out = ((unit * row_of(vecs, G2) + row_of(vecs, S2)) * valid).astype(BF16)
        outs_o[...] = out[:short_rows]
        outl_o[...] = out[short_rows:]
        cot = jnp.concatenate([cot_s[...], cot_l[...]], axis=0).astype(F32) * valid
        back = norm_back(cot * row_of(vecs, G2), unit, inverse)
        gss_o[...] = back
        low_back = back.astype(BF16)
        gffn_o[...] = low_back
        sums_o[...] = jnp.zeros_like(sums_o)
        sums_o[DB : DB + 1] = jnp.sum(low_back.astype(F32), axis=0, keepdims=True)
        sums_o[G2 : G2 + 1] = jnp.sum(cot * unit, axis=0, keepdims=True)
        sums_o[S2 : S2 + 1] = jnp.sum(cot, axis=0, keepdims=True)

    @pl.when(step >= half)
    def _():
        x = step - half
        grad = tn(hidden[x], gffn_o[...]).astype(BF16)
        each = block // (2 * RING)
        first = pos[2] == 0
        for z in range(RING):
            p0, p1 = places(pos, x, z)
            even, odd = grad[2 * z * each : (2 * z + 1) * each], grad[(2 * z + 1) * each : (2 * z + 2) * each]
            keep[jnp.where(first, p0, p1)] = jnp.where(first, even, odd)
            give[jnp.where(first, p1, p0)] = jnp.where(first, odd, even)


def feed_forward(slen, llen, pos, low, unit1, cot_s, cot_l, gathered, ub, vecs, dims):
    rows, width = low.shape
    inner = ub.shape[1]
    half = RING
    block = inner // half
    each, tall = width // SHARDS, inner // SHARDS
    step_of = lambda g: jnp.minimum(g, half - 1)
    cols = lambda r: pl.BlockSpec((r, block), lambda g, *_: (0, step_of(g)))
    return pl.pallas_call(
        functools.partial(feed_forward_body, dims, half),
        grid_spec=pltpu.PrefetchScalarGridSpec(
            num_scalar_prefetch=3,
            grid=(2 * half,),
            in_specs=[
                whole(rows, width), whole(rows, width), whole(*cot_s.shape), whole(*cot_l.shape),
                pl.BlockSpec((SHARDS, each, width), lambda g, *_: (0, 4 + step_of(g), 0)),
                cols(1),
                pl.BlockSpec((SHARDS // half, tall, width), lambda g, *_: (step_of(g), 8 * each // tall, 0)),
                whole(*vecs.shape),
            ],
            out_specs=[
                cols(rows),
                whole(CHIPS, tall, width), whole(CHIPS, tall, width),
                whole(rows, width), whole(rows, width), whole(*cot_s.shape), whole(*cot_l.shape),
                whole(8, width),
            ],
            scratch_shapes=[pltpu.VMEM((half, rows, block), BF16), pltpu.VMEM((rows, width), F32)],
        ),
        out_shape=[
            jax.ShapeDtypeStruct((rows, inner), BF16),
            jax.ShapeDtypeStruct((CHIPS, tall, width), BF16),
            jax.ShapeDtypeStruct((CHIPS, tall, width), BF16),
            jax.ShapeDtypeStruct((rows, width), BF16),
            jax.ShapeDtypeStruct((rows, width), F32),
            jax.ShapeDtypeStruct(cot_s.shape, BF16),
            jax.ShapeDtypeStruct(cot_l.shape, BF16),
            jax.ShapeDtypeStruct((8, width), F32),
        ],
        compiler_params=params(),
        cost_estimate=cost(6 * rows * width * inner, 30e6),
        name="feed_forward",
    )(slen, llen, pos, low, unit1, cot_s, cot_l, gathered, ub, gathered, vecs)


def feed_back_body(
    pos, gffn, gss, gelu, wdown, wup, low, unit1, inv1, vecs,
    keep, give, dub_o, gfs_o, gatt_o, sums_o,
    total,
):
    step = pl.program_id(0)
    width, block = low.shape[1], gelu.shape[1]
    up = (nt(gffn[...], wdown[...].reshape(block, width)) * gelu[...].astype(F32)).astype(BF16)
    dub_o[...] = jnp.sum(up.astype(F32), axis=0, keepdims=True)
    deal(keep, give, pos, tn(low[...], up).astype(BF16), slice(None), width // SHARDS)
    part = nt(up, wup[...].reshape(width, block))

    @pl.when(step == 0)
    def _():
        total[...] = part

    @pl.when(step > 0)
    def _():
        total[...] += part

    @pl.when(step == pl.num_programs(0) - 1)
    def _():
        grad = gss[...] + total[...]
        unit = unit1[...]
        back = norm_back(grad * row_of(vecs, G1), unit, inv1[...])
        gfs_o[...] = back
        low_back = back.astype(BF16)
        gatt_o[...] = low_back
        sums_o[...] = jnp.zeros_like(sums_o)
        sums_o[OB : OB + 1] = jnp.sum(low_back.astype(F32), axis=0, keepdims=True)
        sums_o[G1 : G1 + 1] = jnp.sum(grad * unit, axis=0, keepdims=True)
        sums_o[S1 : S1 + 1] = jnp.sum(grad, axis=0, keepdims=True)


def feed_back(pos, gffn, gss, gelu, gathered, low, unit1, inv1, vecs):
    rows, width = low.shape
    inner = gelu.shape[1]
    half = RING
    block = inner // half
    each, tall = width // SHARDS, inner // SHARDS
    cols = lambda r: pl.BlockSpec((r, block), lambda g, *_: (0, g))
    dealt = pl.BlockSpec((CHIPS, each, width), lambda g, *_: (0, g, 0))
    return pl.pallas_call(
        feed_back_body,
        grid_spec=pltpu.PrefetchScalarGridSpec(
            num_scalar_prefetch=1,
            grid=(half,),
            in_specs=[
                whole(rows, width), whole(rows, width), cols(rows),
                pl.BlockSpec((SHARDS // half, tall, width), lambda g, *_: (g, 8 * each // tall, 0)),
                pl.BlockSpec((SHARDS, each, width), lambda g, *_: (0, 4 + g, 0)),
                whole(rows, width), whole(rows, width), whole(rows, 1), whole(*vecs.shape),
            ],
            out_specs=[dealt, dealt, cols(1), whole(rows, width), whole(rows, width), whole(8, width)],
            scratch_shapes=[pltpu.VMEM((rows, width), F32)],
        ),
        out_shape=[
            jax.ShapeDtypeStruct((CHIPS, tall, width), BF16),
            jax.ShapeDtypeStruct((CHIPS, tall, width), BF16),
            jax.ShapeDtypeStruct((1, inner), F32),
            jax.ShapeDtypeStruct((rows, width), F32),
            jax.ShapeDtypeStruct((rows, width), BF16),
            jax.ShapeDtypeStruct((8, width), F32),
        ],
        compiler_params=params(),
        cost_estimate=cost(6 * rows * width * inner, 25e6),
        name="feed_back",
    )(pos, gffn, gss, gelu, gathered, gathered, low, unit1, inv1, vecs)


def attention_back_body(
    dims,
    pos, gatt, gatt_cols, wo_block, c, q, k, v, ps, plong, xs, xl, sums_f, sums_b, dub,
    keep, give, dq_o, dk_o, dv_o,
    x_all, gc, wo_all, sums,
):
    step = pl.program_id(0)
    short_rows, width = dims[0], x_all.shape[1]
    cols = q.shape[1]
    each = width // SHARDS
    at_cols = pl.ds(pl.multiple_of(step * cols, cols), cols)

    @pl.when(step == 0)
    def _():
        x_all[:short_rows, :] = xs[...]
        x_all[short_rows:, :] = xl[...]
        wo_all[...] = wo_block[...].reshape(width, width)
        sums[...] = sums_f[...] + sums_b[...]

    deal(keep, give, pos, tn(c[...], gatt_cols[...]).astype(BF16), slice(3 * each, 4 * each), each)
    gc[...] = nt(gatt[...], wo_all[at_cols, :]).astype(BF16)
    scale = HEAD_DIM**-0.5
    for first, rows, long_at in segments(dims):
        at = slice(first, first + rows)
        for pair in range(cols // PAIR):
            lanes = slice(pair * PAIR, (pair + 1) * PAIR)
            probs = ps[pair] if long_at is None else plong[long_at, pair]
            grad = gc[at, lanes]
            dp = nt(two_heads(v[at, lanes]), grad)
            ds = []
            for h in range(2):
                half = slice(h * rows, (h + 1) * rows)
                p = probs[half].astype(F32)
                d = dp[half]
                ds.append((p * (d - jnp.sum(d * p, axis=0, keepdims=True))).astype(BF16))
            ds = jnp.concatenate(ds, axis=0)
            dv_o[at, lanes] = own_lanes(nn(probs, grad)).astype(BF16)
            dk_o[at, lanes] = (own_lanes(nn(ds, q[at, lanes])) * scale).astype(BF16)
            dq_o[at, lanes] = (tn(two_heads(k[at, lanes]), ds).T * scale).astype(BF16)
    x = x_all[...]
    for i, d in enumerate((dq_o, dk_o, dv_o)):
        deal(keep, give, pos, tn(x, d[...]).astype(BF16), slice(i * each, (i + 1) * each), each)
    sums[QB : QB + 1, at_cols] = jnp.sum(dq_o[...].astype(F32), axis=0, keepdims=True)
    sums[VB : VB + 1, at_cols] = jnp.sum(dv_o[...].astype(F32), axis=0, keepdims=True)
    keep[:, 4 * each :] = jnp.zeros((CHIPS, 8, cols), BF16)
    give[:, 4 * each :] = jnp.zeros((CHIPS, 8, cols), BF16)

    @pl.when(step == pl.num_programs(0) - 1)
    def _():
        mine = spread(SHARDS, width)
        rest = column_rest(cols, width, each)
        line = jnp.zeros((SHARDS, cols), F32)
        for i in range(8):
            put = (iota(rest.shape, 0) == rest + i * each).astype(BF16)
            line += nt(jnp.where(mine, sums[i : i + 1], 0.0).astype(BF16), put)
        inner = dub.shape[1]
        put = (iota((cols, inner), 0) == column_rest(cols, inner, inner // SHARDS)).astype(BF16)
        wide = nt(jnp.where(spread(SHARDS, inner), dub[...], 0.0).astype(BF16), put)
        both = jnp.concatenate([line[:, None], wide[:, None], jnp.zeros((SHARDS, 6, cols), F32)], axis=1)
        deal(keep, give, pos, both.reshape(SHARDS * 8, cols).astype(BF16), slice(4 * each, 4 * each + 8), 8)


def attention_back(pos, gatt, gathered, c, q, k, v, ps, plong, xs, xl, sums_f, sums_b, dub, dims):
    rows, width = gatt.shape
    short_rows, long_count, long_length, _ = dims
    each = width // SHARDS
    step = 256
    per = step // PAIR
    cols = pl.BlockSpec((rows, step), lambda g, *_: (0, g))
    dealt = pl.BlockSpec((CHIPS, 4 * each + 8, step), lambda g, *_: (0, 0, g))
    return pl.pallas_call(
        functools.partial(attention_back_body, dims),
        grid_spec=pltpu.PrefetchScalarGridSpec(
            num_scalar_prefetch=1,
            grid=(width // step,),
            in_specs=[
                whole(rows, width), cols,
                pl.BlockSpec((SHARDS, each, width), lambda g, *_: (0, 3, 0)),
                whole(rows, width), cols, cols, cols,
                pl.BlockSpec((per, 2 * short_rows, short_rows), lambda g, *_: (g, 0, 0)),
                pl.BlockSpec((long_count, per, 2 * long_length, long_length), lambda g, *_: (0, g, 0, 0)),
                whole(*xs.shape), whole(*xl.shape), whole(8, width), whole(8, width), whole(*dub.shape),
            ],
            out_specs=[dealt, dealt, cols, cols, cols],
            scratch_shapes=[
                pltpu.VMEM((rows, width), BF16), pltpu.VMEM((rows, step), BF16),
                pltpu.VMEM((width, width), BF16), pltpu.VMEM((8, width), F32),
            ],
        ),
        out_shape=[
            *[jax.ShapeDtypeStruct((CHIPS, 4 * each + 8, width), BF16)] * 2,
            *[jax.ShapeDtypeStruct((rows, width), BF16)] * 3,
        ],
        compiler_params=params(),
        cost_estimate=cost(12 * rows * width * width, 25e6),
        name="attention_back",
    )(pos, gatt, gatt, gathered, c, q, k, v, ps, plong, xs, xl, sums_f, sums_b, dub)


def input_back_body(dims, gfs, dq, dk, dv, wq, wk, wv, gs_o, gl_o, total):
    step = pl.program_id(0)
    short_rows, width, cols = dims[0], gfs.shape[1], dq.shape[1]
    part = (
        nt(dq[...], wq[...].reshape(width, cols))
        + nt(dk[...], wk[...].reshape(width, cols))
        + nt(dv[...], wv[...].reshape(width, cols))
    )

    @pl.when(step == 0)
    def _():
        total[...] = gfs[...] + part

    @pl.when(step > 0)
    def _():
        total[...] += part

    @pl.when(step == pl.num_programs(0) - 1)
    def _():
        gs_o[...] = total[:short_rows]
        gl_o[...] = total[short_rows:]


def input_back(gfs, dq, dk, dv, gathered, dims):
    rows, width = gfs.shape
    each = width // SHARDS
    step = 256
    short_rows = dims[0]
    cols = pl.BlockSpec((rows, step), lambda g: (0, g))
    slab = lambda i: pl.BlockSpec((SHARDS, each, step), lambda g: (0, i, g))
    return pl.pallas_call(
        functools.partial(input_back_body, dims),
        grid=(width // step,),
        in_specs=[whole(rows, width), cols, cols, cols, slab(0), slab(1), slab(2)],
        out_specs=[whole(short_rows, width), whole(rows - short_rows, width)],
        scratch_shapes=[pltpu.VMEM((rows, width), F32)],
        out_shape=[
            jax.ShapeDtypeStruct((short_rows, width), F32),
            jax.ShapeDtypeStruct((rows - short_rows, width), F32),
        ],
        compiler_params=params(),
        cost_estimate=cost(6 * rows * width * width, 12e6),
        name="input_back",
    )(gfs, dq, dk, dv, gathered, gathered, gathered)


def pair_sum_body(keep, got, *outs):
    for i, o in enumerate(outs):
        at = slice(i * RING, (i + 1) * RING)
        o[...] = (keep[at].astype(F32) + got[at].astype(F32)).astype(BF16)


def ring_sum_body(own, left, right, far, *outs):
    total = (own[...].astype(F32) + far[...].astype(F32)) + (left[...].astype(F32) + right[...].astype(F32))
    if len(outs) == 1:
        outs[0][...] = total.astype(BF16)
    else:
        for i, o in enumerate(outs):
            o[...] = total[i].astype(BF16)


def turn(delta, stage):
    moves = []
    for x in range(RING):
        for z in range(RING):
            for core in range(2):
                to_x, to_z = x, z
                if (core == 0) == (stage == 0):
                    to_x = (x + delta) % RING
                else:
                    to_z = (z + delta) % RING
                moves.append(((x * RING + z) * 2 + core, (to_x * RING + to_z) * 2 + core))
    return moves


def swap_cores(v):
    return lax.ppermute(v, "shard", [(i, i ^ 1) for i in range(SHARDS)])


def to_owner(keep, give):
    got = swap_cores(give)
    rows, width = keep.shape[1:]
    quarter = jax.ShapeDtypeStruct((RING, rows, width), BF16)
    parts = pl.pallas_call(
        pair_sum_body, out_shape=[quarter] * RING, compiler_params=params(), name="pair_sum",
        cost_estimate=cost(keep.size, 6 * keep.size),
    )(keep, got)
    left, far, right = (lax.ppermute(parts[d], "shard", turn(d, 0)) for d in (1, 2, 3))
    block = jax.ShapeDtypeStruct((rows, width), BF16)
    parts = pl.pallas_call(
        ring_sum_body, out_shape=[block] * RING, compiler_params=params(), name="ring_sum",
        cost_estimate=cost(4 * RING * rows * width, 10 * RING * rows * width),
    )(parts[0], left, right, far)
    left, far, right = (lax.ppermute(parts[d], "shard", turn(d, 1)) for d in (1, 2, 3))
    own = pl.pallas_call(
        ring_sum_body, out_shape=[block], compiler_params=params(), name="ring_sum",
        cost_estimate=cost(4 * rows * width, 10 * rows * width),
    )(parts[0], left, right, far)[0]
    return own, *(lax.ppermute(own, "rep", [(i, (i + d) % RING) for i in range(RING)]) for d in (1, 3, 2))


def replica_sum(own, left, right, far, at):
    return (own[at].astype(F32) + far[at].astype(F32)) + (left[at].astype(F32) + right[at].astype(F32))


def finish_attention_body(own, left, right, far, wqkv_o, wo_o, *vector_os):
    each, width = wo_o.shape
    for j in range(wqkv_o.shape[1] // width):
        at = slice(j * each, (j + 1) * each)
        wqkv_o[:, j * width : (j + 1) * width] = replica_sum(own, left, right, far, at)
    wo_o[...] = replica_sum(own, left, right, far, slice(3 * each, 4 * each))
    last = replica_sum(own, left, right, far, slice(4 * each, 4 * each + 8))[:, width - 256 :]
    for i, o in enumerate(vector_os[:-1]):
        o[...] = last[0:1, i * each : (i + 1) * each]
    o = vector_os[-1]
    o[...] = last[1:2, : o.shape[1]]


def finish_attention(arrays, tall):
    width = arrays[0].shape[1]
    each = width // SHARDS
    return pl.pallas_call(
        finish_attention_body,
        out_shape=[
            jax.ShapeDtypeStruct((each, 3 * width), F32),
            jax.ShapeDtypeStruct((each, width), F32),
            *[jax.ShapeDtypeStruct((1, each), F32)] * 8,
            jax.ShapeDtypeStruct((1, tall), F32),
        ],
        compiler_params=params(),
        name="finish_attention",
    )(*arrays)


def finish_feed_body(own, left, right, far, out):
    each, wide = out.shape
    width = own.shape[1]
    for j in range(wide // width):
        at = slice(j * each, (j + 1) * each)
        out[:, j * width : (j + 1) * width] = replica_sum(own, left, right, far, at)


def finish_feed(arrays, shape):
    return pl.pallas_call(
        finish_feed_body,
        out_shape=jax.ShapeDtypeStruct(shape, F32),
        compiler_params=params(),
        name="finish_feed",
    )(*arrays)


def on_device(
    short_tokens, long_tokens, short_lengths, long_lengths, short_cotangent, long_cotangent,
    input_weight, query_bias, value_bias, output_weight, output_bias, first_gain, first_shift,
    up_weight, up_bias, down_weight, down_bias, second_gain, second_shift,
):
    short_count, short_length, width = short_tokens.shape
    long_count, long_length, _ = long_tokens.shape
    dims = (short_count * short_length, long_count, long_length, short_length)
    each, inner, tall = width // SHARDS, up_weight.shape[1], down_weight.shape[0]
    xs, xl = short_tokens.reshape(-1, width), long_tokens.reshape(-1, width)
    cs, cl = short_cotangent.reshape(-1, width), long_cotangent.reshape(-1, width)
    index = lax.axis_index("shard")
    pos = jnp.stack([index // 8, (index // 2) % 4, index % 2]).astype(jnp.int32)

    packed = pack(
        input_weight, output_weight, up_weight, down_weight,
        (query_bias, value_bias, output_bias, first_gain, first_shift, down_bias, second_gain, second_shift),
        up_bias,
    )
    gathered = lax.all_gather(packed, "shard", axis=0)
    q, k, v, c, ps, plong, unit1, inv1, low, vecs, ub = attention_forward(
        short_lengths, long_lengths, xs, xl, gathered, inner, dims
    )
    gelu, keep_d, give_d, gffn, gss, out_s, out_l, sums_f = feed_forward(
        short_lengths, long_lengths, pos, low, unit1, cs, cl, gathered, ub, vecs, dims
    )
    down = finish_feed(to_owner(keep_d, give_d), (tall, width))
    keep_u, give_u, dub, gfs, gatt, sums_b = feed_back(pos, gffn, gss, gelu, gathered, low, unit1, inv1, vecs)
    up = finish_feed(to_owner(keep_u, give_u), (each, inner))
    keep_a, give_a, dq, dk, dv = attention_back(
        pos, gatt, gathered, c, q, k, v, ps, plong, xs, xl, sums_f, sums_b, dub, dims
    )
    w_in, w_out, *vectors = finish_attention(to_owner(keep_a, give_a), tall)
    grad_s, grad_l = input_back(gfs, dq, dk, dv, gathered, dims)
    vectors = [x.reshape(-1) for x in vectors]
    return (
        out_s.reshape(short_tokens.shape), out_l.reshape(long_tokens.shape),
        grad_s.reshape(short_tokens.shape), grad_l.reshape(long_tokens.shape),
        w_in, vectors[QB], vectors[VB], w_out, vectors[OB], vectors[G1], vectors[S1],
        up, vectors[8], down, vectors[DB], vectors[G2], vectors[S2],
    )


def solution(mesh):
    rows, flat = P(("rep", "shard"), None, None), P("shard")
    tall = P("shard", None)
    return jax.shard_map(
        on_device,
        mesh=mesh,
        in_specs=(
            rows, rows, P(("rep", "shard")), P(("rep", "shard")), rows, rows,
            tall, flat, flat, tall, flat, flat, flat, tall, flat, tall, flat, flat, flat,
        ),
        out_specs=(
            rows, rows, rows, rows,
            tall, flat, flat, tall, flat, flat, flat, tall, flat, tall, flat, flat, flat,
        ),
        check_vma=False,
    )
```

```python
import functools

import jax
import jax.numpy as jnp
from jax import lax
from jax.experimental import pallas as pl
from jax.experimental.pallas import tpu as pltpu
from jax.sharding import PartitionSpec as P

F32 = jnp.float32
BF16 = jnp.bfloat16
HEAD_DIM = 64
PAIR = 128
EPSILON = 1e-06
QB, VB, OB, G1, S1, DB, G2, S2 = range(8)
RING = 4
CHIPS = RING * RING
SHARDS = 2 * CHIPS


def nn(a, b):
    return lax.dot_general(a, b, (((1,), (0,)), ((), ())), preferred_element_type=F32)


def nt(a, b):
    return lax.dot_general(a, b, (((1,), (1,)), ((), ())), preferred_element_type=F32)


def tn(a, b):
    return lax.dot_general(a, b, (((0,), (0,)), ((), ())), preferred_element_type=F32)


def iota(shape, dim):
    return lax.broadcasted_iota(jnp.int32, shape, dim)


def row_of(ref, i):
    return ref[i : i + 1, :].astype(F32)


def whole(*shape):
    return pl.BlockSpec(shape, lambda g, *_: (0,) * len(shape))


def params(mebibytes):
    return pltpu.CompilerParams(vmem_limit_bytes=mebibytes * 1024 * 1024)


def cost(flops, moved):
    return pl.CostEstimate(flops=int(flops), bytes_accessed=int(moved), transcendentals=0)


def places(pos, x, z):
    along_x, along_z = (x - pos[0]) & (RING - 1), (z - pos[1]) & (RING - 1)
    return along_x * RING + along_z, along_z * RING + along_x


def deal(keep, give, pos, value, at, each):
    first = pos[2] == 0
    for x in range(RING):
        for z in range(RING):
            p0, p1 = places(pos, x, z)
            low = 2 * (x * RING + z) * each
            even, odd = value[low : low + each], value[low + each : low + 2 * each]
            keep[jnp.where(first, p0, p1), at] = jnp.where(first, even, odd)
            give[jnp.where(first, p1, p0), at] = jnp.where(first, odd, even)


def spread(owners, width):
    each = width // owners
    at = iota((owners, width), 1)
    low = iota((owners, width), 0) * each
    return (at >= low) & (at < low + each)


def column_rest(rows, width, each):
    at = iota((rows, width), 1)
    return at - (at // each) * each


def two_heads(pair):
    low_half = iota(pair.shape, 1) < HEAD_DIM
    zero = jnp.zeros_like(pair)
    return jnp.concatenate([jnp.where(low_half, pair, zero), jnp.where(low_half, zero, pair)], axis=0)


def own_lanes(stack):
    half = stack.shape[0] // 2
    return jnp.where(iota((half, stack.shape[1]), 1) < HEAD_DIM, stack[:half], stack[half:])


def normalized(hidden):
    center = hidden - jnp.mean(hidden, axis=-1, keepdims=True)
    spread_of = jnp.mean(center * center, axis=-1, keepdims=True)
    inverse = lax.rsqrt(spread_of + EPSILON)
    return center * inverse, inverse


def norm_back(scaled, unit, inverse):
    return inverse * (
        scaled
        - jnp.mean(scaled, axis=-1, keepdims=True)
        - unit * jnp.mean(scaled * unit, axis=-1, keepdims=True)
    )


def segments(dims):
    short_rows, long_count, long_length, _ = dims
    return [(0, short_rows, None)] + [
        (short_rows + i * long_length, long_length, i) for i in range(long_count)
    ]


def key_bias(slen, llen, short_length, rows, long_at):
    key = iota((rows, rows), 0)
    if long_at is not None:
        return jnp.where(key < llen[long_at], 0.0, -1e9).astype(F32)
    query = iota((rows, rows), 1)
    keep = jnp.zeros((rows, rows), jnp.bool_)
    for p in range(rows // short_length):
        low, high = p * short_length, (p + 1) * short_length
        keep = keep | ((key >= low) & (key < low + slen[p]) & (query >= low) & (query < high))
    return jnp.where(keep, 0.0, -1e9).astype(F32)


def valid_rows(slen, llen, dims):
    short_rows, long_count, long_length, short_length = dims
    parts = []
    at = iota((short_length, 1), 0)
    for p in range(short_rows // short_length):
        parts.append((at < slen[p]).astype(F32))
    at = iota((long_length, 1), 0)
    for p in range(long_count):
        parts.append((at < llen[p]).astype(F32))
    return jnp.concatenate(parts, axis=0)


def slabs_of(out, base, source, each, width):
    for j in range(source.shape[1] // width):
        out[base + j * each : base + (j + 1) * each] = source[:, j * width : (j + 1) * width]
    return base + source.shape[1] // width * each


def pack_body(wqkv, wo, wup, wdown, *rest):
    vectors, (attention, feed) = rest[:-2], rest[-2:]
    each, width = wo.shape
    base = slabs_of(attention, 0, wqkv, each, width)
    base = slabs_of(attention, base, wo, each, width)
    attention[base:] = jnp.zeros((8, width), BF16)
    for i, v in enumerate(vectors[:-1]):
        attention[base : base + 1, i * each : (i + 1) * each] = v[...]
    attention[base + 1 : base + 2, : vectors[-1].shape[1]] = vectors[-1][...]
    base = slabs_of(feed, 0, wup, each, width)
    feed[base:] = wdown[...]


def pack(wqkv, wo, wup, wdown, vectors, ub):
    each, width = wo.shape
    rows = wqkv.shape[1] // width * each + each + 8
    return pl.pallas_call(
        pack_body,
        out_shape=[
            jax.ShapeDtypeStruct((rows, width), BF16),
            jax.ShapeDtypeStruct((2 * wdown.shape[0], width), BF16),
        ],
        compiler_params=params(4),
        name="pack",
    )(wqkv, wo, wup, wdown, *[v[None] for v in vectors], ub[None])


STEPS = (0, -1, 1, 2)


def gathered_at(pos, other, k, i):
    core = pos[2] ^ other
    x0, z0 = (pos[0] + STEPS[k]) & (RING - 1), (pos[1] + STEPS[i]) & (RING - 1)
    x1, z1 = (pos[0] + STEPS[i]) & (RING - 1), (pos[1] + STEPS[k]) & (RING - 1)
    return jnp.where(core == 0, (x0 * RING + z0) * 2, (x1 * RING + z1) * 2 + 1)


def arrivals(pos, pieces, target, sems, at):
    copies = []
    for other in range(2):
        for k in range(RING):
            for i in range(RING):
                n = (other * RING + k) * RING + i
                copies.append(
                    pltpu.make_async_copy(
                        pieces[other * RING + k].at[i, at], target.at[gathered_at(pos, other, k, i), at], sems.at[n]
                    )
                )
    return copies


def attention_forward_body(
    dims, slen, llen, pos, xs, xl, p0, p1, p2, p3, p4, p5, p6, p7,
    q_o, k_o, v_o, c_o, ps_o, pl_o, n_o, r_o, low_o, vecs_o, ub_o, gathered_o,
    x_all, total, wo_all, gathered, sems, out_sem,
):
    step = pl.program_id(0)
    short_rows, width = dims[0], x_all.shape[1]
    cols = q_o.shape[1]
    each = width // SHARDS
    keep_all = pltpu.make_async_copy(gathered, gathered_o, out_sem)

    @pl.when(step == 0)
    def _():
        copies = arrivals(pos, (p0, p1, p2, p3, p4, p5, p6, p7), gathered, sems, slice(None))
        for copy in copies:
            copy.start()
        x_all[:short_rows, :] = xs[...]
        x_all[short_rows:, :] = xl[...]
        total[...] = jnp.zeros_like(total)
        for copy in copies:
            copy.wait()
        keep_all.start()
        wo_all[...] = gathered[:, 3 * each : 4 * each].reshape(width, width)
        packed = gathered[:, 4 * each :]
        line = packed[:, 0, : 8 * each + 64]
        rest = column_rest(line.shape[1], width, each)
        mine = spread(SHARDS, width)
        for i in range(8):
            pick = (iota(rest.shape, 0) == rest + i * each).astype(BF16)
            row = jnp.sum(jnp.where(mine, nn(line, pick), 0.0), axis=0, keepdims=True)
            vecs_o[i : i + 1] = row.astype(BF16)
        inner = ub_o.shape[1]
        line = packed[:, 1, :128]
        pick = (iota((128, inner), 0) == column_rest(128, inner, inner // SHARDS)).astype(BF16)
        row = jnp.sum(jnp.where(spread(SHARDS, inner), nn(line, pick), 0.0), axis=0, keepdims=True)
        ub_o[...] = row.astype(BF16)

    x = x_all[...]
    at_cols = pl.ds(pl.multiple_of(step * cols, cols), cols)
    wq, wk, wv = (gathered[:, i * each : (i + 1) * each, at_cols].reshape(width, cols) for i in range(3))
    q_o[...] = (nn(x, wq) + vecs_o[QB : QB + 1, at_cols].astype(F32)).astype(BF16)
    k_o[...] = nn(x, wk).astype(BF16)
    v_o[...] = (nn(x, wv) + vecs_o[VB : VB + 1, at_cols].astype(F32)).astype(BF16)
    for first, rows, long_at in segments(dims):
        bias = key_bias(slen, llen, dims[3], rows, long_at)
        at = slice(first, first + rows)
        for pair in range(cols // PAIR):
            lanes = slice(pair * PAIR, (pair + 1) * PAIR)
            q = q_o[at, lanes] * jnp.asarray(HEAD_DIM**-0.5, BF16)
            scores = nt(two_heads(k_o[at, lanes]), q)
            probs = []
            for h in range(2):
                s = scores[h * rows : (h + 1) * rows] + bias
                e = jnp.exp(s - jnp.max(s, axis=0, keepdims=True))
                probs.append((e * (1.0 / jnp.sum(e, axis=0, keepdims=True))).astype(BF16))
            probs = jnp.concatenate(probs, axis=0)
            if long_at is None:
                ps_o[pair] = probs
            else:
                pl_o[long_at, pair] = probs
            c_o[at, lanes] = tn(two_heads(v_o[at, lanes]), probs).T.astype(BF16)
    total[...] += nn(c_o[...], wo_all[at_cols, :])

    @pl.when(step == pl.num_programs(0) - 1)
    def _():
        h = x_all[...].astype(F32) + (total[...] + row_of(vecs_o, OB))
        unit, inverse = normalized(h)
        n_o[...] = unit
        r_o[...] = inverse
        low_o[...] = (unit * row_of(vecs_o, G1) + row_of(vecs_o, S1)).astype(BF16)
        keep_all.wait()


def attention_forward(slen, llen, pos, xs, xl, pieces, inner, dims):
    rows, width = xs.shape[0] + xl.shape[0], xs.shape[1]
    short_rows, long_count, long_length, _ = dims
    step = 256
    steps, pairs = width // step, width // PAIR
    per = step // PAIR
    each_all = pieces[0].shape[1]
    cols = pl.BlockSpec((rows, step), lambda g, *_: (0, g))
    return pl.pallas_call(
        functools.partial(attention_forward_body, dims),
        grid_spec=pltpu.PrefetchScalarGridSpec(
            num_scalar_prefetch=3,
            grid=(steps,),
            in_specs=[
                whole(*xs.shape), whole(*xl.shape), *[pl.BlockSpec(memory_space=pl.ANY)] * 8,
            ],
            out_specs=[
                cols, cols, cols, cols,
                pl.BlockSpec((per, 2 * short_rows, short_rows), lambda g, *_: (g, 0, 0)),
                pl.BlockSpec((long_count, per, 2 * long_length, long_length), lambda g, *_: (0, g, 0, 0)),
                whole(rows, width), whole(rows, 1), whole(rows, width), whole(8, width), whole(1, inner),
                pl.BlockSpec(memory_space=pl.ANY),
            ],
            scratch_shapes=[
                pltpu.VMEM((rows, width), BF16), pltpu.VMEM((rows, width), F32), pltpu.VMEM((width, width), BF16),
                pltpu.VMEM((SHARDS, each_all, width), BF16), pltpu.SemaphoreType.DMA((SHARDS,)),
                pltpu.SemaphoreType.DMA(()),
            ],
        ),
        out_shape=[
            *[jax.ShapeDtypeStruct((rows, width), BF16)] * 4,
            jax.ShapeDtypeStruct((pairs, 2 * short_rows, short_rows), BF16),
            jax.ShapeDtypeStruct((long_count, pairs, 2 * long_length, long_length), BF16),
            jax.ShapeDtypeStruct((rows, width), F32),
            jax.ShapeDtypeStruct((rows, 1), F32),
            jax.ShapeDtypeStruct((rows, width), BF16),
            jax.ShapeDtypeStruct((8, width), BF16),
            jax.ShapeDtypeStruct((1, inner), BF16),
            jax.ShapeDtypeStruct((SHARDS, each_all, width), BF16),
        ],
        compiler_params=params(27),
        cost_estimate=cost(8 * rows * width * width, 20e6),
        name="attention_forward",
    )(slen, llen, pos, xs, xl, *pieces)


def feed_forward_body(
    dims, half,
    slen, llen, pos, low, unit1, cot_s, cot_l, ub, vecs, p0, p1, p2, p3, p4, p5, p6, p7,
    gelu_o, keep, give, gffn_o, gss_o, outs_o, outl_o, sums_o, gathered_o,
    hidden, total, wup, gathered, sems, out_sem,
):
    step = pl.program_id(0)
    short_rows = dims[0]
    block, width = hidden.shape[2], low.shape[1]
    each, tall = width // SHARDS, gathered.shape[1] // 2
    owners = SHARDS // half
    keep_all = pltpu.make_async_copy(gathered, gathered_o, out_sem)
    pieces = (p0, p1, p2, p3, p4, p5, p6, p7)
    ups = arrivals(pos, pieces, gathered, sems.at[0], slice(0, tall))
    downs = arrivals(pos, pieces, gathered, sems.at[1], slice(tall, 2 * tall))

    @pl.when(step == 0)
    def _():
        for copy in ups + downs:
            copy.start()
        for copy in ups:
            copy.wait()

    @pl.when(step < half)
    def _():
        for j in range(half):

            @pl.when(step == j)
            def _():
                wup[...] = gathered[:, j * each : (j + 1) * each].reshape(width, block)

        pre = nn(low[...], wup[...]) + ub[...].astype(F32)
        cdf = 0.5 + 0.5 * lax.erf(pre * (0.5**0.5))
        density = jnp.exp(-0.5 * pre * pre) * (0.5 / jnp.pi) ** 0.5
        h = (pre * cdf).astype(BF16)
        gelu_o[...] = (cdf + pre * density).astype(BF16)
        hidden[step] = h

        @pl.when(step == 0)
        def _():
            for copy in downs:
                copy.wait()
            keep_all.start()

        part = nn(h, gathered[pl.ds(step * owners, owners), tall:].reshape(block, width))

        @pl.when(step == 0)
        def _():
            total[...] = part

        @pl.when(step > 0)
        def _():
            total[...] += part

    @pl.when(step == half - 1)
    def _():
        first = unit1[...] * row_of(vecs, G1) + row_of(vecs, S1)
        unit, inverse = normalized(first + (total[...] + row_of(vecs, DB)))
        valid = valid_rows(slen, llen, dims)
        out = ((unit * row_of(vecs, G2) + row_of(vecs, S2)) * valid).astype(BF16)
        outs_o[...] = out[:short_rows]
        outl_o[...] = out[short_rows:]
        cot = jnp.concatenate([cot_s[...], cot_l[...]], axis=0).astype(F32) * valid
        back = norm_back(cot * row_of(vecs, G2), unit, inverse)
        gss_o[...] = back
        low_back = back.astype(BF16)
        gffn_o[...] = low_back
        sums_o[...] = jnp.zeros_like(sums_o)
        sums_o[DB : DB + 1] = jnp.sum(low_back.astype(F32), axis=0, keepdims=True)
        sums_o[G2 : G2 + 1] = jnp.sum(cot * unit, axis=0, keepdims=True)
        sums_o[S2 : S2 + 1] = jnp.sum(cot, axis=0, keepdims=True)

    @pl.when(step >= half)
    def _():
        x = step - half
        grad = tn(hidden[x], gffn_o[...]).astype(BF16)
        each = block // (2 * RING)
        first = pos[2] == 0
        for z in range(RING):
            p0, p1 = places(pos, x, z)
            even, odd = grad[2 * z * each : (2 * z + 1) * each], grad[(2 * z + 1) * each : (2 * z + 2) * each]
            keep[jnp.where(first, p0, p1)] = jnp.where(first, even, odd)
            give[jnp.where(first, p1, p0)] = jnp.where(first, odd, even)

    @pl.when(step == 2 * half - 1)
    def _():
        keep_all.wait()


def feed_forward(slen, llen, pos, low, unit1, cot_s, cot_l, ub, vecs, pieces, dims):
    rows, width = low.shape
    inner = ub.shape[1]
    half = RING
    block = inner // half
    tall = inner // SHARDS
    step_of = lambda g: jnp.minimum(g, half - 1)
    cols = lambda r: pl.BlockSpec((r, block), lambda g, *_: (0, step_of(g)))
    return pl.pallas_call(
        functools.partial(feed_forward_body, dims, half),
        grid_spec=pltpu.PrefetchScalarGridSpec(
            num_scalar_prefetch=3,
            grid=(2 * half,),
            in_specs=[
                whole(rows, width), whole(rows, width), whole(*cot_s.shape), whole(*cot_l.shape),
                cols(1), whole(*vecs.shape), *[pl.BlockSpec(memory_space=pl.ANY)] * 8,
            ],
            out_specs=[
                cols(rows),
                whole(CHIPS, tall, width), whole(CHIPS, tall, width),
                whole(rows, width), whole(rows, width), whole(*cot_s.shape), whole(*cot_l.shape),
                whole(8, width), pl.BlockSpec(memory_space=pl.ANY),
            ],
            scratch_shapes=[
                pltpu.VMEM((half, rows, block), BF16), pltpu.VMEM((rows, width), F32), pltpu.VMEM((width, block), BF16),
                pltpu.VMEM((SHARDS, 2 * tall, width), BF16), pltpu.SemaphoreType.DMA((2, SHARDS)),
                pltpu.SemaphoreType.DMA(()),
            ],
        ),
        out_shape=[
            jax.ShapeDtypeStruct((rows, inner), BF16),
            jax.ShapeDtypeStruct((CHIPS, tall, width), BF16),
            jax.ShapeDtypeStruct((CHIPS, tall, width), BF16),
            jax.ShapeDtypeStruct((rows, width), BF16),
            jax.ShapeDtypeStruct((rows, width), F32),
            jax.ShapeDtypeStruct(cot_s.shape, BF16),
            jax.ShapeDtypeStruct(cot_l.shape, BF16),
            jax.ShapeDtypeStruct((8, width), F32),
            jax.ShapeDtypeStruct((SHARDS, 2 * tall, width), BF16),
        ],
        compiler_params=params(40),
        cost_estimate=cost(6 * rows * width * inner, 30e6),
        name="feed_forward",
    )(slen, llen, pos, low, unit1, cot_s, cot_l, ub, vecs, *pieces)


def up_back_body(pos, gffn, gelu, wdown, low, keep, give, up_o, dub_o):
    width, block = low.shape[1], gelu.shape[1]
    up = (nt(gffn[...], wdown[...].reshape(block, width)) * gelu[...].astype(F32)).astype(BF16)
    up_o[...] = up
    dub_o[...] = jnp.sum(up.astype(F32), axis=0, keepdims=True)
    deal(keep, give, pos, tn(low[...], up).astype(BF16), slice(None), width // SHARDS)


def up_back(pos, gffn, gelu, gathered, low):
    rows, width = low.shape
    inner = gelu.shape[1]
    half = RING
    block = inner // half
    each, tall = width // SHARDS, inner // SHARDS
    cols = lambda r: pl.BlockSpec((r, block), lambda g, *_: (0, g))
    dealt = pl.BlockSpec((CHIPS, each, width), lambda g, *_: (0, g, 0))
    return pl.pallas_call(
        up_back_body,
        grid_spec=pltpu.PrefetchScalarGridSpec(
            num_scalar_prefetch=1,
            grid=(half,),
            in_specs=[
                whole(rows, width), cols(rows),
                pl.BlockSpec((SHARDS // half, tall, width), lambda g, *_: (g, 1, 0)),
                whole(rows, width),
            ],
            out_specs=[dealt, dealt, cols(rows), cols(1)],
        ),
        out_shape=[
            jax.ShapeDtypeStruct((CHIPS, tall, width), BF16),
            jax.ShapeDtypeStruct((CHIPS, tall, width), BF16),
            jax.ShapeDtypeStruct((rows, inner), BF16),
            jax.ShapeDtypeStruct((1, inner), F32),
        ],
        compiler_params=params(17),
        cost_estimate=cost(4 * rows * width * inner, 20e6),
        name="up_back",
    )(pos, gffn, gelu, gathered, low)


def first_back_body(gss, up, wup, unit1, inv1, vecs, gfs_o, gatt_o, sums_o, total):
    step = pl.program_id(0)
    width, block = gss.shape[1], up.shape[1]
    part = nt(up[...], wup[...].reshape(width, block))

    @pl.when(step == 0)
    def _():
        total[...] = part

    @pl.when(step > 0)
    def _():
        total[...] += part

    @pl.when(step == pl.num_programs(0) - 1)
    def _():
        grad = gss[...] + total[...]
        unit = unit1[...]
        back = norm_back(grad * row_of(vecs, G1), unit, inv1[...])
        gfs_o[...] = back
        low_back = back.astype(BF16)
        gatt_o[...] = low_back
        sums_o[...] = jnp.zeros_like(sums_o)
        sums_o[OB : OB + 1] = jnp.sum(low_back.astype(F32), axis=0, keepdims=True)
        sums_o[G1 : G1 + 1] = jnp.sum(grad * unit, axis=0, keepdims=True)
        sums_o[S1 : S1 + 1] = jnp.sum(grad, axis=0, keepdims=True)


def first_back(gss, up, gathered, unit1, inv1, vecs):
    rows, width = gss.shape
    inner = up.shape[1]
    half = RING
    block = inner // half
    return pl.pallas_call(
        first_back_body,
        grid=(half,),
        in_specs=[
            whole(rows, width), pl.BlockSpec((rows, block), lambda g: (0, g)),
            pl.BlockSpec((SHARDS, width // SHARDS, width), lambda g: (0, g, 0)),
            whole(rows, width), whole(rows, 1), whole(*vecs.shape),
        ],
        out_specs=[whole(rows, width), whole(rows, width), whole(8, width)],
        scratch_shapes=[pltpu.VMEM((rows, width), F32)],
        out_shape=[
            jax.ShapeDtypeStruct((rows, width), F32),
            jax.ShapeDtypeStruct((rows, width), BF16),
            jax.ShapeDtypeStruct((8, width), F32),
        ],
        compiler_params=params(23),
        cost_estimate=cost(2 * rows * width * inner, 15e6),
        name="first_back",
    )(gss, up, gathered, unit1, inv1, vecs)


def attention_back_body(
    dims,
    pos, gatt, gatt_cols, wo_block, c, q, k, v, ps, plong, xs, xl, sums_f, sums_b, dub,
    keep, give, dq_o, dk_o, dv_o,
    x_all, gc, wo_all, sums,
):
    step = pl.program_id(0)
    short_rows, width = dims[0], x_all.shape[1]
    cols = q.shape[1]
    each = width // SHARDS
    at_cols = pl.ds(pl.multiple_of(step * cols, cols), cols)

    @pl.when(step == 0)
    def _():
        x_all[:short_rows, :] = xs[...]
        x_all[short_rows:, :] = xl[...]
        wo_all[...] = wo_block[...].reshape(width, width)
        sums[...] = sums_f[...] + sums_b[...]

    deal(keep, give, pos, tn(c[...], gatt_cols[...]).astype(BF16), slice(3 * each, 4 * each), each)
    gc[...] = nt(gatt[...], wo_all[at_cols, :]).astype(BF16)
    scale = HEAD_DIM**-0.5
    for first, rows, long_at in segments(dims):
        at = slice(first, first + rows)
        for pair in range(cols // PAIR):
            lanes = slice(pair * PAIR, (pair + 1) * PAIR)
            probs = ps[pair] if long_at is None else plong[long_at, pair]
            grad = gc[at, lanes]
            dp = nt(two_heads(v[at, lanes]), grad)
            ds = []
            for h in range(2):
                half = slice(h * rows, (h + 1) * rows)
                p = probs[half].astype(F32)
                d = dp[half]
                ds.append((p * (d - jnp.sum(d * p, axis=0, keepdims=True))).astype(BF16))
            ds = jnp.concatenate(ds, axis=0)
            dv_o[at, lanes] = own_lanes(nn(probs, grad)).astype(BF16)
            dk_o[at, lanes] = (own_lanes(nn(ds, q[at, lanes])) * scale).astype(BF16)
            dq_o[at, lanes] = (tn(two_heads(k[at, lanes]), ds).T * scale).astype(BF16)
    x = x_all[...]
    for i, d in enumerate((dq_o, dk_o, dv_o)):
        deal(keep, give, pos, tn(x, d[...]).astype(BF16), slice(i * each, (i + 1) * each), each)
    sums[QB : QB + 1, at_cols] = jnp.sum(dq_o[...].astype(F32), axis=0, keepdims=True)
    sums[VB : VB + 1, at_cols] = jnp.sum(dv_o[...].astype(F32), axis=0, keepdims=True)
    keep[:, 4 * each :] = jnp.zeros((CHIPS, 8, cols), BF16)
    give[:, 4 * each :] = jnp.zeros((CHIPS, 8, cols), BF16)

    @pl.when(step == pl.num_programs(0) - 1)
    def _():
        mine = spread(SHARDS, width)
        rest = column_rest(cols, width, each)
        line = jnp.zeros((SHARDS, cols), F32)
        for i in range(8):
            put = (iota(rest.shape, 0) == rest + i * each).astype(BF16)
            line += nt(jnp.where(mine, sums[i : i + 1], 0.0).astype(BF16), put)
        inner = dub.shape[1]
        put = (iota((cols, inner), 0) == column_rest(cols, inner, inner // SHARDS)).astype(BF16)
        wide = nt(jnp.where(spread(SHARDS, inner), dub[...], 0.0).astype(BF16), put)
        both = jnp.concatenate([line[:, None], wide[:, None], jnp.zeros((SHARDS, 6, cols), F32)], axis=1)
        deal(keep, give, pos, both.reshape(SHARDS * 8, cols).astype(BF16), slice(4 * each, 4 * each + 8), 8)


def attention_back(pos, gatt, gathered, c, q, k, v, ps, plong, xs, xl, sums_f, sums_b, dub, dims):
    rows, width = gatt.shape
    short_rows, long_count, long_length, _ = dims
    each = width // SHARDS
    step = 256
    per = step // PAIR
    cols = pl.BlockSpec((rows, step), lambda g, *_: (0, g))
    dealt = pl.BlockSpec((CHIPS, 4 * each + 8, step), lambda g, *_: (0, 0, g))
    return pl.pallas_call(
        functools.partial(attention_back_body, dims),
        grid_spec=pltpu.PrefetchScalarGridSpec(
            num_scalar_prefetch=1,
            grid=(width // step,),
            in_specs=[
                whole(rows, width), cols,
                pl.BlockSpec((SHARDS, each, width), lambda g, *_: (0, 3, 0)),
                whole(rows, width), cols, cols, cols,
                pl.BlockSpec((per, 2 * short_rows, short_rows), lambda g, *_: (g, 0, 0)),
                pl.BlockSpec((long_count, per, 2 * long_length, long_length), lambda g, *_: (0, g, 0, 0)),
                whole(*xs.shape), whole(*xl.shape), whole(8, width), whole(8, width), whole(*dub.shape),
            ],
            out_specs=[dealt, dealt, cols, cols, cols],
            scratch_shapes=[
                pltpu.VMEM((rows, width), BF16), pltpu.VMEM((rows, step), BF16),
                pltpu.VMEM((width, width), BF16), pltpu.VMEM((8, width), F32),
            ],
        ),
        out_shape=[
            *[jax.ShapeDtypeStruct((CHIPS, 4 * each + 8, width), BF16)] * 2,
            *[jax.ShapeDtypeStruct((rows, width), BF16)] * 3,
        ],
        compiler_params=params(23),
        cost_estimate=cost(12 * rows * width * width, 25e6),
        name="attention_back",
    )(pos, gatt, gatt, gathered, c, q, k, v, ps, plong, xs, xl, sums_f, sums_b, dub)


def input_back_body(dims, gfs, dq, dk, dv, wq, wk, wv, gs_o, gl_o, total):
    step = pl.program_id(0)
    short_rows, width, cols = dims[0], gfs.shape[1], dq.shape[1]
    part = (
        nt(dq[...], wq[...].reshape(width, cols))
        + nt(dk[...], wk[...].reshape(width, cols))
        + nt(dv[...], wv[...].reshape(width, cols))
    )

    @pl.when(step == 0)
    def _():
        total[...] = gfs[...] + part

    @pl.when(step > 0)
    def _():
        total[...] += part

    @pl.when(step == pl.num_programs(0) - 1)
    def _():
        gs_o[...] = total[:short_rows]
        gl_o[...] = total[short_rows:]


def input_back(gfs, dq, dk, dv, gathered, dims):
    rows, width = gfs.shape
    each = width // SHARDS
    step = 256
    short_rows = dims[0]
    cols = pl.BlockSpec((rows, step), lambda g: (0, g))
    slab = lambda i: pl.BlockSpec((SHARDS, each, step), lambda g: (0, i, g))
    return pl.pallas_call(
        functools.partial(input_back_body, dims),
        grid=(width // step,),
        in_specs=[whole(rows, width), cols, cols, cols, slab(0), slab(1), slab(2)],
        out_specs=[whole(short_rows, width), whole(rows - short_rows, width)],
        scratch_shapes=[pltpu.VMEM((rows, width), F32)],
        out_shape=[
            jax.ShapeDtypeStruct((short_rows, width), F32),
            jax.ShapeDtypeStruct((rows - short_rows, width), F32),
        ],
        compiler_params=params(16),
        cost_estimate=cost(6 * rows * width * width, 12e6),
        name="input_back",
    )(gfs, dq, dk, dv, gathered, gathered, gathered)


def pair_sum(kept):
    parts = []
    for d in range(RING):
        at = slice(d * RING, (d + 1) * RING)
        rows = [(keep[at].astype(F32) + got[at].astype(F32)).astype(BF16) for keep, got in kept]
        parts.append(rows[0] if len(rows) == 1 else jnp.concatenate(rows, axis=1))
    return parts


def four_sum(own, left, right, far):
    return (own.astype(F32) + far.astype(F32)) + (left.astype(F32) + right.astype(F32))


def turn(delta, stage):
    moves = []
    for x in range(RING):
        for z in range(RING):
            for core in range(2):
                to_x, to_z = x, z
                if (core == 0) == (stage == 0):
                    to_x = (x + delta) % RING
                else:
                    to_z = (z + delta) % RING
                moves.append(((x * RING + z) * 2 + core, (to_x * RING + to_z) * 2 + core))
    return moves


def swap_cores(v):
    return lax.ppermute(v, "shard", [(i, i ^ 1) for i in range(SHARDS)])


def around(v, stage):
    return tuple(lax.ppermute(v[d] if isinstance(v, (list, tuple)) else v, "shard", turn(d, stage)) for d in (1, 3, 2))


def gather(shard):
    near = jnp.stack([shard, *around(shard, 1)])
    return near


def both_cores(pieces):
    return (*pieces, *(swap_cores(p) for p in pieces))


def second_turn(own, left, right, far):
    parts = [four_sum(own[d], left[d], right[d], far[d]).astype(BF16) for d in range(RING)]
    own = four_sum(parts[0], *around(parts, 1)).astype(BF16)
    return own, *(lax.ppermute(own, "rep", [(i, (i + d) % RING) for i in range(RING)]) for d in (1, 3, 2))


def replica_sum(own, left, right, far, at):
    return (own[at].astype(F32) + far[at].astype(F32)) + (left[at].astype(F32) + right[at].astype(F32))


def finish_attention_body(own, left, right, far, wqkv_o, wo_o, *vector_os):
    each, width = wo_o.shape
    for j in range(wqkv_o.shape[1] // width):
        at = slice(j * each, (j + 1) * each)
        wqkv_o[:, j * width : (j + 1) * width] = replica_sum(own, left, right, far, at)
    wo_o[...] = replica_sum(own, left, right, far, slice(3 * each, 4 * each))
    last = replica_sum(own, left, right, far, slice(4 * each, 4 * each + 8))[:, width - 256 :]
    for i, o in enumerate(vector_os[:-1]):
        o[...] = last[0:1, i * each : (i + 1) * each]
    o = vector_os[-1]
    o[...] = last[1:2, : o.shape[1]]


def finish_attention(arrays, tall):
    width = arrays[0].shape[1]
    each = width // SHARDS
    return pl.pallas_call(
        finish_attention_body,
        out_shape=[
            jax.ShapeDtypeStruct((each, 3 * width), F32),
            jax.ShapeDtypeStruct((each, width), F32),
            *[jax.ShapeDtypeStruct((1, each), F32)] * 8,
            jax.ShapeDtypeStruct((1, tall), F32),
        ],
        compiler_params=params(4),
        name="finish_attention",
    )(*arrays)


def finish_feed_body(own, left, right, far, up_o, down_o):
    each, wide = up_o.shape
    tall, width = down_o.shape
    down_o[...] = replica_sum(own, left, right, far, slice(0, tall))
    for j in range(wide // width):
        at = slice(tall + j * each, tall + (j + 1) * each)
        up_o[:, j * width : (j + 1) * width] = replica_sum(own, left, right, far, at)


def finish_feed(arrays, each, inner, tall):
    width = arrays[0].shape[1]
    return pl.pallas_call(
        finish_feed_body,
        out_shape=[jax.ShapeDtypeStruct((each, inner), F32), jax.ShapeDtypeStruct((tall, width), F32)],
        compiler_params=params(4),
        name="finish_feed",
    )(*arrays)


def on_device(
    short_tokens, long_tokens, short_lengths, long_lengths, short_cotangent, long_cotangent,
    input_weight, query_bias, value_bias, output_weight, output_bias, first_gain, first_shift,
    up_weight, up_bias, down_weight, down_bias, second_gain, second_shift,
):
    short_count, short_length, width = short_tokens.shape
    long_count, long_length, _ = long_tokens.shape
    dims = (short_count * short_length, long_count, long_length, short_length)
    each, inner, tall = width // SHARDS, up_weight.shape[1], down_weight.shape[0]
    xs, xl = short_tokens.reshape(-1, width), long_tokens.reshape(-1, width)
    cs, cl = short_cotangent.reshape(-1, width), long_cotangent.reshape(-1, width)
    index = lax.axis_index("shard")
    pos = jnp.stack([index // 8, (index // 2) % 4, index % 2]).astype(jnp.int32)

    packed_a, packed_f = pack(
        input_weight, output_weight, up_weight, down_weight,
        (query_bias, value_bias, output_bias, first_gain, first_shift, down_bias, second_gain, second_shift),
        up_bias,
    )
    near_a = gather(packed_a)
    near_f = gather(packed_f)
    far_f = around(near_f, 0)
    pieces_a = both_cores((near_a, *around(near_a, 0)))
    xs, near_f = lax.optimization_barrier((xs, near_f))
    q, k, v, c, ps, plong, unit1, inv1, low, vecs, ub, gathered_a = attention_forward(
        short_lengths, long_lengths, pos, xs, xl, pieces_a, inner, dims
    )
    low, *far_f = lax.optimization_barrier((low, *far_f))
    gelu, keep_d, give_d, gffn, gss, out_s, out_l, sums_f, gathered_f = feed_forward(
        short_lengths, long_lengths, pos, low, unit1, cs, cl, ub, vecs, dims=dims,
        pieces=both_cores((near_f, *far_f)),
    )
    got_d = swap_cores(give_d)
    keep_u, give_u, grad_up, dub = up_back(pos, gffn, gelu, gathered_f, low)
    got_u = swap_cores(give_u)
    gfs, gatt, sums_b = first_back(gss, grad_up, gathered_f, unit1, inv1, vecs)
    parts_f = pair_sum(((keep_d, got_d), (keep_u, got_u)))
    gatt, *parts_f = lax.optimization_barrier((gatt, *parts_f))
    around_f = around(parts_f, 0)
    keep_a, give_a, dq, dk, dv = attention_back(
        pos, gatt, gathered_a, c, q, k, v, ps, plong, xs, xl, sums_f, sums_b, dub, dims
    )
    give_a, *around_f = lax.optimization_barrier((give_a, *around_f))
    parts_a = pair_sum(((keep_a, swap_cores(give_a)),))
    gfs, *parts_a = lax.optimization_barrier((gfs, *parts_a))
    around_a = around(parts_a, 0)
    grad_s, grad_l = input_back(gfs, dq, dk, dv, gathered_a, dims)
    grad_s, *around_a = lax.optimization_barrier((grad_s, *around_a))
    up, down = finish_feed(second_turn(parts_f[0], *around_f), each, inner, tall)
    w_in, w_out, *vectors = finish_attention(second_turn(parts_a[0], *around_a), tall)
    vectors = [x.reshape(-1) for x in vectors]
    return (
        out_s.reshape(short_tokens.shape), out_l.reshape(long_tokens.shape),
        grad_s.reshape(short_tokens.shape), grad_l.reshape(long_tokens.shape),
        w_in, vectors[QB], vectors[VB], w_out, vectors[OB], vectors[G1], vectors[S1],
        up, vectors[8], down, vectors[DB], vectors[G2], vectors[S2],
    )


def solution(mesh):
    rows, flat = P(("rep", "shard"), None, None), P("shard")
    tall = P("shard", None)
    return jax.shard_map(
        on_device,
        mesh=mesh,
        in_specs=(
            rows, rows, P(("rep", "shard")), P(("rep", "shard")), rows, rows,
            tall, flat, flat, tall, flat, flat, flat, tall, flat, tall, flat, flat, flat,
        ),
        out_specs=(
            rows, rows, rows, rows,
            tall, flat, flat, tall, flat, flat, flat, tall, flat, tall, flat, flat, flat,
        ),
        check_vma=False,
    )
```

```python
import functools

import jax
import jax.numpy as jnp
from jax import lax
from jax.experimental import pallas as pl
from jax.experimental.pallas import tpu as pltpu
from jax.sharding import PartitionSpec as P

F32 = jnp.float32
BF16 = jnp.bfloat16
HEAD_DIM = 64
PAIR = 128
EPSILON = 1e-06
QB, VB, OB, G1, S1, DB, G2, S2 = range(8)
RING = 4
CHIPS = RING * RING
SHARDS = 2 * CHIPS


def nn(a, b):
    return lax.dot_general(a, b, (((1,), (0,)), ((), ())), preferred_element_type=F32)


def nt(a, b):
    return lax.dot_general(a, b, (((1,), (1,)), ((), ())), preferred_element_type=F32)


def tn(a, b):
    return lax.dot_general(a, b, (((0,), (0,)), ((), ())), preferred_element_type=F32)


def iota(shape, dim):
    return lax.broadcasted_iota(jnp.int32, shape, dim)


def row_of(ref, i):
    return ref[i : i + 1, :].astype(F32)


def whole(*shape):
    return pl.BlockSpec(shape, lambda g, *_: (0,) * len(shape))


def params(mebibytes):
    return pltpu.CompilerParams(vmem_limit_bytes=mebibytes * 1024 * 1024)


def cost(flops, moved):
    return pl.CostEstimate(flops=int(flops), bytes_accessed=int(moved), transcendentals=0)


def places(pos, x, z):
    along_x, along_z = (x - pos[0]) & (RING - 1), (z - pos[1]) & (RING - 1)
    return along_x * RING + along_z, along_z * RING + along_x


def deal(keep, give, pos, value, at, each):
    first = pos[2] == 0
    for x in range(RING):
        for z in range(RING):
            p0, p1 = places(pos, x, z)
            low = 2 * (x * RING + z) * each
            even, odd = value[low : low + each], value[low + each : low + 2 * each]
            keep[jnp.where(first, p0, p1), at] = jnp.where(first, even, odd)
            give[jnp.where(first, p1, p0), at] = jnp.where(first, odd, even)


def spread(owners, width):
    each = width // owners
    at = iota((owners, width), 1)
    low = iota((owners, width), 0) * each
    return (at >= low) & (at < low + each)


def column_rest(rows, width, each):
    at = iota((rows, width), 1)
    return at - (at // each) * each


def two_heads(pair):
    low_half = iota(pair.shape, 1) < HEAD_DIM
    zero = jnp.zeros_like(pair)
    return jnp.concatenate([jnp.where(low_half, pair, zero), jnp.where(low_half, zero, pair)], axis=0)


def own_lanes(stack):
    half = stack.shape[0] // 2
    return jnp.where(iota((half, stack.shape[1]), 1) < HEAD_DIM, stack[:half], stack[half:])


def normalized(hidden):
    center = hidden - jnp.mean(hidden, axis=-1, keepdims=True)
    spread_of = jnp.mean(center * center, axis=-1, keepdims=True)
    inverse = lax.rsqrt(spread_of + EPSILON)
    return center * inverse, inverse


def norm_back(scaled, unit, inverse):
    return inverse * (
        scaled
        - jnp.mean(scaled, axis=-1, keepdims=True)
        - unit * jnp.mean(scaled * unit, axis=-1, keepdims=True)
    )


def segments(dims):
    short_rows, long_count, long_length, _ = dims
    return [(0, short_rows, None)] + [
        (short_rows + i * long_length, long_length, i) for i in range(long_count)
    ]


def key_bias(slen, llen, short_length, rows, long_at):
    key = iota((rows, rows), 0)
    if long_at is not None:
        return jnp.where(key < llen[long_at], 0.0, -1e9).astype(F32)
    query = iota((rows, rows), 1)
    keep = jnp.zeros((rows, rows), jnp.bool_)
    for p in range(rows // short_length):
        low, high = p * short_length, (p + 1) * short_length
        keep = keep | ((key >= low) & (key < low + slen[p]) & (query >= low) & (query < high))
    return jnp.where(keep, 0.0, -1e9).astype(F32)


def valid_rows(slen, llen, dims):
    short_rows, long_count, long_length, short_length = dims
    parts = []
    at = iota((short_length, 1), 0)
    for p in range(short_rows // short_length):
        parts.append((at < slen[p]).astype(F32))
    at = iota((long_length, 1), 0)
    for p in range(long_count):
        parts.append((at < llen[p]).astype(F32))
    return jnp.concatenate(parts, axis=0)


def slabs_of(out, base, source, each, width):
    for j in range(source.shape[1] // width):
        out[base + j * each : base + (j + 1) * each] = source[:, j * width : (j + 1) * width]
    return base + source.shape[1] // width * each


def pack_body(wqkv, wo, wup, wdown, *rest):
    vectors, out = rest[:-1], rest[-1]
    each, width = wo.shape
    base = slabs_of(out, 0, wqkv, each, width)
    base = slabs_of(out, base, wo, each, width)
    out[base : base + 8] = jnp.zeros((8, width), BF16)
    for i, v in enumerate(vectors[:-1]):
        out[base : base + 1, i * each : (i + 1) * each] = v[...]
    out[base + 1 : base + 2, : vectors[-1].shape[1]] = vectors[-1][...]
    base = slabs_of(out, base + 8, wup, each, width)
    out[base:] = wdown[...]


def pack(wqkv, wo, wup, wdown, vectors, ub):
    each, width = wo.shape
    rows = wqkv.shape[1] // width * each + each + 8 + 2 * wdown.shape[0]
    return pl.pallas_call(
        pack_body,
        out_shape=jax.ShapeDtypeStruct((rows, width), BF16),
        compiler_params=params(58),
        name="pack",
    )(wqkv, wo, wup, wdown, *[v[None] for v in vectors], ub[None])


STEPS = (0, -1, 1, 2)


def gathered_at(pos, other, k, i):
    core = pos[2] ^ other
    x0, z0 = (pos[0] + STEPS[k]) & (RING - 1), (pos[1] + STEPS[i]) & (RING - 1)
    x1, z1 = (pos[0] + STEPS[i]) & (RING - 1), (pos[1] + STEPS[k]) & (RING - 1)
    return jnp.where(core == 0, (x0 * RING + z0) * 2, (x1 * RING + z1) * 2 + 1)


def arrivals(pos, pieces, target, sems, at):
    copies = []
    for other in range(2):
        for k in range(RING):
            for i in range(RING):
                n = (other * RING + k) * RING + i
                copies.append(
                    pltpu.make_async_copy(
                        pieces[other * RING + k].at[i, at], target.at[gathered_at(pos, other, k, i), at], sems.at[n]
                    )
                )
    return copies


def attention_forward_body(
    dims, slen, llen, pos, xs, xl, p0, p1, p2, p3, p4, p5, p6, p7,
    q_o, k_o, v_o, c_o, ps_o, pl_o, n_o, r_o, low_o, vecs_o, ub_o, gathered_o,
    x_all, total, wo_all, gathered, sems, out_sem,
):
    step = pl.program_id(0)
    short_rows, width = dims[0], x_all.shape[1]
    cols = q_o.shape[1]
    each = width // SHARDS
    keep_all = pltpu.make_async_copy(gathered, gathered_o, out_sem)

    @pl.when(step == 0)
    def _():
        copies = arrivals(pos, (p0, p1, p2, p3, p4, p5, p6, p7), gathered, sems, slice(None))
        for copy in copies:
            copy.start()
        x_all[:short_rows, :] = xs[...]
        x_all[short_rows:, :] = xl[...]
        total[...] = jnp.zeros_like(total)
        for copy in copies:
            copy.wait()
        keep_all.start()
        wo_all[...] = gathered[:, 3 * each : 4 * each].reshape(width, width)
        packed = gathered[:, 4 * each :]
        line = packed[:, 0, : 8 * each + 64]
        rest = column_rest(line.shape[1], width, each)
        mine = spread(SHARDS, width)
        for i in range(8):
            pick = (iota(rest.shape, 0) == rest + i * each).astype(BF16)
            row = jnp.sum(jnp.where(mine, nn(line, pick), 0.0), axis=0, keepdims=True)
            vecs_o[i : i + 1] = row.astype(BF16)
        inner = ub_o.shape[1]
        line = packed[:, 1, :128]
        pick = (iota((128, inner), 0) == column_rest(128, inner, inner // SHARDS)).astype(BF16)
        row = jnp.sum(jnp.where(spread(SHARDS, inner), nn(line, pick), 0.0), axis=0, keepdims=True)
        ub_o[...] = row.astype(BF16)

    x = x_all[...]
    at_cols = pl.ds(pl.multiple_of(step * cols, cols), cols)
    wq, wk, wv = (gathered[:, i * each : (i + 1) * each, at_cols].reshape(width, cols) for i in range(3))
    q_o[...] = (nn(x, wq) + vecs_o[QB : QB + 1, at_cols].astype(F32)).astype(BF16)
    k_o[...] = nn(x, wk).astype(BF16)
    v_o[...] = (nn(x, wv) + vecs_o[VB : VB + 1, at_cols].astype(F32)).astype(BF16)
    for first, rows, long_at in segments(dims):
        bias = key_bias(slen, llen, dims[3], rows, long_at)
        at = slice(first, first + rows)
        for pair in range(cols // PAIR):
            lanes = slice(pair * PAIR, (pair + 1) * PAIR)
            q = q_o[at, lanes] * jnp.asarray(HEAD_DIM**-0.5, BF16)
            scores = nt(two_heads(k_o[at, lanes]), q)
            probs = []
            for h in range(2):
                s = scores[h * rows : (h + 1) * rows] + bias
                e = jnp.exp(s - jnp.max(s, axis=0, keepdims=True))
                probs.append((e * (1.0 / jnp.sum(e, axis=0, keepdims=True))).astype(BF16))
            probs = jnp.concatenate(probs, axis=0)
            if long_at is None:
                ps_o[pair] = probs
            else:
                pl_o[long_at, pair] = probs
            c_o[at, lanes] = tn(two_heads(v_o[at, lanes]), probs).T.astype(BF16)
    total[...] += nn(c_o[...], wo_all[at_cols, :])

    @pl.when(step == pl.num_programs(0) - 1)
    def _():
        h = x_all[...].astype(F32) + (total[...] + row_of(vecs_o, OB))
        unit, inverse = normalized(h)
        n_o[...] = unit
        r_o[...] = inverse
        low_o[...] = (unit * row_of(vecs_o, G1) + row_of(vecs_o, S1)).astype(BF16)
        keep_all.wait()


def attention_forward(slen, llen, pos, xs, xl, pieces, inner, dims):
    rows, width = xs.shape[0] + xl.shape[0], xs.shape[1]
    short_rows, long_count, long_length, _ = dims
    step = 256
    steps, pairs = width // step, width // PAIR
    per = step // PAIR
    each_all = pieces[0].shape[1]
    cols = pl.BlockSpec((rows, step), lambda g, *_: (0, g))
    return pl.pallas_call(
        functools.partial(attention_forward_body, dims),
        grid_spec=pltpu.PrefetchScalarGridSpec(
            num_scalar_prefetch=3,
            grid=(steps,),
            in_specs=[
                whole(*xs.shape), whole(*xl.shape), *[pl.BlockSpec(memory_space=pl.ANY)] * 8,
            ],
            out_specs=[
                cols, cols, cols, cols,
                pl.BlockSpec((per, 2 * short_rows, short_rows), lambda g, *_: (g, 0, 0)),
                pl.BlockSpec((long_count, per, 2 * long_length, long_length), lambda g, *_: (0, g, 0, 0)),
                whole(rows, width), whole(rows, 1), whole(rows, width), whole(8, width), whole(1, inner),
                pl.BlockSpec(memory_space=pl.ANY),
            ],
            scratch_shapes=[
                pltpu.VMEM((rows, width), BF16), pltpu.VMEM((rows, width), F32), pltpu.VMEM((width, width), BF16),
                pltpu.VMEM((SHARDS, each_all, width), BF16), pltpu.SemaphoreType.DMA((SHARDS,)),
                pltpu.SemaphoreType.DMA(()),
            ],
        ),
        out_shape=[
            *[jax.ShapeDtypeStruct((rows, width), BF16)] * 4,
            jax.ShapeDtypeStruct((pairs, 2 * short_rows, short_rows), BF16),
            jax.ShapeDtypeStruct((long_count, pairs, 2 * long_length, long_length), BF16),
            jax.ShapeDtypeStruct((rows, width), F32),
            jax.ShapeDtypeStruct((rows, 1), F32),
            jax.ShapeDtypeStruct((rows, width), BF16),
            jax.ShapeDtypeStruct((8, width), BF16),
            jax.ShapeDtypeStruct((1, inner), BF16),
            jax.ShapeDtypeStruct((SHARDS, each_all, width), BF16),
        ],
        compiler_params=params(58),
        cost_estimate=cost(8 * rows * width * width, 20e6),
        name="attention_forward",
    )(slen, llen, pos, xs, xl, *pieces)


def feed_forward_body(
    dims, half,
    slen, llen, pos, low, unit1, cot_s, cot_l, ub, vecs, p0, p1, p2, p3, p4, p5, p6, p7,
    gelu_o, keep, give, gffn_o, gss_o, outs_o, outl_o, sums_o, gathered_o,
    hidden, total, wup, gathered, sems, out_sem,
):
    step = pl.program_id(0)
    short_rows = dims[0]
    block, width = hidden.shape[2], low.shape[1]
    each, tall = width // SHARDS, gathered.shape[1] // 2
    owners = SHARDS // half
    keep_all = pltpu.make_async_copy(gathered, gathered_o, out_sem)
    pieces = (p0, p1, p2, p3, p4, p5, p6, p7)
    ups = arrivals(pos, pieces, gathered, sems.at[0], slice(0, tall))
    downs = arrivals(pos, pieces, gathered, sems.at[1], slice(tall, 2 * tall))

    @pl.when(step == 0)
    def _():
        for copy in ups + downs:
            copy.start()
        for copy in ups:
            copy.wait()

    @pl.when(step < half)
    def _():
        for j in range(half):

            @pl.when(step == j)
            def _():
                wup[...] = gathered[:, j * each : (j + 1) * each].reshape(width, block)

        pre = nn(low[...], wup[...]) + ub[...].astype(F32)
        cdf = 0.5 + 0.5 * lax.erf(pre * (0.5**0.5))
        density = jnp.exp(-0.5 * pre * pre) * (0.5 / jnp.pi) ** 0.5
        h = (pre * cdf).astype(BF16)
        gelu_o[...] = (cdf + pre * density).astype(BF16)
        hidden[step] = h

        @pl.when(step == 0)
        def _():
            for copy in downs:
                copy.wait()
            keep_all.start()

        part = nn(h, gathered[pl.ds(step * owners, owners), tall:].reshape(block, width))

        @pl.when(step == 0)
        def _():
            total[...] = part

        @pl.when(step > 0)
        def _():
            total[...] += part

    @pl.when(step == half - 1)
    def _():
        first = unit1[...] * row_of(vecs, G1) + row_of(vecs, S1)
        unit, inverse = normalized(first + (total[...] + row_of(vecs, DB)))
        valid = valid_rows(slen, llen, dims)
        out = ((unit * row_of(vecs, G2) + row_of(vecs, S2)) * valid).astype(BF16)
        outs_o[...] = out[:short_rows]
        outl_o[...] = out[short_rows:]
        cot = jnp.concatenate([cot_s[...], cot_l[...]], axis=0).astype(F32) * valid
        back = norm_back(cot * row_of(vecs, G2), unit, inverse)
        gss_o[...] = back
        low_back = back.astype(BF16)
        gffn_o[...] = low_back
        sums_o[...] = jnp.zeros_like(sums_o)
        sums_o[DB : DB + 1] = jnp.sum(low_back.astype(F32), axis=0, keepdims=True)
        sums_o[G2 : G2 + 1] = jnp.sum(cot * unit, axis=0, keepdims=True)
        sums_o[S2 : S2 + 1] = jnp.sum(cot, axis=0, keepdims=True)

    @pl.when(step >= half)
    def _():
        x = step - half
        grad = tn(hidden[x], gffn_o[...]).astype(BF16)
        each = block // (2 * RING)
        first = pos[2] == 0
        for z in range(RING):
            p0, p1 = places(pos, x, z)
            even, odd = grad[2 * z * each : (2 * z + 1) * each], grad[(2 * z + 1) * each : (2 * z + 2) * each]
            keep[jnp.where(first, p0, p1)] = jnp.where(first, even, odd)
            give[jnp.where(first, p1, p0)] = jnp.where(first, odd, even)

    @pl.when(step == 2 * half - 1)
    def _():
        keep_all.wait()


def feed_forward(slen, llen, pos, low, unit1, cot_s, cot_l, ub, vecs, pieces, dims):
    rows, width = low.shape
    inner = ub.shape[1]
    half = RING
    block = inner // half
    tall = inner // SHARDS
    step_of = lambda g: jnp.minimum(g, half - 1)
    cols = lambda r: pl.BlockSpec((r, block), lambda g, *_: (0, step_of(g)))
    return pl.pallas_call(
        functools.partial(feed_forward_body, dims, half),
        grid_spec=pltpu.PrefetchScalarGridSpec(
            num_scalar_prefetch=3,
            grid=(2 * half,),
            in_specs=[
                whole(rows, width), whole(rows, width), whole(*cot_s.shape), whole(*cot_l.shape),
                cols(1), whole(*vecs.shape), *[pl.BlockSpec(memory_space=pl.ANY)] * 8,
            ],
            out_specs=[
                cols(rows),
                whole(CHIPS, tall, width), whole(CHIPS, tall, width),
                whole(rows, width), whole(rows, width), whole(*cot_s.shape), whole(*cot_l.shape),
                whole(8, width), pl.BlockSpec(memory_space=pl.ANY),
            ],
            scratch_shapes=[
                pltpu.VMEM((half, rows, block), BF16), pltpu.VMEM((rows, width), F32), pltpu.VMEM((width, block), BF16),
                pltpu.VMEM((SHARDS, 2 * tall, width), BF16), pltpu.SemaphoreType.DMA((2, SHARDS)),
                pltpu.SemaphoreType.DMA(()),
            ],
        ),
        out_shape=[
            jax.ShapeDtypeStruct((rows, inner), BF16),
            jax.ShapeDtypeStruct((CHIPS, tall, width), BF16),
            jax.ShapeDtypeStruct((CHIPS, tall, width), BF16),
            jax.ShapeDtypeStruct((rows, width), BF16),
            jax.ShapeDtypeStruct((rows, width), F32),
            jax.ShapeDtypeStruct(cot_s.shape, BF16),
            jax.ShapeDtypeStruct(cot_l.shape, BF16),
            jax.ShapeDtypeStruct((8, width), F32),
            jax.ShapeDtypeStruct((SHARDS, 2 * tall, width), BF16),
        ],
        compiler_params=params(58),
        cost_estimate=cost(6 * rows * width * inner, 30e6),
        name="feed_forward",
    )(slen, llen, pos, low, unit1, cot_s, cot_l, ub, vecs, *pieces)


def up_back_body(pos, gffn, gelu, wdown, low, keep, give, up_o, dub_o):
    width, block = low.shape[1], gelu.shape[1]
    up = (nt(gffn[...], wdown[...].reshape(block, width)) * gelu[...].astype(F32)).astype(BF16)
    up_o[...] = up
    dub_o[...] = jnp.sum(up.astype(F32), axis=0, keepdims=True)
    deal(keep, give, pos, tn(low[...], up).astype(BF16), slice(None), width // SHARDS)


def up_back(pos, gffn, gelu, gathered, low):
    rows, width = low.shape
    inner = gelu.shape[1]
    half = RING
    block = inner // half
    each, tall = width // SHARDS, inner // SHARDS
    cols = lambda r: pl.BlockSpec((r, block), lambda g, *_: (0, g))
    dealt = pl.BlockSpec((CHIPS, each, width), lambda g, *_: (0, g, 0))
    return pl.pallas_call(
        up_back_body,
        grid_spec=pltpu.PrefetchScalarGridSpec(
            num_scalar_prefetch=1,
            grid=(half,),
            in_specs=[
                whole(rows, width), cols(rows),
                pl.BlockSpec((SHARDS // half, tall, width), lambda g, *_: (g, 1, 0)),
                whole(rows, width),
            ],
            out_specs=[dealt, dealt, cols(rows), cols(1)],
        ),
        out_shape=[
            jax.ShapeDtypeStruct((CHIPS, tall, width), BF16),
            jax.ShapeDtypeStruct((CHIPS, tall, width), BF16),
            jax.ShapeDtypeStruct((rows, inner), BF16),
            jax.ShapeDtypeStruct((1, inner), F32),
        ],
        compiler_params=params(58),
        cost_estimate=cost(4 * rows * width * inner, 20e6),
        name="up_back",
    )(pos, gffn, gelu, gathered, low)


def first_back_body(gss, up, wup, unit1, inv1, vecs, gfs_o, gatt_o, sums_o, total):
    step = pl.program_id(0)
    width, block = gss.shape[1], up.shape[1]
    part = nt(up[...], wup[...].reshape(width, block))

    @pl.when(step == 0)
    def _():
        total[...] = part

    @pl.when(step > 0)
    def _():
        total[...] += part

    @pl.when(step == pl.num_programs(0) - 1)
    def _():
        grad = gss[...] + total[...]
        unit = unit1[...]
        back = norm_back(grad * row_of(vecs, G1), unit, inv1[...])
        gfs_o[...] = back
        low_back = back.astype(BF16)
        gatt_o[...] = low_back
        sums_o[...] = jnp.zeros_like(sums_o)
        sums_o[OB : OB + 1] = jnp.sum(low_back.astype(F32), axis=0, keepdims=True)
        sums_o[G1 : G1 + 1] = jnp.sum(grad * unit, axis=0, keepdims=True)
        sums_o[S1 : S1 + 1] = jnp.sum(grad, axis=0, keepdims=True)


def first_back(gss, up, gathered, unit1, inv1, vecs):
    rows, width = gss.shape
    inner = up.shape[1]
    half = RING
    block = inner // half
    return pl.pallas_call(
        first_back_body,
        grid=(half,),
        in_specs=[
            whole(rows, width), pl.BlockSpec((rows, block), lambda g: (0, g)),
            pl.BlockSpec((SHARDS, width // SHARDS, width), lambda g: (0, g, 0)),
            whole(rows, width), whole(rows, 1), whole(*vecs.shape),
        ],
        out_specs=[whole(rows, width), whole(rows, width), whole(8, width)],
        scratch_shapes=[pltpu.VMEM((rows, width), F32)],
        out_shape=[
            jax.ShapeDtypeStruct((rows, width), F32),
            jax.ShapeDtypeStruct((rows, width), BF16),
            jax.ShapeDtypeStruct((8, width), F32),
        ],
        compiler_params=params(58),
        cost_estimate=cost(2 * rows * width * inner, 15e6),
        name="first_back",
    )(gss, up, gathered, unit1, inv1, vecs)


def attention_back_body(
    dims,
    pos, gatt, gatt_cols, wo_block, c, q, k, v, ps, plong, xs, xl, sums_f, sums_b, dub,
    keep, give, dq_o, dk_o, dv_o,
    x_all, gc, wo_all, sums,
):
    step = pl.program_id(0)
    short_rows, width = dims[0], x_all.shape[1]
    cols = q.shape[1]
    each = width // SHARDS
    at_cols = pl.ds(pl.multiple_of(step * cols, cols), cols)

    @pl.when(step == 0)
    def _():
        x_all[:short_rows, :] = xs[...]
        x_all[short_rows:, :] = xl[...]
        wo_all[...] = wo_block[...].reshape(width, width)
        sums[...] = sums_f[...] + sums_b[...]

    deal(keep, give, pos, tn(c[...], gatt_cols[...]).astype(BF16), slice(3 * each, 4 * each), each)
    gc[...] = nt(gatt[...], wo_all[at_cols, :]).astype(BF16)
    scale = HEAD_DIM**-0.5
    for first, rows, long_at in segments(dims):
        at = slice(first, first + rows)
        for pair in range(cols // PAIR):
            lanes = slice(pair * PAIR, (pair + 1) * PAIR)
            probs = ps[pair] if long_at is None else plong[long_at, pair]
            grad = gc[at, lanes]
            dp = nt(two_heads(v[at, lanes]), grad)
            ds = []
            for h in range(2):
                half = slice(h * rows, (h + 1) * rows)
                p = probs[half].astype(F32)
                d = dp[half]
                ds.append((p * (d - jnp.sum(d * p, axis=0, keepdims=True))).astype(BF16))
            ds = jnp.concatenate(ds, axis=0)
            dv_o[at, lanes] = own_lanes(nn(probs, grad)).astype(BF16)
            dk_o[at, lanes] = (own_lanes(nn(ds, q[at, lanes])) * scale).astype(BF16)
            dq_o[at, lanes] = (tn(two_heads(k[at, lanes]), ds).T * scale).astype(BF16)
    x = x_all[...]
    for i, d in enumerate((dq_o, dk_o, dv_o)):
        deal(keep, give, pos, tn(x, d[...]).astype(BF16), slice(i * each, (i + 1) * each), each)
    sums[QB : QB + 1, at_cols] = jnp.sum(dq_o[...].astype(F32), axis=0, keepdims=True)
    sums[VB : VB + 1, at_cols] = jnp.sum(dv_o[...].astype(F32), axis=0, keepdims=True)
    keep[:, 4 * each :] = jnp.zeros((CHIPS, 8, cols), BF16)
    give[:, 4 * each :] = jnp.zeros((CHIPS, 8, cols), BF16)

    @pl.when(step == pl.num_programs(0) - 1)
    def _():
        mine = spread(SHARDS, width)
        rest = column_rest(cols, width, each)
        line = jnp.zeros((SHARDS, cols), F32)
        for i in range(8):
            put = (iota(rest.shape, 0) == rest + i * each).astype(BF16)
            line += nt(jnp.where(mine, sums[i : i + 1], 0.0).astype(BF16), put)
        inner = dub.shape[1]
        put = (iota((cols, inner), 0) == column_rest(cols, inner, inner // SHARDS)).astype(BF16)
        wide = nt(jnp.where(spread(SHARDS, inner), dub[...], 0.0).astype(BF16), put)
        both = jnp.concatenate([line[:, None], wide[:, None], jnp.zeros((SHARDS, 6, cols), F32)], axis=1)
        deal(keep, give, pos, both.reshape(SHARDS * 8, cols).astype(BF16), slice(4 * each, 4 * each + 8), 8)


def attention_back(pos, gatt, gathered, c, q, k, v, ps, plong, xs, xl, sums_f, sums_b, dub, dims):
    rows, width = gatt.shape
    short_rows, long_count, long_length, _ = dims
    each = width // SHARDS
    step = 256
    per = step // PAIR
    cols = pl.BlockSpec((rows, step), lambda g, *_: (0, g))
    dealt = pl.BlockSpec((CHIPS, 4 * each + 8, step), lambda g, *_: (0, 0, g))
    return pl.pallas_call(
        functools.partial(attention_back_body, dims),
        grid_spec=pltpu.PrefetchScalarGridSpec(
            num_scalar_prefetch=1,
            grid=(width // step,),
            in_specs=[
                whole(rows, width), cols,
                pl.BlockSpec((SHARDS, each, width), lambda g, *_: (0, 3, 0)),
                whole(rows, width), cols, cols, cols,
                pl.BlockSpec((per, 2 * short_rows, short_rows), lambda g, *_: (g, 0, 0)),
                pl.BlockSpec((long_count, per, 2 * long_length, long_length), lambda g, *_: (0, g, 0, 0)),
                whole(*xs.shape), whole(*xl.shape), whole(8, width), whole(8, width), whole(*dub.shape),
            ],
            out_specs=[dealt, dealt, cols, cols, cols],
            scratch_shapes=[
                pltpu.VMEM((rows, width), BF16), pltpu.VMEM((rows, step), BF16),
                pltpu.VMEM((width, width), BF16), pltpu.VMEM((8, width), F32),
            ],
        ),
        out_shape=[
            *[jax.ShapeDtypeStruct((CHIPS, 4 * each + 8, width), BF16)] * 2,
            *[jax.ShapeDtypeStruct((rows, width), BF16)] * 3,
        ],
        compiler_params=params(58),
        cost_estimate=cost(12 * rows * width * width, 25e6),
        name="attention_back",
    )(pos, gatt, gatt, gathered, c, q, k, v, ps, plong, xs, xl, sums_f, sums_b, dub)


def input_back_body(dims, gfs, dq, dk, dv, wq, wk, wv, gs_o, gl_o, total):
    step = pl.program_id(0)
    short_rows, width, cols = dims[0], gfs.shape[1], dq.shape[1]
    part = (
        nt(dq[...], wq[...].reshape(width, cols))
        + nt(dk[...], wk[...].reshape(width, cols))
        + nt(dv[...], wv[...].reshape(width, cols))
    )

    @pl.when(step == 0)
    def _():
        total[...] = gfs[...] + part

    @pl.when(step > 0)
    def _():
        total[...] += part

    @pl.when(step == pl.num_programs(0) - 1)
    def _():
        gs_o[...] = total[:short_rows]
        gl_o[...] = total[short_rows:]


def input_back(gfs, dq, dk, dv, gathered, dims):
    rows, width = gfs.shape
    each = width // SHARDS
    step = 256
    short_rows = dims[0]
    cols = pl.BlockSpec((rows, step), lambda g: (0, g))
    slab = lambda i: pl.BlockSpec((SHARDS, each, step), lambda g: (0, i, g))
    return pl.pallas_call(
        functools.partial(input_back_body, dims),
        grid=(width // step,),
        in_specs=[whole(rows, width), cols, cols, cols, slab(0), slab(1), slab(2)],
        out_specs=[whole(short_rows, width), whole(rows - short_rows, width)],
        scratch_shapes=[pltpu.VMEM((rows, width), F32)],
        out_shape=[
            jax.ShapeDtypeStruct((short_rows, width), F32),
            jax.ShapeDtypeStruct((rows - short_rows, width), F32),
        ],
        compiler_params=params(16),
        cost_estimate=cost(6 * rows * width * width, 12e6),
        name="input_back",
    )(gfs, dq, dk, dv, gathered, gathered, gathered)


def pair_sum(kept):
    parts = []
    for d in range(RING):
        at = slice(d * RING, (d + 1) * RING)
        rows = [(keep[at].astype(F32) + got[at].astype(F32)).astype(BF16) for keep, got in kept]
        parts.append(rows[0] if len(rows) == 1 else jnp.concatenate(rows, axis=1))
    return parts


def four_sum(own, left, right, far):
    return (own.astype(F32) + far.astype(F32)) + (left.astype(F32) + right.astype(F32))


def turn(delta, stage):
    moves = []
    for x in range(RING):
        for z in range(RING):
            for core in range(2):
                to_x, to_z = x, z
                if (core == 0) == (stage == 0):
                    to_x = (x + delta) % RING
                else:
                    to_z = (z + delta) % RING
                moves.append(((x * RING + z) * 2 + core, (to_x * RING + to_z) * 2 + core))
    return moves


def swap_cores(v):
    return lax.ppermute(v, "shard", [(i, i ^ 1) for i in range(SHARDS)])


def around(v, stage):
    return tuple(lax.ppermute(v[d] if isinstance(v, (list, tuple)) else v, "shard", turn(d, stage)) for d in (1, 3, 2))


def both_cores(pieces):
    return (*pieces, *(swap_cores(p) for p in pieces))


def second_turn(own, left, right, far):
    parts = [four_sum(own[d], left[d], right[d], far[d]).astype(BF16) for d in range(RING)]
    own = four_sum(parts[0], *around(parts, 1)).astype(BF16)
    return own, *(lax.ppermute(own, "rep", [(i, (i + d) % RING) for i in range(RING)]) for d in (1, 3, 2))


def replica_sum(own, left, right, far, at):
    return (own[at].astype(F32) + far[at].astype(F32)) + (left[at].astype(F32) + right[at].astype(F32))


def finish_attention_body(own, left, right, far, wqkv_o, wo_o, *vector_os):
    each, width = wo_o.shape
    for j in range(wqkv_o.shape[1] // width):
        at = slice(j * each, (j + 1) * each)
        wqkv_o[:, j * width : (j + 1) * width] = replica_sum(own, left, right, far, at)
    wo_o[...] = replica_sum(own, left, right, far, slice(3 * each, 4 * each))
    last = replica_sum(own, left, right, far, slice(4 * each, 4 * each + 8))[:, width - 256 :]
    for i, o in enumerate(vector_os[:-1]):
        o[...] = last[0:1, i * each : (i + 1) * each]
    o = vector_os[-1]
    o[...] = last[1:2, : o.shape[1]]


def finish_attention(arrays, tall):
    width = arrays[0].shape[1]
    each = width // SHARDS
    return pl.pallas_call(
        finish_attention_body,
        out_shape=[
            jax.ShapeDtypeStruct((each, 3 * width), F32),
            jax.ShapeDtypeStruct((each, width), F32),
            *[jax.ShapeDtypeStruct((1, each), F32)] * 8,
            jax.ShapeDtypeStruct((1, tall), F32),
        ],
        compiler_params=params(4),
        name="finish_attention",
    )(*arrays)


def finish_feed_body(own, left, right, far, up_o, down_o):
    each, wide = up_o.shape
    tall, width = down_o.shape
    down_o[...] = replica_sum(own, left, right, far, slice(0, tall))
    for j in range(wide // width):
        at = slice(tall + j * each, tall + (j + 1) * each)
        up_o[:, j * width : (j + 1) * width] = replica_sum(own, left, right, far, at)


def finish_feed(arrays, each, inner, tall):
    width = arrays[0].shape[1]
    return pl.pallas_call(
        finish_feed_body,
        out_shape=[jax.ShapeDtypeStruct((each, inner), F32), jax.ShapeDtypeStruct((tall, width), F32)],
        compiler_params=params(4),
        name="finish_feed",
    )(*arrays)


def on_device(
    short_tokens, long_tokens, short_lengths, long_lengths, short_cotangent, long_cotangent,
    input_weight, query_bias, value_bias, output_weight, output_bias, first_gain, first_shift,
    up_weight, up_bias, down_weight, down_bias, second_gain, second_shift,
):
    short_count, short_length, width = short_tokens.shape
    long_count, long_length, _ = long_tokens.shape
    dims = (short_count * short_length, long_count, long_length, short_length)
    each, inner, tall = width // SHARDS, up_weight.shape[1], down_weight.shape[0]
    xs, xl = short_tokens.reshape(-1, width), long_tokens.reshape(-1, width)
    cs, cl = short_cotangent.reshape(-1, width), long_cotangent.reshape(-1, width)
    index = lax.axis_index("shard")
    pos = jnp.stack([index // 8, (index // 2) % 4, index % 2]).astype(jnp.int32)

    packed = pack(
        input_weight, output_weight, up_weight, down_weight,
        (query_bias, value_bias, output_bias, first_gain, first_shift, down_bias, second_gain, second_shift),
        up_bias,
    )
    near = (packed, *around(packed, 1))
    cut = 4 * each + 8
    near_a = jnp.stack([n[:cut] for n in near])
    near_f = jnp.stack([n[cut:] for n in near])
    around_a = around(near_a, 0)
    near_f, left_a = lax.optimization_barrier((near_f, around_a[0]))
    far_f = around(near_f, 0)
    pieces_a = both_cores((near_a, left_a, *around_a[1:]))
    xs, near_f = lax.optimization_barrier((xs, near_f))
    q, k, v, c, ps, plong, unit1, inv1, low, vecs, ub, gathered_a = attention_forward(
        short_lengths, long_lengths, pos, xs, xl, pieces_a, inner, dims
    )
    low, *far_f = lax.optimization_barrier((low, *far_f))
    gelu, keep_d, give_d, gffn, gss, out_s, out_l, sums_f, gathered_f = feed_forward(
        short_lengths, long_lengths, pos, low, unit1, cs, cl, ub, vecs, dims=dims,
        pieces=both_cores((near_f, *far_f)),
    )
    got_d = swap_cores(give_d)
    keep_u, give_u, grad_up, dub = up_back(pos, gffn, gelu, gathered_f, low)
    got_u = swap_cores(give_u)
    gfs, gatt, sums_b = first_back(gss, grad_up, gathered_f, unit1, inv1, vecs)
    parts_f = pair_sum(((keep_d, got_d), (keep_u, got_u)))
    gatt, *parts_f = lax.optimization_barrier((gatt, *parts_f))
    around_f = around(parts_f, 0)
    keep_a, give_a, dq, dk, dv = attention_back(
        pos, gatt, gathered_a, c, q, k, v, ps, plong, xs, xl, sums_f, sums_b, dub, dims
    )
    give_a, *around_f = lax.optimization_barrier((give_a, *around_f))
    parts_a = pair_sum(((keep_a, swap_cores(give_a)),))
    gfs, *parts_a = lax.optimization_barrier((gfs, *parts_a))
    around_a = around(parts_a, 0)
    grad_s, grad_l = input_back(gfs, dq, dk, dv, gathered_a, dims)
    grad_s, *around_a = lax.optimization_barrier((grad_s, *around_a))
    up, down = finish_feed(second_turn(parts_f[0], *around_f), each, inner, tall)
    w_in, w_out, *vectors = finish_attention(second_turn(parts_a[0], *around_a), tall)
    vectors = [x.reshape(-1) for x in vectors]
    return (
        out_s.reshape(short_tokens.shape), out_l.reshape(long_tokens.shape),
        grad_s.reshape(short_tokens.shape), grad_l.reshape(long_tokens.shape),
        w_in, vectors[QB], vectors[VB], w_out, vectors[OB], vectors[G1], vectors[S1],
        up, vectors[8], down, vectors[DB], vectors[G2], vectors[S2],
    )


def solution(mesh):
    rows, flat = P(("rep", "shard"), None, None), P("shard")
    tall = P("shard", None)
    return jax.shard_map(
        on_device,
        mesh=mesh,
        in_specs=(
            rows, rows, P(("rep", "shard")), P(("rep", "shard")), rows, rows,
            tall, flat, flat, tall, flat, flat, flat, tall, flat, tall, flat, flat, flat,
        ),
        out_specs=(
            rows, rows, rows, rows,
            tall, flat, flat, tall, flat, flat, flat, tall, flat, tall, flat, flat, flat,
        ),
        check_vma=False,
    )
```

```python
import functools

import jax
import jax.numpy as jnp
from jax import lax
from jax.experimental import pallas as pl
from jax.experimental.pallas import tpu as pltpu
from jax.sharding import PartitionSpec as P

F32 = jnp.float32
BF16 = jnp.bfloat16
HEAD_DIM = 64
PAIR = 128
EPSILON = 1e-06
BACK_MIB = 58
QB, VB, OB, G1, S1, DB, G2, S2 = range(8)
RING = 4
CHIPS = RING * RING
SHARDS = 2 * CHIPS


def nn(a, b):
    return lax.dot_general(a, b, (((1,), (0,)), ((), ())), preferred_element_type=F32)


def nt(a, b):
    return lax.dot_general(a, b, (((1,), (1,)), ((), ())), preferred_element_type=F32)


def tn(a, b):
    return lax.dot_general(a, b, (((0,), (0,)), ((), ())), preferred_element_type=F32)


def iota(shape, dim):
    return lax.broadcasted_iota(jnp.int32, shape, dim)


def row_of(ref, i):
    return ref[i : i + 1, :].astype(F32)


def whole(*shape):
    return pl.BlockSpec(shape, lambda g, *_: (0,) * len(shape))


def params(mebibytes):
    return pltpu.CompilerParams(vmem_limit_bytes=mebibytes * 1024 * 1024)


def cost(flops, moved):
    return pl.CostEstimate(flops=int(flops), bytes_accessed=int(moved), transcendentals=0)


def places(pos, x, z):
    along_x, along_z = (x - pos[0]) & (RING - 1), (z - pos[1]) & (RING - 1)
    return along_x * RING + along_z, along_z * RING + along_x


def deal(keep, give, pos, value, at, each):
    first = pos[2] == 0
    for x in range(RING):
        for z in range(RING):
            p0, p1 = places(pos, x, z)
            low = 2 * (x * RING + z) * each
            even, odd = value[low : low + each], value[low + each : low + 2 * each]
            keep[jnp.where(first, p0, p1), at] = jnp.where(first, even, odd)
            give[jnp.where(first, p1, p0), at] = jnp.where(first, odd, even)


def spread(owners, width):
    each = width // owners
    at = iota((owners, width), 1)
    low = iota((owners, width), 0) * each
    return (at >= low) & (at < low + each)


def column_rest(rows, width, each):
    at = iota((1, width), 1)
    return jnp.broadcast_to(at - (at // each) * each, (rows, width))


def two_heads(pair):
    low_half = iota(pair.shape, 1) < HEAD_DIM
    zero = jnp.zeros_like(pair)
    return jnp.concatenate([jnp.where(low_half, pair, zero), jnp.where(low_half, zero, pair)], axis=0)


def own_lanes(stack):
    half = stack.shape[0] // 2
    return jnp.where(iota((half, stack.shape[1]), 1) < HEAD_DIM, stack[:half], stack[half:])


def normalized(hidden):
    center = hidden - jnp.mean(hidden, axis=-1, keepdims=True)
    spread_of = jnp.mean(center * center, axis=-1, keepdims=True)
    inverse = lax.rsqrt(spread_of + EPSILON)
    return center * inverse, inverse


def norm_back(scaled, unit, inverse):
    return inverse * (
        scaled
        - jnp.mean(scaled, axis=-1, keepdims=True)
        - unit * jnp.mean(scaled * unit, axis=-1, keepdims=True)
    )


def segments(dims):
    short_rows, long_count, long_length, _ = dims
    return [(0, short_rows, None)] + [
        (short_rows + i * long_length, long_length, i) for i in range(long_count)
    ]


def key_bias(slen, llen, short_length, rows, long_at):
    key = iota((rows, rows), 0)
    if long_at is not None:
        return jnp.where(key < llen[long_at], 0.0, -1e9).astype(F32)
    query = iota((rows, rows), 1)
    keep = jnp.zeros((rows, rows), jnp.bool_)
    for p in range(rows // short_length):
        low, high = p * short_length, (p + 1) * short_length
        keep = keep | ((key >= low) & (key < low + slen[p]) & (query >= low) & (query < high))
    return jnp.where(keep, 0.0, -1e9).astype(F32)


def valid_rows(slen, llen, dims):
    short_rows, long_count, long_length, short_length = dims
    parts = []
    at = iota((short_length, 1), 0)
    for p in range(short_rows // short_length):
        parts.append((at < slen[p]).astype(F32))
    at = iota((long_length, 1), 0)
    for p in range(long_count):
        parts.append((at < llen[p]).astype(F32))
    return jnp.concatenate(parts, axis=0)


def slabs_of(out, base, source, each, width):
    for j in range(source.shape[1] // width):
        out[base + j * each : base + (j + 1) * each] = source[:, j * width : (j + 1) * width]
    return base + source.shape[1] // width * each


def pack_body(wqkv, wo, wup, wdown, *rest):
    vectors, out = rest[:-1], rest[-1]
    each, width = wo.shape
    base = slabs_of(out, 0, wqkv, each, width)
    base = slabs_of(out, base, wo, each, width)
    out[base : base + 8] = jnp.zeros((8, width), BF16)
    for i, v in enumerate(vectors[:-1]):
        out[base : base + 1, i * each : (i + 1) * each] = v[...]
    out[base + 1 : base + 2, : vectors[-1].shape[1]] = vectors[-1][...]
    base = slabs_of(out, base + 8, wup, each, width)
    out[base:] = wdown[...]


def pack(wqkv, wo, wup, wdown, vectors, ub):
    each, width = wo.shape
    rows = wqkv.shape[1] // width * each + each + 8 + 2 * wdown.shape[0]
    return pl.pallas_call(
        pack_body,
        out_shape=jax.ShapeDtypeStruct((rows, width), BF16),
        compiler_params=params(58),
        name="pack",
    )(wqkv, wo, wup, wdown, *[v[None] for v in vectors], ub[None])


STEPS = (0, -1, 1, 2)


def gathered_at(pos, other, k, i):
    core = pos[2] ^ other
    x0, z0 = (pos[0] + STEPS[k]) & (RING - 1), (pos[1] + STEPS[i]) & (RING - 1)
    x1, z1 = (pos[0] + STEPS[i]) & (RING - 1), (pos[1] + STEPS[k]) & (RING - 1)
    return jnp.where(core == 0, (x0 * RING + z0) * 2, (x1 * RING + z1) * 2 + 1)


def arrivals(pos, pieces, target, sems, at):
    copies = []
    for other in range(2):
        for k in range(RING):
            for i in range(RING):
                n = (other * RING + k) * RING + i
                copies.append(
                    pltpu.make_async_copy(
                        pieces[other * RING + k].at[i, at], target.at[gathered_at(pos, other, k, i), at], sems.at[n]
                    )
                )
    return copies


def attention_forward_body(
    dims, slen, llen, pos, xs, xl, p0, p1, p2, p3, p4, p5, p6, p7,
    q_o, k_o, v_o, c_o, ps_o, pl_o, n_o, r_o, vecs_o, ub_o, gathered_o,
    x_all, total, wo_all, gathered, sems, out_sem,
):
    step = pl.program_id(0)
    short_rows, width = dims[0], x_all.shape[1]
    cols = q_o.shape[1]
    each = width // SHARDS
    keep_all = pltpu.make_async_copy(gathered, gathered_o, out_sem)

    @pl.when(step == 0)
    def _():
        copies = arrivals(pos, (p0, p1, p2, p3, p4, p5, p6, p7), gathered, sems, slice(None))
        for copy in copies:
            copy.start()
        x_all[:short_rows, :] = xs[...]
        x_all[short_rows:, :] = xl[...]
        total[...] = jnp.zeros_like(total)
        for copy in copies:
            copy.wait()
        keep_all.start()
        wo_all[...] = gathered[:, 3 * each : 4 * each].reshape(width, width)
        packed = gathered[:, 4 * each :]
        line = packed[:, 0, : 8 * each + 64]
        rest = column_rest(line.shape[1], width, each)
        mine = spread(SHARDS, width)
        for i in range(8):
            pick = (iota(rest.shape, 0) == rest + i * each).astype(BF16)
            row = jnp.sum(jnp.where(mine, nn(line, pick), 0.0), axis=0, keepdims=True)
            vecs_o[i : i + 1] = row.astype(BF16)
        inner = ub_o.shape[1]
        line = packed[:, 1, :128]
        pick = (iota((128, inner), 0) == column_rest(128, inner, inner // SHARDS)).astype(BF16)
        row = jnp.sum(jnp.where(spread(SHARDS, inner), nn(line, pick), 0.0), axis=0, keepdims=True)
        ub_o[...] = row.astype(BF16)

    x = x_all[...]
    at_cols = pl.ds(pl.multiple_of(step * cols, cols), cols)
    wq, wk, wv = (gathered[:, i * each : (i + 1) * each, at_cols].reshape(width, cols) for i in range(3))
    q_o[...] = (nn(x, wq) + vecs_o[QB : QB + 1, at_cols].astype(F32)).astype(BF16)
    k_o[...] = nn(x, wk).astype(BF16)
    v_o[...] = (nn(x, wv) + vecs_o[VB : VB + 1, at_cols].astype(F32)).astype(BF16)
    for first, rows, long_at in segments(dims):
        bias = key_bias(slen, llen, dims[3], rows, long_at)
        at = slice(first, first + rows)
        for pair in range(cols // PAIR):
            lanes = slice(pair * PAIR, (pair + 1) * PAIR)
            q = q_o[at, lanes] * jnp.asarray(HEAD_DIM**-0.5, BF16)
            scores = nt(two_heads(k_o[at, lanes]), q)
            probs = []
            for h in range(2):
                s = scores[h * rows : (h + 1) * rows] + bias
                e = jnp.exp(s - jnp.max(s, axis=0, keepdims=True))
                probs.append((e * (1.0 / jnp.sum(e, axis=0, keepdims=True))).astype(BF16))
            probs = jnp.concatenate(probs, axis=0)
            if long_at is None:
                ps_o[pair] = probs
            else:
                pl_o[long_at, pair] = probs
            c_o[at, lanes] = tn(probs, two_heads(v_o[at, lanes])).astype(BF16)
    total[...] += nn(c_o[...], wo_all[at_cols, :])

    @pl.when(step == pl.num_programs(0) - 1)
    def _():
        h = x_all[...].astype(F32) + (total[...] + row_of(vecs_o, OB))
        unit, inverse = normalized(h)
        n_o[...] = unit
        r_o[...] = inverse
        keep_all.wait()


def attention_forward(slen, llen, pos, xs, xl, pieces, inner, dims):
    rows, width = xs.shape[0] + xl.shape[0], xs.shape[1]
    short_rows, long_count, long_length, _ = dims
    step = 256
    steps, pairs = width // step, width // PAIR
    per = step // PAIR
    each_all = pieces[0].shape[1]
    cols = pl.BlockSpec((rows, step), lambda g, *_: (0, g))
    return pl.pallas_call(
        functools.partial(attention_forward_body, dims),
        grid_spec=pltpu.PrefetchScalarGridSpec(
            num_scalar_prefetch=3,
            grid=(steps,),
            in_specs=[
                whole(*xs.shape), whole(*xl.shape), *[pl.BlockSpec(memory_space=pl.ANY)] * 8,
            ],
            out_specs=[
                cols, cols, cols, cols,
                pl.BlockSpec((per, 2 * short_rows, short_rows), lambda g, *_: (g, 0, 0)),
                pl.BlockSpec((long_count, per, 2 * long_length, long_length), lambda g, *_: (0, g, 0, 0)),
                whole(rows, width), whole(rows, 1), whole(8, width), whole(1, inner),
                pl.BlockSpec(memory_space=pl.ANY),
            ],
            scratch_shapes=[
                pltpu.VMEM((rows, width), BF16), pltpu.VMEM((rows, width), F32), pltpu.VMEM((width, width), BF16),
                pltpu.VMEM((SHARDS, each_all, width), BF16), pltpu.SemaphoreType.DMA((SHARDS,)),
                pltpu.SemaphoreType.DMA(()),
            ],
        ),
        out_shape=[
            *[jax.ShapeDtypeStruct((rows, width), BF16)] * 4,
            jax.ShapeDtypeStruct((pairs, 2 * short_rows, short_rows), BF16),
            jax.ShapeDtypeStruct((long_count, pairs, 2 * long_length, long_length), BF16),
            jax.ShapeDtypeStruct((rows, width), F32),
            jax.ShapeDtypeStruct((rows, 1), F32),
            jax.ShapeDtypeStruct((8, width), BF16),
            jax.ShapeDtypeStruct((1, inner), BF16),
            jax.ShapeDtypeStruct((SHARDS, each_all, width), BF16),
        ],
        compiler_params=params(58),
        cost_estimate=cost(8 * rows * width * width, 20e6),
        name="attention_forward",
    )(slen, llen, pos, xs, xl, *pieces)


HBM = pl.BlockSpec(memory_space=pl.ANY)
ON_CHIP = pl.BlockSpec(memory_space=pltpu.VMEM)
SCALARS = pl.BlockSpec(memory_space=pltpu.SMEM)


class Copies:
    def __init__(self, sems):
        self.sems, self.used, self.open = sems, 0, []

    def start(self, source, target):
        copy = pltpu.make_async_copy(source, target, self.sems.at[self.used])
        self.used += 1
        copy.start()
        return copy

    def send(self, source, target):
        self.open.append(self.start(source, target))

    def finish(self):
        for copy in self.open:
            copy.wait()


def feed_body(
    dims, slen, llen, pos, unit1, cot_s, cot_l, inv1, ub, vecs, p0, p1, p2, p3, p4, p5, p6, p7,
    keep, give, outs_o, outl_o, gfs_o, gatt_o, sums_o, dub_o,
    wup, wdown, unit_v, cot_v, low_v, low_t, hidden, gelu_v, grad_v, gffn, out_v, gatt, valid_v,
    keep_dv, give_dv, keep_uv, give_uv, sems, piece_sems, down_sems, up_sems,
):
    short_rows = dims[0]
    rows, width = low_v.shape
    parts, block = hidden.shape[0], hidden.shape[2]
    each, tall = width // SHARDS, block * parts // SHARDS
    owners, lanes, tile = SHARDS // parts, 256, 128
    copies = Copies(sems)
    pieces = (p0, p1, p2, p3, p4, p5, p6, p7)
    unit_here = copies.start(unit1, unit_v)
    groups = [[], [], []]
    for other in range(2):
        for k in range(RING):
            for i in range(RING):
                n = (other * RING + k) * RING + i
                at = gathered_at(pos, other, k, i)
                source = pieces[other * RING + k]
                half = parts // 2
                targets = (wup.at[:half, at], wup.at[half:, at], wdown.at[at])
                sources = (source.at[i, :half], source.at[i, half:parts], source.at[i, parts:])
                for group, sem, src, target in zip(groups, range(3), sources, targets):
                    group.append(pltpu.make_async_copy(src, target, piece_sems.at[sem, n]))
    for copy in groups[0]:
        copy.start()
    valid_v[...] = valid_rows(slen, llen, dims)
    grad_v[...] = jnp.zeros_like(grad_v)
    unit_here.wait()

    @pl.loop(0, rows // tile)
    def _(r):
        at = pl.ds(pl.multiple_of(r * tile, tile), tile)
        low_v[at] = (unit_v[at] * row_of(vecs, G1) + row_of(vecs, S1)).astype(BF16)

    @pl.loop(0, parts)
    def _(j):
        for n in range(2):

            @pl.when(j == n * (parts // 2))
            def _():
                for copy in groups[n]:
                    copy.wait()
                for copy in groups[n + 1]:
                    copy.start()

        bias = ub[:, pl.ds(pl.multiple_of(j * block, block), block)].astype(F32)
        pre = nn(low_v[...], wup[j].reshape(width, block)) + bias
        cdf = 0.5 + 0.5 * lax.erf(pre * (0.5**0.5))
        density = jnp.exp(-0.5 * pre * pre) * (0.5 / jnp.pi) ** 0.5
        hidden[j] = (pre * cdf).astype(BF16)
        gelu_v[j] = (cdf + pre * density).astype(BF16)

    for copy in groups[2]:
        copy.wait()
    cots_here = copies.start(cot_s, cot_v.at[:short_rows]), copies.start(cot_l, cot_v.at[short_rows:])

    @pl.loop(0, parts)
    def _(j):
        grad_v[...] += nn(hidden[j], wdown[pl.ds(j * owners, owners)].reshape(block, width))

    for copy in cots_here:
        copy.wait()
    sums_o[...] = jnp.zeros_like(sums_o)

    @pl.loop(0, rows // tile)
    def _(r):
        at = pl.ds(pl.multiple_of(r * tile, tile), tile)
        first = unit_v[at] * row_of(vecs, G1) + row_of(vecs, S1)
        unit, inverse = normalized(first + (grad_v[at] + row_of(vecs, DB)))
        valid = valid_v[at]
        out_v[at] = ((unit * row_of(vecs, G2) + row_of(vecs, S2)) * valid).astype(BF16)
        cot = cot_v[at].astype(F32) * valid
        back = norm_back(cot * row_of(vecs, G2), unit, inverse)
        grad_v[at] = back
        low_back = back.astype(BF16)
        gffn[at] = low_back
        sums_o[DB : DB + 1] += jnp.sum(low_back.astype(F32), axis=0, keepdims=True)
        sums_o[G2 : G2 + 1] += jnp.sum(cot * unit, axis=0, keepdims=True)
        sums_o[S2 : S2 + 1] += jnp.sum(cot, axis=0, keepdims=True)

    copies.send(out_v.at[:short_rows], outs_o)
    copies.send(out_v.at[short_rows:], outl_o)
    on_first = pos[2] == 0

    def down_copies(at, p0, p1):
        return (
            pltpu.make_async_copy(keep_dv.at[at], keep.at[jnp.where(on_first, p0, p1), :parts], down_sems.at[0, at]),
            pltpu.make_async_copy(give_dv.at[at], give.at[jnp.where(on_first, p1, p0), :parts], down_sems.at[1, at]),
        )

    @pl.loop(0, RING)
    def _(x):
        grad = tn(hidden[x], gffn[...]).astype(BF16)
        for z in range(RING):
            place = x * RING + z
            even, odd = grad[2 * z * tall : (2 * z + 1) * tall], grad[(2 * z + 1) * tall : (2 * z + 2) * tall]
            keep_dv[place] = jnp.where(on_first, even, odd).reshape(parts, each, width)
            give_dv[place] = jnp.where(on_first, odd, even).reshape(parts, each, width)
            for copy in down_copies(place, *places(pos, x, z)):
                copy.start()

    def up_copies(j):
        return (
            pltpu.make_async_copy(keep_uv.at[j], keep.at[:, parts + j], up_sems.at[0, j]),
            pltpu.make_async_copy(give_uv.at[j], give.at[:, parts + j], up_sems.at[1, j]),
        )

    low_t[:width] = low_v[...].T
    low_t[width:] = jnp.ones((16, rows), BF16)

    @pl.loop(0, parts)
    def _(j):
        weight = wdown[pl.ds(j * owners, owners)].reshape(block, width)
        up = (nt(gffn[...], weight) * gelu_v[j].astype(F32)).astype(BF16)
        hidden[j] = up
        grad = nn(low_t[...], hidden[j])
        dub_o[:, pl.ds(pl.multiple_of(j * block, block), block)] = grad[width : width + 1]
        deal(keep_uv.at[j], give_uv.at[j], pos, grad[:width].astype(BF16), slice(None), each)
        for copy in up_copies(j):
            copy.start()

    @pl.loop(0, parts)
    def _(j):
        grad_v[...] += nt(hidden[j], wup[j].reshape(width, block))

    @pl.loop(0, rows // tile)
    def _(r):
        at = pl.ds(pl.multiple_of(r * tile, tile), tile)
        grad, unit = grad_v[at], unit_v[at]
        back = norm_back(grad * row_of(vecs, G1), unit, inv1[at])
        grad_v[at] = back
        low_back = back.astype(BF16)
        gatt[at] = low_back
        sums_o[OB : OB + 1] += jnp.sum(low_back.astype(F32), axis=0, keepdims=True)
        sums_o[G1 : G1 + 1] += jnp.sum(grad * unit, axis=0, keepdims=True)
        sums_o[S1 : S1 + 1] += jnp.sum(grad, axis=0, keepdims=True)

    copies.send(gatt, gatt_o)
    copies.send(grad_v, gfs_o)
    for at in range(CHIPS):
        for copy in down_copies(at, at, at):
            copy.wait()
    for j in range(parts):
        for copy in up_copies(j):
            copy.wait()
    copies.finish()


def feed(slen, llen, pos, unit1, cot_s, cot_l, inv1, ub, vecs, pieces, dims):
    rows, width = unit1.shape
    inner = ub.shape[1]
    parts = RING
    block, tall, each = inner // parts, inner // SHARDS, width // SHARDS
    down, up = (CHIPS, parts, each, width), (parts, CHIPS, each, width)
    return pl.pallas_call(
        functools.partial(feed_body, dims),
        in_specs=[SCALARS] * 3 + [HBM] * 3 + [ON_CHIP] * 3 + [HBM] * 8,
        out_specs=[HBM] * 6 + [ON_CHIP] * 2,
        scratch_shapes=[
            pltpu.VMEM((parts, SHARDS, each, width), BF16), pltpu.VMEM((SHARDS, parts, each, width), BF16),
            pltpu.VMEM((rows, width), F32), pltpu.VMEM((rows, width), BF16), pltpu.VMEM((rows, width), BF16),
            pltpu.VMEM((width + 16, rows), BF16), pltpu.VMEM((parts, rows, block), BF16),
            pltpu.VMEM((parts, rows, block), BF16), pltpu.VMEM((rows, width), F32), pltpu.VMEM((rows, width), BF16),
            pltpu.VMEM((rows, width), BF16), pltpu.VMEM((rows, width), BF16), pltpu.VMEM((rows, 1), F32),
            pltpu.VMEM(down, BF16), pltpu.VMEM(down, BF16), pltpu.VMEM(up, BF16), pltpu.VMEM(up, BF16),
            pltpu.SemaphoreType.DMA((8,)), pltpu.SemaphoreType.DMA((3, SHARDS)),
            pltpu.SemaphoreType.DMA((2, CHIPS)), pltpu.SemaphoreType.DMA((2, parts)),
        ],
        out_shape=[
            *[jax.ShapeDtypeStruct((CHIPS, 2 * parts, each, width), BF16)] * 2,
            jax.ShapeDtypeStruct(cot_s.shape, BF16),
            jax.ShapeDtypeStruct(cot_l.shape, BF16),
            jax.ShapeDtypeStruct((rows, width), F32),
            jax.ShapeDtypeStruct((rows, width), BF16),
            jax.ShapeDtypeStruct((8, width), F32),
            jax.ShapeDtypeStruct((1, inner), F32),
        ],
        compiler_params=params(58),
        cost_estimate=cost(12 * rows * width * inner, 30e6),
        name="feed",
    )(slen, llen, pos, unit1, cot_s, cot_l, inv1, ub, vecs, *pieces)


def attention_back_body(dims, gatt, wo_block, q, k, v, ps, plong, dq_o, dk_o, dv_o, gc, wo_all):
    step = pl.program_id(0)
    width, cols = gatt.shape[1], q.shape[1]
    at_cols = pl.ds(pl.multiple_of(step * cols, cols), cols)

    @pl.when(step == 0)
    def _():
        wo_all[...] = wo_block[...].reshape(width, width)

    gc[...] = nt(gatt[...], wo_all[at_cols, :]).astype(BF16)
    scale = HEAD_DIM**-0.5
    for first, rows, long_at in segments(dims):
        at = slice(first, first + rows)
        for pair in range(cols // PAIR):
            lanes = slice(pair * PAIR, (pair + 1) * PAIR)
            probs = ps[pair] if long_at is None else plong[long_at, pair]
            grad = gc[at, lanes]
            dp = nt(two_heads(v[at, lanes]), grad)
            ds = []
            for h in range(2):
                half = slice(h * rows, (h + 1) * rows)
                p = probs[half].astype(F32)
                d = dp[half]
                ds.append((p * (d - jnp.sum(d * p, axis=0, keepdims=True))).astype(BF16))
            ds = jnp.concatenate(ds, axis=0)
            dv_o[at, lanes] = own_lanes(nn(probs, grad)).astype(BF16)
            dk_o[at, lanes] = (own_lanes(nn(ds, q[at, lanes])) * scale).astype(BF16)
            dq_o[at, lanes] = (tn(ds, two_heads(k[at, lanes])) * scale).astype(BF16)


def attention_back(gatt, gathered, q, k, v, ps, plong, dims):
    rows, width = gatt.shape
    short_rows, long_count, long_length, _ = dims
    step = 256
    per = step // PAIR
    cols = pl.BlockSpec((rows, step), lambda g: (0, g))
    return pl.pallas_call(
        functools.partial(attention_back_body, dims),
        grid=(width // step,),
        in_specs=[
            whole(rows, width),
            pl.BlockSpec((SHARDS, width // SHARDS, width), lambda g: (0, 3, 0)),
            cols, cols, cols,
            pl.BlockSpec((per, 2 * short_rows, short_rows), lambda g: (g, 0, 0)),
            pl.BlockSpec((long_count, per, 2 * long_length, long_length), lambda g: (0, g, 0, 0)),
        ],
        out_specs=[cols, cols, cols],
        scratch_shapes=[pltpu.VMEM((rows, step), BF16), pltpu.VMEM((width, width), BF16)],
        out_shape=[jax.ShapeDtypeStruct((rows, width), BF16)] * 3,
        compiler_params=params(BACK_MIB),
        cost_estimate=cost(8 * rows * width * width, 15e6),
        name="attention_back",
    )(gatt, gathered, q, k, v, ps, plong)


def weight_back_body(
    dims, pos, gatt_cols, c, dq, dk, dv, xs, xl, sums_f, dub,
    keep, give,
    x_t, c_t, sums,
):
    step = pl.program_id(0)
    short_rows = dims[0]
    rows, width = c.shape
    cols = dq.shape[1]
    each = width // SHARDS
    at_cols = pl.ds(pl.multiple_of(step * cols, cols), cols)

    @pl.when(step == 0)
    def _():
        x_t[:width, :short_rows] = xs[...].T
        x_t[:width, short_rows:] = xl[...].T
        x_t[width:] = jnp.ones((16, rows), BF16)
        c_t[...] = c[...].T
        sums[...] = sums_f[...]

    deal(keep, give, pos, nn(c_t[...], gatt_cols[...]).astype(BF16), slice(3 * each, 4 * each), each)
    for i, d in enumerate((dq, dk, dv)):
        grad = nn(x_t[...], d[...])
        deal(keep, give, pos, grad[:width].astype(BF16), slice(i * each, (i + 1) * each), each)
        if i != 1:
            at = QB if i == 0 else VB
            sums[at : at + 1, at_cols] = grad[width : width + 1]
    keep[:, 4 * each :] = jnp.zeros((CHIPS, 8, cols), BF16)
    give[:, 4 * each :] = jnp.zeros((CHIPS, 8, cols), BF16)

    @pl.when(step == pl.num_programs(0) - 1)
    def _():
        mine = spread(SHARDS, width)
        rest = column_rest(cols, width, each)
        line = jnp.zeros((SHARDS, cols), F32)
        for i in range(8):
            put = (iota(rest.shape, 0) == rest + i * each).astype(BF16)
            line += nt(jnp.where(mine, sums[i : i + 1], 0.0).astype(BF16), put)
        inner = dub.shape[1]
        put = (iota((cols, inner), 0) == column_rest(cols, inner, inner // SHARDS)).astype(BF16)
        wide = nt(jnp.where(spread(SHARDS, inner), dub[...], 0.0).astype(BF16), put)
        both = jnp.concatenate([line[:, None], wide[:, None], jnp.zeros((SHARDS, 6, cols), F32)], axis=1)
        deal(keep, give, pos, both.reshape(SHARDS * 8, cols).astype(BF16), slice(4 * each, 4 * each + 8), 8)


def weight_back(pos, gatt, c, dq, dk, dv, xs, xl, sums_f, dub, dims):
    rows, width = gatt.shape
    each = width // SHARDS
    step = 256
    cols = pl.BlockSpec((rows, step), lambda g, *_: (0, g))
    dealt = pl.BlockSpec((CHIPS, 4 * each + 8, step), lambda g, *_: (0, 0, g))
    return pl.pallas_call(
        functools.partial(weight_back_body, dims),
        grid_spec=pltpu.PrefetchScalarGridSpec(
            num_scalar_prefetch=1,
            grid=(width // step,),
            in_specs=[
                cols, whole(rows, width), cols, cols, cols,
                whole(*xs.shape), whole(*xl.shape), whole(8, width), whole(*dub.shape),
            ],
            out_specs=[dealt, dealt],
            scratch_shapes=[
                pltpu.VMEM((width + 16, rows), BF16), pltpu.VMEM((width, rows), BF16), pltpu.VMEM((8, width), F32),
            ],
        ),
        out_shape=[jax.ShapeDtypeStruct((CHIPS, 4 * each + 8, width), BF16)] * 2,
        compiler_params=params(BACK_MIB),
        cost_estimate=cost(8 * rows * width * width, 12e6),
        name="weight_back",
    )(pos, gatt, c, dq, dk, dv, xs, xl, sums_f, dub)


def input_back_body(dims, gfs, dq, dk, dv, wq, wk, wv, gs_o, gl_o, total):
    step = pl.program_id(0)
    short_rows, width, cols = dims[0], gfs.shape[1], dq.shape[1]
    part = (
        nt(dq[...], wq[...].reshape(width, cols))
        + nt(dk[...], wk[...].reshape(width, cols))
        + nt(dv[...], wv[...].reshape(width, cols))
    )

    @pl.when(step == 0)
    def _():
        total[...] = gfs[...] + part

    @pl.when(step > 0)
    def _():
        total[...] += part

    @pl.when(step == pl.num_programs(0) - 1)
    def _():
        gs_o[...] = total[:short_rows]
        gl_o[...] = total[short_rows:]


def input_back(gfs, dq, dk, dv, gathered, dims):
    rows, width = gfs.shape
    each = width // SHARDS
    step = 256
    short_rows = dims[0]
    cols = pl.BlockSpec((rows, step), lambda g: (0, g))
    slab = lambda i: pl.BlockSpec((SHARDS, each, step), lambda g: (0, i, g))
    return pl.pallas_call(
        functools.partial(input_back_body, dims),
        grid=(width // step,),
        in_specs=[whole(rows, width), cols, cols, cols, slab(0), slab(1), slab(2)],
        out_specs=[whole(short_rows, width), whole(rows - short_rows, width)],
        scratch_shapes=[pltpu.VMEM((rows, width), F32)],
        out_shape=[
            jax.ShapeDtypeStruct((short_rows, width), F32),
            jax.ShapeDtypeStruct((rows - short_rows, width), F32),
        ],
        compiler_params=params(16),
        cost_estimate=cost(6 * rows * width * width, 12e6),
        name="input_back",
    )(gfs, dq, dk, dv, gathered, gathered, gathered)


def pair_sum(keep, got):
    parts = []
    for d in range(RING):
        at = slice(d * RING, (d + 1) * RING)
        parts.append((keep[at].astype(F32) + got[at].astype(F32)).astype(BF16))
    return parts


def four_sum(own, left, right, far):
    return (own.astype(F32) + far.astype(F32)) + (left.astype(F32) + right.astype(F32))


def turn(delta, stage):
    moves = []
    for x in range(RING):
        for z in range(RING):
            for core in range(2):
                to_x, to_z = x, z
                if (core == 0) == (stage == 0):
                    to_x = (x + delta) % RING
                else:
                    to_z = (z + delta) % RING
                moves.append(((x * RING + z) * 2 + core, (to_x * RING + to_z) * 2 + core))
    return moves


def swap_cores(v):
    return lax.ppermute(v, "shard", [(i, i ^ 1) for i in range(SHARDS)])


def around(v, stage):
    return tuple(lax.ppermute(v[d] if isinstance(v, (list, tuple)) else v, "shard", turn(d, stage)) for d in (1, 3, 2))


def both_cores(pieces):
    return (*pieces, *(swap_cores(p) for p in pieces))


def second_turn(own, left, right, far):
    parts = [four_sum(own[d], left[d], right[d], far[d]).astype(BF16) for d in range(RING)]
    own = four_sum(parts[0], *around(parts, 1)).astype(BF16)
    return own, *(lax.ppermute(own, "rep", [(i, (i + d) % RING) for i in range(RING)]) for d in (1, 3, 2))


def replica_sum(own, left, right, far, at):
    return (own[at].astype(F32) + far[at].astype(F32)) + (left[at].astype(F32) + right[at].astype(F32))


def finish_attention_body(own, left, right, far, wqkv_o, wo_o, *vector_os):
    each, width = wo_o.shape
    for j in range(wqkv_o.shape[1] // width):
        at = slice(j * each, (j + 1) * each)
        wqkv_o[:, j * width : (j + 1) * width] = replica_sum(own, left, right, far, at)
    wo_o[...] = replica_sum(own, left, right, far, slice(3 * each, 4 * each))
    last = replica_sum(own, left, right, far, slice(4 * each, 4 * each + 8))[:, width - 256 :]
    for i, o in enumerate(vector_os[:-1]):
        o[...] = last[0:1, i * each : (i + 1) * each]
    o = vector_os[-1]
    o[...] = last[1:2, : o.shape[1]]


def finish_attention(arrays, tall):
    width = arrays[0].shape[1]
    each = width // SHARDS
    return pl.pallas_call(
        finish_attention_body,
        out_shape=[
            jax.ShapeDtypeStruct((each, 3 * width), F32),
            jax.ShapeDtypeStruct((each, width), F32),
            *[jax.ShapeDtypeStruct((1, each), F32)] * 8,
            jax.ShapeDtypeStruct((1, tall), F32),
        ],
        compiler_params=params(4),
        name="finish_attention",
    )(*arrays)


def finish_feed_body(own, left, right, far, up_o, down_o):
    parts = own.shape[0] // 2
    each, width = own.shape[1:]
    for j in range(parts):
        down_o[j * each : (j + 1) * each] = replica_sum(own, left, right, far, j)
        up_o[:, j * width : (j + 1) * width] = replica_sum(own, left, right, far, parts + j)


def finish_feed(arrays, each, inner, tall):
    width = arrays[0].shape[2]
    return pl.pallas_call(
        finish_feed_body,
        out_shape=[jax.ShapeDtypeStruct((each, inner), F32), jax.ShapeDtypeStruct((tall, width), F32)],
        compiler_params=params(4),
        name="finish_feed",
    )(*arrays)


def on_device(
    short_tokens, long_tokens, short_lengths, long_lengths, short_cotangent, long_cotangent,
    input_weight, query_bias, value_bias, output_weight, output_bias, first_gain, first_shift,
    up_weight, up_bias, down_weight, down_bias, second_gain, second_shift,
):
    short_count, short_length, width = short_tokens.shape
    long_count, long_length, _ = long_tokens.shape
    dims = (short_count * short_length, long_count, long_length, short_length)
    each, inner, tall = width // SHARDS, up_weight.shape[1], down_weight.shape[0]
    xs, xl = short_tokens.reshape(-1, width), long_tokens.reshape(-1, width)
    cs, cl = short_cotangent.reshape(-1, width), long_cotangent.reshape(-1, width)
    index = lax.axis_index("shard")
    pos = jnp.stack([index // 8, (index // 2) % 4, index % 2]).astype(jnp.int32)

    packed = pack(
        input_weight, output_weight, up_weight, down_weight,
        (query_bias, value_bias, output_bias, first_gain, first_shift, down_bias, second_gain, second_shift),
        up_bias,
    )
    near = (packed, *around(packed, 1))
    cut = 4 * each + 8
    near_a = jnp.stack([n[:cut] for n in near])
    near_f = jnp.stack([n[cut:].reshape(-1, each, width) for n in near])
    around_a = around(near_a, 0)
    far_f = around(near_f, 0)
    pieces_a = both_cores((near_a, *around_a))
    xs, near_f = lax.optimization_barrier((xs, near_f))
    q, k, v, c, ps, plong, unit1, inv1, vecs, ub, gathered_a = attention_forward(
        short_lengths, long_lengths, pos, xs, xl, pieces_a, inner, dims
    )
    unit1, *far_f = lax.optimization_barrier((unit1, *far_f))
    keep_f, give_f, out_s, out_l, gfs, gatt, sums_f, dub = feed(
        short_lengths, long_lengths, pos, unit1, cs, cl, inv1, ub, vecs, both_cores((near_f, *far_f)), dims
    )
    dq, dk, dv = attention_back(gatt, gathered_a, q, k, v, ps, plong, dims)
    parts_f = pair_sum(keep_f, swap_cores(give_f))
    dv, *parts_f = lax.optimization_barrier((dv, *parts_f))
    around_f = around(parts_f, 0)
    keep_a, give_a = weight_back(pos, gatt, c, dq, dk, dv, xs, xl, sums_f, dub, dims)
    parts_a = pair_sum(keep_a, swap_cores(give_a))
    gfs, *parts_a = lax.optimization_barrier((gfs, *parts_a))
    around_a = around(parts_a, 0)
    grad_s, grad_l = input_back(gfs, dq, dk, dv, gathered_a, dims)
    grad_s, *around_a = lax.optimization_barrier((grad_s, *around_a))
    up, down = finish_feed(second_turn(parts_f[0], *around_f), each, inner, tall)
    w_in, w_out, *vectors = finish_attention(second_turn(parts_a[0], *around_a), tall)
    vectors = [x.reshape(-1) for x in vectors]
    return (
        out_s.reshape(short_tokens.shape), out_l.reshape(long_tokens.shape),
        grad_s.reshape(short_tokens.shape), grad_l.reshape(long_tokens.shape),
        w_in, vectors[QB], vectors[VB], w_out, vectors[OB], vectors[G1], vectors[S1],
        up, vectors[8], down, vectors[DB], vectors[G2], vectors[S2],
    )


def solution(mesh):
    rows, flat = P(("rep", "shard"), None, None), P("shard")
    tall = P("shard", None)
    return jax.shard_map(
        on_device,
        mesh=mesh,
        in_specs=(
            rows, rows, P(("rep", "shard")), P(("rep", "shard")), rows, rows,
            tall, flat, flat, tall, flat, flat, flat, tall, flat, tall, flat, flat, flat,
        ),
        out_specs=(
            rows, rows, rows, rows,
            tall, flat, flat, tall, flat, flat, flat, tall, flat, tall, flat, flat, flat,
        ),
        check_vma=False,
    )
```

```python
import functools

import jax
import jax.numpy as jnp
from jax import lax
from jax.experimental import pallas as pl
from jax.experimental.pallas import tpu as pltpu
from jax.sharding import PartitionSpec as P

F32 = jnp.float32
BF16 = jnp.bfloat16
HEAD_DIM = 64
PAIR = 128
EPSILON = 1e-06
BACK_MIB = 58
QB, VB, OB, G1, S1, DB, G2, S2 = range(8)
RING = 4
CHIPS = RING * RING
SHARDS = 2 * CHIPS


def nn(a, b):
    return lax.dot_general(a, b, (((1,), (0,)), ((), ())), preferred_element_type=F32)


def nt(a, b):
    return lax.dot_general(a, b, (((1,), (1,)), ((), ())), preferred_element_type=F32)


def tn(a, b):
    return lax.dot_general(a, b, (((0,), (0,)), ((), ())), preferred_element_type=F32)


def iota(shape, dim):
    return lax.broadcasted_iota(jnp.int32, shape, dim)


def row_of(ref, i):
    return ref[i : i + 1, :].astype(F32)


def whole(*shape):
    return pl.BlockSpec(shape, lambda g, *_: (0,) * len(shape))


def params(mebibytes):
    return pltpu.CompilerParams(vmem_limit_bytes=mebibytes * 1024 * 1024)


def cost(flops, moved):
    return pl.CostEstimate(flops=int(flops), bytes_accessed=int(moved), transcendentals=0)


def places(pos, x, z):
    along_x, along_z = (x - pos[0]) & (RING - 1), (z - pos[1]) & (RING - 1)
    return along_x * RING + along_z, along_z * RING + along_x


def deal(keep, give, pos, value, at, each):
    first = pos[2] == 0
    for x in range(RING):
        for z in range(RING):
            p0, p1 = places(pos, x, z)
            low = 2 * (x * RING + z) * each
            even, odd = value[low : low + each], value[low + each : low + 2 * each]
            keep[jnp.where(first, p0, p1), at] = jnp.where(first, even, odd)
            give[jnp.where(first, p1, p0), at] = jnp.where(first, odd, even)


def spread(owners, width):
    each = width // owners
    at = iota((owners, width), 1)
    low = iota((owners, width), 0) * each
    return (at >= low) & (at < low + each)


def column_rest(rows, width, each):
    at = iota((1, width), 1)
    return jnp.broadcast_to(at - (at // each) * each, (rows, width))


def two_heads(pair):
    low_half = iota(pair.shape, 1) < HEAD_DIM
    zero = jnp.zeros_like(pair)
    return jnp.concatenate([jnp.where(low_half, pair, zero), jnp.where(low_half, zero, pair)], axis=0)


def own_lanes(stack):
    half = stack.shape[0] // 2
    return jnp.where(iota((half, stack.shape[1]), 1) < HEAD_DIM, stack[:half], stack[half:])


def normalized(hidden):
    center = hidden - jnp.mean(hidden, axis=-1, keepdims=True)
    spread_of = jnp.mean(center * center, axis=-1, keepdims=True)
    inverse = lax.rsqrt(spread_of + EPSILON)
    return center * inverse, inverse


def norm_back(scaled, unit, inverse):
    return inverse * (
        scaled
        - jnp.mean(scaled, axis=-1, keepdims=True)
        - unit * jnp.mean(scaled * unit, axis=-1, keepdims=True)
    )


def segments(dims):
    short_rows, long_count, long_length, _ = dims
    return [(0, short_rows, None)] + [
        (short_rows + i * long_length, long_length, i) for i in range(long_count)
    ]


def key_bias(slen, llen, short_length, rows, long_at):
    key = iota((rows, rows), 0)
    if long_at is not None:
        return jnp.where(key < llen[long_at], 0.0, -1e9).astype(F32)
    query = iota((rows, rows), 1)
    keep = jnp.zeros((rows, rows), jnp.bool_)
    for p in range(rows // short_length):
        low, high = p * short_length, (p + 1) * short_length
        keep = keep | ((key >= low) & (key < low + slen[p]) & (query >= low) & (query < high))
    return jnp.where(keep, 0.0, -1e9).astype(F32)


def valid_rows(slen, llen, dims):
    short_rows, long_count, long_length, short_length = dims
    parts = []
    at = iota((short_length, 1), 0)
    for p in range(short_rows // short_length):
        parts.append((at < slen[p]).astype(F32))
    at = iota((long_length, 1), 0)
    for p in range(long_count):
        parts.append((at < llen[p]).astype(F32))
    return jnp.concatenate(parts, axis=0)


def slabs_of(out, base, source, each, width):
    for j in range(source.shape[1] // width):
        out[base + j * each : base + (j + 1) * each] = source[:, j * width : (j + 1) * width]
    return base + source.shape[1] // width * each


def pack_body(wqkv, wo, wup, wdown, *rest):
    vectors, out = rest[:-1], rest[-1]
    each, width = wo.shape
    base = slabs_of(out, 0, wqkv, each, width)
    base = slabs_of(out, base, wo, each, width)
    out[base : base + 8] = jnp.zeros((8, width), BF16)
    for i, v in enumerate(vectors[:-1]):
        out[base : base + 1, i * each : (i + 1) * each] = v[...]
    out[base + 1 : base + 2, : vectors[-1].shape[1]] = vectors[-1][...]
    base = slabs_of(out, base + 8, wup, each, width)
    out[base:] = wdown[...]


def pack(wqkv, wo, wup, wdown, vectors, ub):
    each, width = wo.shape
    rows = wqkv.shape[1] // width * each + each + 8 + 2 * wdown.shape[0]
    return pl.pallas_call(
        pack_body,
        out_shape=jax.ShapeDtypeStruct((rows, width), BF16),
        compiler_params=params(58),
        name="pack",
    )(wqkv, wo, wup, wdown, *[v[None] for v in vectors], ub[None])


STEPS = (0, -1, 1, 2)


def gathered_at(pos, other, k, i):
    core = pos[2] ^ other
    x0, z0 = (pos[0] + STEPS[k]) & (RING - 1), (pos[1] + STEPS[i]) & (RING - 1)
    x1, z1 = (pos[0] + STEPS[i]) & (RING - 1), (pos[1] + STEPS[k]) & (RING - 1)
    return jnp.where(core == 0, (x0 * RING + z0) * 2, (x1 * RING + z1) * 2 + 1)


def arrivals(pos, pieces, target, sems, at):
    copies = []
    for other in range(2):
        for k in range(RING):
            for i in range(RING):
                n = (other * RING + k) * RING + i
                copies.append(
                    pltpu.make_async_copy(
                        pieces[other * RING + k].at[i, at], target.at[gathered_at(pos, other, k, i), at], sems.at[n]
                    )
                )
    return copies


def attention_forward_body(
    dims, slen, llen, pos, xs, xl, p0, p1, p2, p3, p4, p5, p6, p7,
    q_o, k_o, v_o, c_o, ps_o, pl_o, n_o, r_o, vecs_o, ub_o, gathered_o,
    x_all, total, wo_all, gathered, sems, out_sem,
):
    step = pl.program_id(0)
    short_rows, width = dims[0], x_all.shape[1]
    cols = q_o.shape[1]
    each = width // SHARDS
    keep_all = pltpu.make_async_copy(gathered, gathered_o, out_sem)

    @pl.when(step == 0)
    def _():
        copies = arrivals(pos, (p0, p1, p2, p3, p4, p5, p6, p7), gathered, sems, slice(None))
        for copy in copies:
            copy.start()
        x_all[:short_rows, :] = xs[...]
        x_all[short_rows:, :] = xl[...]
        total[...] = jnp.zeros_like(total)
        for copy in copies:
            copy.wait()
        keep_all.start()
        wo_all[...] = gathered[:, 3 * each : 4 * each].reshape(width, width)
        packed = gathered[:, 4 * each :]
        line = packed[:, 0, : 8 * each + 64]
        rest = column_rest(line.shape[1], width, each)
        mine = spread(SHARDS, width)
        for i in range(8):
            pick = (iota(rest.shape, 0) == rest + i * each).astype(BF16)
            row = jnp.sum(jnp.where(mine, nn(line, pick), 0.0), axis=0, keepdims=True)
            vecs_o[i : i + 1] = row.astype(BF16)
        inner = ub_o.shape[1]
        line = packed[:, 1, :128]
        pick = (iota((128, inner), 0) == column_rest(128, inner, inner // SHARDS)).astype(BF16)
        row = jnp.sum(jnp.where(spread(SHARDS, inner), nn(line, pick), 0.0), axis=0, keepdims=True)
        ub_o[...] = row.astype(BF16)

    x = x_all[...]
    at_cols = pl.ds(pl.multiple_of(step * cols, cols), cols)
    wq, wk, wv = (gathered[:, i * each : (i + 1) * each, at_cols].reshape(width, cols) for i in range(3))
    q_o[...] = (nn(x, wq) + vecs_o[QB : QB + 1, at_cols].astype(F32)).astype(BF16)
    k_o[...] = nn(x, wk).astype(BF16)
    v_o[...] = (nn(x, wv) + vecs_o[VB : VB + 1, at_cols].astype(F32)).astype(BF16)
    for first, rows, long_at in segments(dims):
        bias = key_bias(slen, llen, dims[3], rows, long_at)
        at = slice(first, first + rows)
        for pair in range(cols // PAIR):
            lanes = slice(pair * PAIR, (pair + 1) * PAIR)
            q = q_o[at, lanes] * jnp.asarray(HEAD_DIM**-0.5, BF16)
            scores = nt(two_heads(k_o[at, lanes]), q)
            probs = []
            for h in range(2):
                s = scores[h * rows : (h + 1) * rows] + bias
                e = jnp.exp(s - jnp.max(s, axis=0, keepdims=True))
                probs.append((e * (1.0 / jnp.sum(e, axis=0, keepdims=True))).astype(BF16))
            probs = jnp.concatenate(probs, axis=0)
            if long_at is None:
                ps_o[pair] = probs
            else:
                pl_o[long_at, pair] = probs
            c_o[at, lanes] = tn(probs, two_heads(v_o[at, lanes])).astype(BF16)
    total[...] += nn(c_o[...], wo_all[at_cols, :])

    @pl.when(step == pl.num_programs(0) - 1)
    def _():
        h = x_all[...].astype(F32) + (total[...] + row_of(vecs_o, OB))
        unit, inverse = normalized(h)
        n_o[...] = unit
        r_o[...] = inverse
        keep_all.wait()


def attention_forward(slen, llen, pos, xs, xl, pieces, inner, dims):
    rows, width = xs.shape[0] + xl.shape[0], xs.shape[1]
    short_rows, long_count, long_length, _ = dims
    step = 256
    steps, pairs = width // step, width // PAIR
    per = step // PAIR
    each_all = pieces[0].shape[1]
    cols = pl.BlockSpec((rows, step), lambda g, *_: (0, g))
    return pl.pallas_call(
        functools.partial(attention_forward_body, dims),
        grid_spec=pltpu.PrefetchScalarGridSpec(
            num_scalar_prefetch=3,
            grid=(steps,),
            in_specs=[
                whole(*xs.shape), whole(*xl.shape), *[pl.BlockSpec(memory_space=pl.ANY)] * 8,
            ],
            out_specs=[
                cols, cols, cols, cols,
                pl.BlockSpec((per, 2 * short_rows, short_rows), lambda g, *_: (g, 0, 0)),
                pl.BlockSpec((long_count, per, 2 * long_length, long_length), lambda g, *_: (0, g, 0, 0)),
                whole(rows, width), whole(rows, 1), whole(8, width), whole(1, inner),
                pl.BlockSpec(memory_space=pl.ANY),
            ],
            scratch_shapes=[
                pltpu.VMEM((rows, width), BF16), pltpu.VMEM((rows, width), F32), pltpu.VMEM((width, width), BF16),
                pltpu.VMEM((SHARDS, each_all, width), BF16), pltpu.SemaphoreType.DMA((SHARDS,)),
                pltpu.SemaphoreType.DMA(()),
            ],
        ),
        out_shape=[
            *[jax.ShapeDtypeStruct((rows, width), BF16)] * 4,
            jax.ShapeDtypeStruct((pairs, 2 * short_rows, short_rows), BF16),
            jax.ShapeDtypeStruct((long_count, pairs, 2 * long_length, long_length), BF16),
            jax.ShapeDtypeStruct((rows, width), F32),
            jax.ShapeDtypeStruct((rows, 1), F32),
            jax.ShapeDtypeStruct((8, width), BF16),
            jax.ShapeDtypeStruct((1, inner), BF16),
            jax.ShapeDtypeStruct((SHARDS, each_all, width), BF16),
        ],
        compiler_params=params(58),
        cost_estimate=cost(8 * rows * width * width, 20e6),
        name="attention_forward",
    )(slen, llen, pos, xs, xl, *pieces)


HBM = pl.BlockSpec(memory_space=pl.ANY)
ON_CHIP = pl.BlockSpec(memory_space=pltpu.VMEM)
SCALARS = pl.BlockSpec(memory_space=pltpu.SMEM)


class Copies:
    def __init__(self, sems):
        self.sems, self.used, self.open = sems, 0, []

    def start(self, source, target):
        copy = pltpu.make_async_copy(source, target, self.sems.at[self.used])
        self.used += 1
        copy.start()
        return copy

    def send(self, source, target):
        self.open.append(self.start(source, target))

    def finish(self):
        for copy in self.open:
            copy.wait()


def feed_body(
    dims, slen, llen, pos, unit1, cot_s, cot_l, inv1, ub, vecs, p0, p1, p2, p3, p4, p5, p6, p7,
    keep, give, outs_o, outl_o, gfs_o, gatt_o, sums_o,
    wup, wdown, unit_v, cot_v, low_v, low_t, hidden, gelu_v, grad_v, gffn, out_v, gatt, valid_v,
    keep_dv, give_dv, keep_uv, give_uv, sems, piece_sems, down_sems, up_sems,
):
    short_rows = dims[0]
    rows, width = low_v.shape
    parts, block = hidden.shape[0], hidden.shape[2]
    each, tall = width // SHARDS, block * parts // SHARDS
    owners, lanes, tile = SHARDS // parts, 256, 128
    copies = Copies(sems)
    pieces = (p0, p1, p2, p3, p4, p5, p6, p7)
    unit_here = copies.start(unit1, unit_v)
    groups = [[], [], []]
    for other in range(2):
        for k in range(RING):
            for i in range(RING):
                n = (other * RING + k) * RING + i
                at = gathered_at(pos, other, k, i)
                source = pieces[other * RING + k]
                half = parts // 2
                targets = (wup.at[:half, at], wup.at[half:, at], wdown.at[at])
                sources = (source.at[i, :half], source.at[i, half:parts], source.at[i, parts:])
                for group, sem, src, target in zip(groups, range(3), sources, targets):
                    group.append(pltpu.make_async_copy(src, target, piece_sems.at[sem, n]))
    for copy in groups[0]:
        copy.start()
    valid_v[...] = valid_rows(slen, llen, dims)
    grad_v[...] = jnp.zeros_like(grad_v)
    unit_here.wait()

    @pl.loop(0, rows // tile)
    def _(r):
        at = pl.ds(pl.multiple_of(r * tile, tile), tile)
        low_v[at] = (unit_v[at] * row_of(vecs, G1) + row_of(vecs, S1)).astype(BF16)

    @pl.loop(0, parts)
    def _(j):
        for n in range(2):

            @pl.when(j == n * (parts // 2))
            def _():
                for copy in groups[n]:
                    copy.wait()
                for copy in groups[n + 1]:
                    copy.start()

        bias = ub[:, pl.ds(pl.multiple_of(j * block, block), block)].astype(F32)
        pre = nn(low_v[...], wup[j].reshape(width, block)) + bias
        cdf = 0.5 + 0.5 * lax.erf(pre * (0.5**0.5))
        density = jnp.exp(-0.5 * pre * pre) * (0.5 / jnp.pi) ** 0.5
        hidden[j] = (pre * cdf).astype(BF16)
        gelu_v[j] = (cdf + pre * density).astype(BF16)

    for copy in groups[2]:
        copy.wait()
    cots_here = copies.start(cot_s, cot_v.at[:short_rows]), copies.start(cot_l, cot_v.at[short_rows:])

    @pl.loop(0, parts)
    def _(j):
        grad_v[...] += nn(hidden[j], wdown[pl.ds(j * owners, owners)].reshape(block, width))

    for copy in cots_here:
        copy.wait()
    sums_o[...] = jnp.zeros_like(sums_o)

    @pl.loop(0, rows // tile)
    def _(r):
        at = pl.ds(pl.multiple_of(r * tile, tile), tile)
        first = unit_v[at] * row_of(vecs, G1) + row_of(vecs, S1)
        unit, inverse = normalized(first + (grad_v[at] + row_of(vecs, DB)))
        valid = valid_v[at]
        out_v[at] = ((unit * row_of(vecs, G2) + row_of(vecs, S2)) * valid).astype(BF16)
        cot = cot_v[at].astype(F32) * valid
        back = norm_back(cot * row_of(vecs, G2), unit, inverse)
        grad_v[at] = back
        low_back = back.astype(BF16)
        gffn[at] = low_back
        sums_o[DB : DB + 1] += jnp.sum(low_back.astype(F32), axis=0, keepdims=True)
        sums_o[G2 : G2 + 1] += jnp.sum(cot * unit, axis=0, keepdims=True)
        sums_o[S2 : S2 + 1] += jnp.sum(cot, axis=0, keepdims=True)

    copies.send(out_v.at[:short_rows], outs_o)
    copies.send(out_v.at[short_rows:], outl_o)
    on_first = pos[2] == 0

    def down_copies(at, p0, p1):
        return (
            pltpu.make_async_copy(keep_dv.at[at], keep.at[jnp.where(on_first, p0, p1), :parts], down_sems.at[0, at]),
            pltpu.make_async_copy(give_dv.at[at], give.at[jnp.where(on_first, p1, p0), :parts], down_sems.at[1, at]),
        )

    @pl.loop(0, RING)
    def _(x):
        grad = tn(hidden[x], gffn[...]).astype(BF16)
        for z in range(RING):
            place = x * RING + z
            even, odd = grad[2 * z * tall : (2 * z + 1) * tall], grad[(2 * z + 1) * tall : (2 * z + 2) * tall]
            keep_dv[place] = jnp.where(on_first, even, odd).reshape(parts, each, width)
            give_dv[place] = jnp.where(on_first, odd, even).reshape(parts, each, width)
            for copy in down_copies(place, *places(pos, x, z)):
                copy.start()

    def up_copies(j):
        return (
            pltpu.make_async_copy(keep_uv.at[j], keep.at[:, parts + j], up_sems.at[0, j]),
            pltpu.make_async_copy(give_uv.at[j], give.at[:, parts + j], up_sems.at[1, j]),
        )

    low_t[:width] = low_v[...].T
    low_t[width:] = jnp.ones((16, rows), BF16)

    @pl.loop(0, parts)
    def _(j):
        weight = wdown[pl.ds(j * owners, owners)].reshape(block, width)
        up = (nt(gffn[...], weight) * gelu_v[j].astype(F32)).astype(BF16)
        hidden[j] = up
        grad = nn(low_t[...], hidden[j])
        sums_o[pl.ds(8 + j, 1)] = grad[width : width + 1]
        deal(keep_uv.at[j], give_uv.at[j], pos, grad[:width].astype(BF16), slice(None), each)
        for copy in up_copies(j):
            copy.start()

    @pl.loop(0, parts)
    def _(j):
        grad_v[...] += nt(hidden[j], wup[j].reshape(width, block))

    @pl.loop(0, rows // tile)
    def _(r):
        at = pl.ds(pl.multiple_of(r * tile, tile), tile)
        grad, unit = grad_v[at], unit_v[at]
        back = norm_back(grad * row_of(vecs, G1), unit, inv1[at])
        grad_v[at] = back
        low_back = back.astype(BF16)
        gatt[at] = low_back
        sums_o[OB : OB + 1] += jnp.sum(low_back.astype(F32), axis=0, keepdims=True)
        sums_o[G1 : G1 + 1] += jnp.sum(grad * unit, axis=0, keepdims=True)
        sums_o[S1 : S1 + 1] += jnp.sum(grad, axis=0, keepdims=True)

    copies.send(gatt, gatt_o)
    copies.send(grad_v, gfs_o)
    for at in range(CHIPS):
        for copy in down_copies(at, at, at):
            copy.wait()
    for j in range(parts):
        for copy in up_copies(j):
            copy.wait()
    copies.finish()


def feed(slen, llen, pos, unit1, cot_s, cot_l, inv1, ub, vecs, pieces, dims):
    rows, width = unit1.shape
    inner = ub.shape[1]
    parts = RING
    block, tall, each = inner // parts, inner // SHARDS, width // SHARDS
    down, up = (CHIPS, parts, each, width), (parts, CHIPS, each, width)
    return pl.pallas_call(
        functools.partial(feed_body, dims),
        in_specs=[SCALARS] * 3 + [HBM] * 3 + [ON_CHIP] * 3 + [HBM] * 8,
        out_specs=[HBM] * 6 + [ON_CHIP],
        scratch_shapes=[
            pltpu.VMEM((parts, SHARDS, each, width), BF16), pltpu.VMEM((SHARDS, parts, each, width), BF16),
            pltpu.VMEM((rows, width), F32), pltpu.VMEM((rows, width), BF16), pltpu.VMEM((rows, width), BF16),
            pltpu.VMEM((width + 16, rows), BF16), pltpu.VMEM((parts, rows, block), BF16),
            pltpu.VMEM((parts, rows, block), BF16), pltpu.VMEM((rows, width), F32), pltpu.VMEM((rows, width), BF16),
            pltpu.VMEM((rows, width), BF16), pltpu.VMEM((rows, width), BF16), pltpu.VMEM((rows, 1), F32),
            pltpu.VMEM(down, BF16), pltpu.VMEM(down, BF16), pltpu.VMEM(up, BF16), pltpu.VMEM(up, BF16),
            pltpu.SemaphoreType.DMA((8,)), pltpu.SemaphoreType.DMA((3, SHARDS)),
            pltpu.SemaphoreType.DMA((2, CHIPS)), pltpu.SemaphoreType.DMA((2, parts)),
        ],
        out_shape=[
            *[jax.ShapeDtypeStruct((CHIPS, 2 * parts, each, width), BF16)] * 2,
            jax.ShapeDtypeStruct(cot_s.shape, BF16),
            jax.ShapeDtypeStruct(cot_l.shape, BF16),
            jax.ShapeDtypeStruct((rows, width), F32),
            jax.ShapeDtypeStruct((rows, width), BF16),
            jax.ShapeDtypeStruct((16, width), F32),
        ],
        compiler_params=params(58),
        cost_estimate=cost(12 * rows * width * inner, 30e6),
        name="feed",
    )(slen, llen, pos, unit1, cot_s, cot_l, inv1, ub, vecs, *pieces)


def attention_back_body(dims, gatt, wo_block, q, k, v, ps, plong, grads, gc, wo_all):
    step = pl.program_id(0)
    width, cols = gatt.shape[1], q.shape[1]
    at_cols = pl.ds(pl.multiple_of(step * cols, cols), cols)

    @pl.when(step == 0)
    def _():
        wo_all[...] = wo_block[...].reshape(width, width)

    gc[...] = nt(gatt[...], wo_all[at_cols, :]).astype(BF16)
    scale = HEAD_DIM**-0.5
    for first, rows, long_at in segments(dims):
        at = slice(first, first + rows)
        for pair in range(cols // PAIR):
            lanes = slice(pair * PAIR, (pair + 1) * PAIR)
            probs = ps[pair] if long_at is None else plong[long_at, pair]
            grad = gc[at, lanes]
            dp = nt(two_heads(v[at, lanes]), grad)
            ds = []
            for h in range(2):
                half = slice(h * rows, (h + 1) * rows)
                p = probs[half].astype(F32)
                d = dp[half]
                ds.append((p * (d - jnp.sum(d * p, axis=0, keepdims=True))).astype(BF16))
            ds = jnp.concatenate(ds, axis=0)
            grads[2, at, lanes] = own_lanes(nn(probs, grad)).astype(BF16)
            grads[1, at, lanes] = (own_lanes(nn(ds, q[at, lanes])) * scale).astype(BF16)
            grads[0, at, lanes] = (tn(ds, two_heads(k[at, lanes])) * scale).astype(BF16)


def attention_back(gatt, gathered, q, k, v, ps, plong, dims):
    rows, width = gatt.shape
    short_rows, long_count, long_length, _ = dims
    step = 256
    per = step // PAIR
    cols = pl.BlockSpec((rows, step), lambda g: (0, g))
    return pl.pallas_call(
        functools.partial(attention_back_body, dims),
        grid=(width // step,),
        in_specs=[
            whole(rows, width),
            pl.BlockSpec((SHARDS, width // SHARDS, width), lambda g: (0, 3, 0)),
            cols, cols, cols,
            pl.BlockSpec((per, 2 * short_rows, short_rows), lambda g: (g, 0, 0)),
            pl.BlockSpec((long_count, per, 2 * long_length, long_length), lambda g: (0, g, 0, 0)),
        ],
        out_specs=pl.BlockSpec((3, rows, step), lambda g: (0, 0, g)),
        scratch_shapes=[pltpu.VMEM((rows, step), BF16), pltpu.VMEM((width, width), BF16)],
        out_shape=jax.ShapeDtypeStruct((3, rows, width), BF16),
        compiler_params=params(BACK_MIB),
        cost_estimate=cost(8 * rows * width * width, 15e6),
        name="attention_back",
    )(gatt, gathered, q, k, v, ps, plong)


def weight_back_body(
    pos, gatt, gatt_other, c, c_other, d, d_other, xs, xl, xs_other, xl_other, sums_own, sums_other,
    o0, o1, o2, o3,
    x_t, c_t, grad, sums,
):
    step = pl.program_id(0)
    rows, width = c.shape
    cols = gatt.shape[1]
    each = width // SHARDS
    mine = CHIPS * each
    on_first = pos[2] == 0
    at_cols = pl.ds(pl.multiple_of(step * cols, cols), cols)

    def take(target, first, source):
        turned = source[...].T
        for i in range(CHIPS):
            low = 2 * i * each
            target[i * each : (i + 1) * each, first : first + turned.shape[1]] = jnp.where(
                on_first, turned[low : low + each], turned[low + each : low + 2 * each]
            )

    @pl.when(step == 0)
    def _():
        first = 0
        for source in (xs, xl, xs_other, xl_other):
            take(x_t, first, source)
            first += source.shape[0]
        x_t[mine:] = jnp.ones((16, 2 * rows), BF16)
        take(c_t, 0, c)
        take(c_t, rows, c_other)
        sums[...] = sums_own[...] + sums_other[...]

    def hand_out(value, at):
        n = value.shape[0] // CHIPS
        grad[:, :n] = value.reshape(CHIPS, n, cols)
        for along, out in enumerate((o0, o1, o2, o3)):
            for e in range(RING):
                x0, z0 = (pos[0] + along) & (RING - 1), (pos[1] + e) & (RING - 1)
                x1, z1 = (pos[0] + e) & (RING - 1), (pos[1] + along) & (RING - 1)
                out[e, at : at + n] = grad[jnp.where(on_first, x0 * RING + z0, x1 * RING + z1), :n]

    both = jnp.concatenate([gatt[...], gatt_other[...]], axis=0)
    hand_out(nn(c_t[...], both).astype(BF16), 3 * each)
    for i in range(3):
        both = jnp.concatenate([d[i], d_other[i]], axis=0)
        total = nn(x_t[...], both)
        hand_out(total[:mine].astype(BF16), i * each)
        if i != 1:
            at = QB if i == 0 else VB
            sums[at : at + 1, at_cols] = total[mine : mine + 1]
    for out in (o0, o1, o2, o3):
        out[:, 4 * each :] = jnp.zeros((RING, 8, cols), BF16)

    @pl.when(step == pl.num_programs(0) - 1)
    def _():
        owned = spread(SHARDS, width)
        rest = column_rest(cols, width, each)
        line = jnp.zeros((SHARDS, cols), F32)
        for i in range(8):
            put = (iota(rest.shape, 0) == rest + i * each).astype(BF16)
            line += nt(jnp.where(owned, sums[i : i + 1], 0.0).astype(BF16), put)
        parts = RING
        place = width * parts // SHARDS
        wide_owned = spread(SHARDS // parts, width)
        put = (iota((cols, width), 0) == column_rest(cols, width, place)).astype(BF16)
        wide = jnp.concatenate(
            [nt(jnp.where(wide_owned, sums[8 + j : 9 + j], 0.0).astype(BF16), put) for j in range(parts)], axis=0
        )
        small = jnp.concatenate([line[:, None], wide[:, None], jnp.zeros((SHARDS, 6, cols), F32)], axis=1)
        small = small.reshape(CHIPS, 2, 8, cols)
        small = jnp.where(on_first, small[:, 0], small[:, 1])
        hand_out(small.reshape(CHIPS * 8, cols).astype(BF16), 4 * each)


def weight_back(pos, gatt, c, d, xs, xl, sums, others):
    gatt_other, c_other, d_other, xs_other, xl_other, sums_other = others
    rows, width = gatt.shape
    each = width // SHARDS
    step = 256
    cols = pl.BlockSpec((rows, step), lambda g, *_: (0, g))
    three = pl.BlockSpec((3, rows, step), lambda g, *_: (0, 0, g))
    out = pl.BlockSpec((RING, 4 * each + 8, step), lambda g, *_: (0, 0, g))
    return pl.pallas_call(
        weight_back_body,
        grid_spec=pltpu.PrefetchScalarGridSpec(
            num_scalar_prefetch=1,
            grid=(width // step,),
            in_specs=[
                cols, cols, whole(rows, width), whole(rows, width), three, three,
                whole(*xs.shape), whole(*xl.shape), whole(*xs.shape), whole(*xl.shape),
                whole(16, width), whole(16, width),
            ],
            out_specs=[out] * RING,
            scratch_shapes=[
                pltpu.VMEM((width // 2 + 16, 2 * rows), BF16), pltpu.VMEM((width // 2, 2 * rows), BF16),
                pltpu.VMEM((CHIPS, each, step), BF16), pltpu.VMEM((16, width), F32),
            ],
        ),
        out_shape=[jax.ShapeDtypeStruct((RING, 4 * each + 8, width), BF16)] * RING,
        compiler_params=params(BACK_MIB),
        cost_estimate=cost(8 * rows * width * width, 12e6),
        name="weight_back",
    )(pos, gatt, gatt_other, c, c_other, d, d_other, xs, xl, xs_other, xl_other, sums, sums_other)


def input_back_body(dims, gfs, d, wq, wk, wv, gs_o, gl_o, total):
    step = pl.program_id(0)
    short_rows, width, cols = dims[0], gfs.shape[1], d.shape[2]
    part = (
        nt(d[0], wq[...].reshape(width, cols))
        + nt(d[1], wk[...].reshape(width, cols))
        + nt(d[2], wv[...].reshape(width, cols))
    )

    @pl.when(step == 0)
    def _():
        total[...] = gfs[...] + part

    @pl.when(step > 0)
    def _():
        total[...] += part

    @pl.when(step == pl.num_programs(0) - 1)
    def _():
        gs_o[...] = total[:short_rows]
        gl_o[...] = total[short_rows:]


def input_back(gfs, d, gathered, dims):
    rows, width = gfs.shape
    each = width // SHARDS
    step = 256
    short_rows = dims[0]
    slab = lambda i: pl.BlockSpec((SHARDS, each, step), lambda g: (0, i, g))
    return pl.pallas_call(
        functools.partial(input_back_body, dims),
        grid=(width // step,),
        in_specs=[whole(rows, width), pl.BlockSpec((3, rows, step), lambda g: (0, 0, g)), slab(0), slab(1), slab(2)],
        out_specs=[whole(short_rows, width), whole(rows - short_rows, width)],
        scratch_shapes=[pltpu.VMEM((rows, width), F32)],
        out_shape=[
            jax.ShapeDtypeStruct((short_rows, width), F32),
            jax.ShapeDtypeStruct((rows - short_rows, width), F32),
        ],
        compiler_params=params(16),
        cost_estimate=cost(6 * rows * width * width, 12e6),
        name="input_back",
    )(gfs, d, gathered, gathered, gathered)


def pair_sum(keep, got):
    parts = []
    for d in range(RING):
        at = slice(d * RING, (d + 1) * RING)
        parts.append((keep[at].astype(F32) + got[at].astype(F32)).astype(BF16))
    return parts


def four_sum(own, left, right, far):
    return (own.astype(F32) + far.astype(F32)) + (left.astype(F32) + right.astype(F32))


def turn(delta, stage):
    moves = []
    for x in range(RING):
        for z in range(RING):
            for core in range(2):
                to_x, to_z = x, z
                if (core == 0) == (stage == 0):
                    to_x = (x + delta) % RING
                else:
                    to_z = (z + delta) % RING
                moves.append(((x * RING + z) * 2 + core, (to_x * RING + to_z) * 2 + core))
    return moves


def swap_cores(v):
    return lax.ppermute(v, "shard", [(i, i ^ 1) for i in range(SHARDS)])


def around(v, stage):
    return tuple(lax.ppermute(v[d] if isinstance(v, (list, tuple)) else v, "shard", turn(d, stage)) for d in (1, 3, 2))


def both_cores(pieces):
    return (*pieces, *(swap_cores(p) for p in pieces))


def second_turn(own, left, right, far):
    parts = [four_sum(own[d], left[d], right[d], far[d]).astype(BF16) for d in range(RING)]
    own = four_sum(parts[0], *around(parts, 1)).astype(BF16)
    return own, *(lax.ppermute(own, "rep", [(i, (i + d) % RING) for i in range(RING)]) for d in (1, 3, 2))


def replica_sum(own, left, right, far, at):
    return (own[at].astype(F32) + far[at].astype(F32)) + (left[at].astype(F32) + right[at].astype(F32))


def finish_attention_body(own, left, right, far, wqkv_o, wo_o, *vector_os):
    each, width = wo_o.shape
    for j in range(wqkv_o.shape[1] // width):
        at = slice(j * each, (j + 1) * each)
        wqkv_o[:, j * width : (j + 1) * width] = replica_sum(own, left, right, far, at)
    wo_o[...] = replica_sum(own, left, right, far, slice(3 * each, 4 * each))
    last = replica_sum(own, left, right, far, slice(4 * each, 4 * each + 8))[:, width - 256 :]
    for i, o in enumerate(vector_os[:-1]):
        o[...] = last[0:1, i * each : (i + 1) * each]
    o = vector_os[-1]
    o[...] = last[1:2, : o.shape[1]]


def finish_attention(arrays, tall):
    width = arrays[0].shape[1]
    each = width // SHARDS
    return pl.pallas_call(
        finish_attention_body,
        out_shape=[
            jax.ShapeDtypeStruct((each, 3 * width), F32),
            jax.ShapeDtypeStruct((each, width), F32),
            *[jax.ShapeDtypeStruct((1, each), F32)] * 8,
            jax.ShapeDtypeStruct((1, tall), F32),
        ],
        compiler_params=params(4),
        name="finish_attention",
    )(*arrays)


def finish_feed_body(own, left, right, far, up_o, down_o):
    parts = own.shape[0] // 2
    each, width = own.shape[1:]
    for j in range(parts):
        down_o[j * each : (j + 1) * each] = replica_sum(own, left, right, far, j)
        up_o[:, j * width : (j + 1) * width] = replica_sum(own, left, right, far, parts + j)


def finish_feed(arrays, each, inner, tall):
    width = arrays[0].shape[2]
    return pl.pallas_call(
        finish_feed_body,
        out_shape=[jax.ShapeDtypeStruct((each, inner), F32), jax.ShapeDtypeStruct((tall, width), F32)],
        compiler_params=params(4),
        name="finish_feed",
    )(*arrays)


def on_device(
    short_tokens, long_tokens, short_lengths, long_lengths, short_cotangent, long_cotangent,
    input_weight, query_bias, value_bias, output_weight, output_bias, first_gain, first_shift,
    up_weight, up_bias, down_weight, down_bias, second_gain, second_shift,
):
    short_count, short_length, width = short_tokens.shape
    long_count, long_length, _ = long_tokens.shape
    dims = (short_count * short_length, long_count, long_length, short_length)
    each, inner, tall = width // SHARDS, up_weight.shape[1], down_weight.shape[0]
    xs, xl = short_tokens.reshape(-1, width), long_tokens.reshape(-1, width)
    cs, cl = short_cotangent.reshape(-1, width), long_cotangent.reshape(-1, width)
    index = lax.axis_index("shard")
    pos = jnp.stack([index // 8, (index // 2) % 4, index % 2]).astype(jnp.int32)

    packed = pack(
        input_weight, output_weight, up_weight, down_weight,
        (query_bias, value_bias, output_bias, first_gain, first_shift, down_bias, second_gain, second_shift),
        up_bias,
    )
    near = (packed, *around(packed, 1))
    cut = 4 * each + 8
    near_a = jnp.stack([n[:cut] for n in near])
    near_f = jnp.stack([n[cut:].reshape(-1, each, width) for n in near])
    around_a = around(near_a, 0)
    far_f = around(near_f, 0)
    pieces_a = both_cores((near_a, *around_a))
    xs, near_f = lax.optimization_barrier((xs, near_f))
    q, k, v, c, ps, plong, unit1, inv1, vecs, ub, gathered_a = attention_forward(
        short_lengths, long_lengths, pos, xs, xl, pieces_a, inner, dims
    )
    unit1, *far_f = lax.optimization_barrier((unit1, *far_f))
    early = (swap_cores(c), swap_cores(xs), swap_cores(xl))
    ub, *early = lax.optimization_barrier((ub, *early))
    keep_f, give_f, out_s, out_l, gfs, gatt, sums = feed(
        short_lengths, long_lengths, pos, unit1, cs, cl, inv1, ub, vecs, both_cores((near_f, *far_f)), dims
    )
    grads = attention_back(gatt, gathered_a, q, k, v, ps, plong, dims)
    grads, gatt_other, sums_other = lax.optimization_barrier((grads, swap_cores(gatt), swap_cores(sums)))
    others = (gatt_other, early[0], swap_cores(grads), *early[1:], sums_other)
    parts_f = pair_sum(keep_f, swap_cores(give_f))
    c, *parts_f = lax.optimization_barrier((c, *parts_f))
    around_f = around(parts_f, 0)
    parts_a = weight_back(pos, gatt, c, grads, xs, xl, sums, others)
    gfs, *both = lax.optimization_barrier((gfs, *parts_a, *around_f[:2]))
    parts_a, around_f = both[:RING], (*both[RING:], around_f[2])
    around_a = around(parts_a, 0)
    grad_s, grad_l = input_back(gfs, grads, gathered_a, dims)
    grad_s, *around_a = lax.optimization_barrier((grad_s, *around_a))
    up, down = finish_feed(second_turn(parts_f[0], *around_f), each, inner, tall)
    w_in, w_out, *vectors = finish_attention(second_turn(parts_a[0], *around_a), tall)
    vectors = [x.reshape(-1) for x in vectors]
    return (
        out_s.reshape(short_tokens.shape), out_l.reshape(long_tokens.shape),
        grad_s.reshape(short_tokens.shape), grad_l.reshape(long_tokens.shape),
        w_in, vectors[QB], vectors[VB], w_out, vectors[OB], vectors[G1], vectors[S1],
        up, vectors[8], down, vectors[DB], vectors[G2], vectors[S2],
    )


def solution(mesh):
    rows, flat = P(("rep", "shard"), None, None), P("shard")
    tall = P("shard", None)
    return jax.shard_map(
        on_device,
        mesh=mesh,
        in_specs=(
            rows, rows, P(("rep", "shard")), P(("rep", "shard")), rows, rows,
            tall, flat, flat, tall, flat, flat, flat, tall, flat, tall, flat, flat, flat,
        ),
        out_specs=(
            rows, rows, rows, rows,
            tall, flat, flat, tall, flat, flat, flat, tall, flat, tall, flat, flat, flat,
        ),
        check_vma=False,
    )
```

```python
import functools

import jax
import jax.numpy as jnp
from jax import lax
from jax.experimental import pallas as pl
from jax.experimental.pallas import tpu as pltpu
from jax.sharding import PartitionSpec as P

F32 = jnp.float32
BF16 = jnp.bfloat16
HEAD_DIM = 64
PAIR = 128
EPSILON = 1e-06
BACK_MIB = 58
QB, VB, OB, G1, S1, DB, G2, S2 = range(8)
RING = 4
CHIPS = RING * RING
SHARDS = 2 * CHIPS


def nn(a, b):
    return lax.dot_general(a, b, (((1,), (0,)), ((), ())), preferred_element_type=F32)


def nt(a, b):
    return lax.dot_general(a, b, (((1,), (1,)), ((), ())), preferred_element_type=F32)


def tn(a, b):
    return lax.dot_general(a, b, (((0,), (0,)), ((), ())), preferred_element_type=F32)


def iota(shape, dim):
    return lax.broadcasted_iota(jnp.int32, shape, dim)


def row_of(ref, i):
    return ref[i : i + 1, :].astype(F32)


def whole(*shape):
    return pl.BlockSpec(shape, lambda g, *_: (0,) * len(shape))


def params(mebibytes):
    return pltpu.CompilerParams(vmem_limit_bytes=mebibytes * 1024 * 1024)


def cost(flops, moved):
    return pl.CostEstimate(flops=int(flops), bytes_accessed=int(moved), transcendentals=0)


def places(pos, x, z):
    along_x, along_z = (x - pos[0]) & (RING - 1), (z - pos[1]) & (RING - 1)
    return along_x * RING + along_z, along_z * RING + along_x


def deal(keep, give, pos, value, at, each):
    first = pos[2] == 0
    for x in range(RING):
        for z in range(RING):
            p0, p1 = places(pos, x, z)
            low = 2 * (x * RING + z) * each
            even, odd = value[low : low + each], value[low + each : low + 2 * each]
            keep[jnp.where(first, p0, p1), at] = jnp.where(first, even, odd)
            give[jnp.where(first, p1, p0), at] = jnp.where(first, odd, even)


def spread(owners, width):
    each = width // owners
    at = iota((owners, width), 1)
    low = iota((owners, width), 0) * each
    return (at >= low) & (at < low + each)


def column_rest(rows, width, each):
    at = iota((1, width), 1)
    return jnp.broadcast_to(at - (at // each) * each, (rows, width))


def two_heads(pair):
    low_half = iota(pair.shape, 1) < HEAD_DIM
    zero = jnp.zeros_like(pair)
    return jnp.concatenate([jnp.where(low_half, pair, zero), jnp.where(low_half, zero, pair)], axis=0)


def own_lanes(stack):
    half = stack.shape[0] // 2
    return jnp.where(iota((half, stack.shape[1]), 1) < HEAD_DIM, stack[:half], stack[half:])


def normalized(hidden):
    center = hidden - jnp.mean(hidden, axis=-1, keepdims=True)
    spread_of = jnp.mean(center * center, axis=-1, keepdims=True)
    inverse = lax.rsqrt(spread_of + EPSILON)
    return center * inverse, inverse


def norm_back(scaled, unit, inverse):
    return inverse * (
        scaled
        - jnp.mean(scaled, axis=-1, keepdims=True)
        - unit * jnp.mean(scaled * unit, axis=-1, keepdims=True)
    )


def segments(dims):
    short_rows, long_count, long_length, _ = dims
    return [(0, short_rows, None)] + [
        (short_rows + i * long_length, long_length, i) for i in range(long_count)
    ]


def key_bias(slen, llen, short_length, rows, long_at):
    key = iota((rows, rows), 0)
    if long_at is not None:
        return jnp.where(key < llen[long_at], 0.0, -1e9).astype(F32)
    query = iota((rows, rows), 1)
    keep = jnp.zeros((rows, rows), jnp.bool_)
    for p in range(rows // short_length):
        low, high = p * short_length, (p + 1) * short_length
        keep = keep | ((key >= low) & (key < low + slen[p]) & (query >= low) & (query < high))
    return jnp.where(keep, 0.0, -1e9).astype(F32)


def valid_rows(slen, llen, dims):
    short_rows, long_count, long_length, short_length = dims
    parts = []
    at = iota((short_length, 1), 0)
    for p in range(short_rows // short_length):
        parts.append((at < slen[p]).astype(F32))
    at = iota((long_length, 1), 0)
    for p in range(long_count):
        parts.append((at < llen[p]).astype(F32))
    return jnp.concatenate(parts, axis=0)


def slabs_of(out, base, source, each, width):
    for j in range(source.shape[1] // width):
        out[base + j * each : base + (j + 1) * each] = source[:, j * width : (j + 1) * width]
    return base + source.shape[1] // width * each


def pack_body(wqkv, wo, wup, wdown, *rest):
    vectors, out = rest[:-1], rest[-1]
    each, width = wo.shape
    base = slabs_of(out, 0, wqkv, each, width)
    base = slabs_of(out, base, wo, each, width)
    out[base : base + 8] = jnp.zeros((8, width), BF16)
    for i, v in enumerate(vectors[:-1]):
        out[base : base + 1, i * each : (i + 1) * each] = v[...]
    out[base + 1 : base + 2, : vectors[-1].shape[1]] = vectors[-1][...]
    base = slabs_of(out, base + 8, wup, each, width)
    out[base:] = wdown[...]


def pack(wqkv, wo, wup, wdown, vectors, ub):
    each, width = wo.shape
    rows = wqkv.shape[1] // width * each + each + 8 + 2 * wdown.shape[0]
    return pl.pallas_call(
        pack_body,
        out_shape=jax.ShapeDtypeStruct((rows, width), BF16),
        compiler_params=params(58),
        name="pack",
    )(wqkv, wo, wup, wdown, *[v[None] for v in vectors], ub[None])


STEPS = (0, -1, 1, 2)


def gathered_at(pos, other, k, i):
    core = pos[2] ^ other
    x0, z0 = (pos[0] + STEPS[k]) & (RING - 1), (pos[1] + STEPS[i]) & (RING - 1)
    x1, z1 = (pos[0] + STEPS[i]) & (RING - 1), (pos[1] + STEPS[k]) & (RING - 1)
    return jnp.where(core == 0, (x0 * RING + z0) * 2, (x1 * RING + z1) * 2 + 1)


def arrivals(pos, pieces, target, sems, at):
    copies = []
    for other in range(2):
        for k in range(RING):
            for i in range(RING):
                n = (other * RING + k) * RING + i
                copies.append(
                    pltpu.make_async_copy(
                        pieces[other * RING + k].at[i, at], target.at[gathered_at(pos, other, k, i), at], sems.at[n]
                    )
                )
    return copies


def attention_forward_body(
    dims, slen, llen, pos, xs, xl, p0, p1, p2, p3, p4, p5, p6, p7,
    q_o, k_o, v_o, c_o, ps_o, pl_o, n_o, r_o, vecs_o, ub_o, gathered_o,
    x_all, total, wo_all, gathered, sems, out_sem,
):
    step = pl.program_id(0)
    short_rows, width = dims[0], x_all.shape[1]
    cols = q_o.shape[1]
    each = width // SHARDS
    keep_all = pltpu.make_async_copy(gathered, gathered_o, out_sem)

    @pl.when(step == 0)
    def _():
        copies = arrivals(pos, (p0, p1, p2, p3, p4, p5, p6, p7), gathered, sems, slice(None))
        for copy in copies:
            copy.start()
        x_all[:short_rows, :] = xs[...]
        x_all[short_rows:, :] = xl[...]
        total[...] = jnp.zeros_like(total)
        for copy in copies:
            copy.wait()
        keep_all.start()
        wo_all[...] = gathered[:, 3 * each : 4 * each].reshape(width, width)
        packed = gathered[:, 4 * each :]
        line = packed[:, 0, : 8 * each + 64]
        rest = column_rest(line.shape[1], width, each)
        mine = spread(SHARDS, width)
        for i in range(8):
            pick = (iota(rest.shape, 0) == rest + i * each).astype(BF16)
            row = jnp.sum(jnp.where(mine, nn(line, pick), 0.0), axis=0, keepdims=True)
            vecs_o[i : i + 1] = row.astype(BF16)
        inner = ub_o.shape[1]
        line = packed[:, 1, :128]
        pick = (iota((128, inner), 0) == column_rest(128, inner, inner // SHARDS)).astype(BF16)
        row = jnp.sum(jnp.where(spread(SHARDS, inner), nn(line, pick), 0.0), axis=0, keepdims=True)
        ub_o[...] = row.astype(BF16)

    x = x_all[...]
    at_cols = pl.ds(pl.multiple_of(step * cols, cols), cols)
    wq, wk, wv = (gathered[:, i * each : (i + 1) * each, at_cols].reshape(width, cols) for i in range(3))
    q_o[...] = (nn(x, wq) + vecs_o[QB : QB + 1, at_cols].astype(F32)).astype(BF16)
    k_o[...] = nn(x, wk).astype(BF16)
    v_o[...] = (nn(x, wv) + vecs_o[VB : VB + 1, at_cols].astype(F32)).astype(BF16)
    for first, rows, long_at in segments(dims):
        bias = key_bias(slen, llen, dims[3], rows, long_at)
        at = slice(first, first + rows)
        for pair in range(cols // PAIR):
            lanes = slice(pair * PAIR, (pair + 1) * PAIR)
            q = q_o[at, lanes] * jnp.asarray(HEAD_DIM**-0.5, BF16)
            scores = nt(two_heads(k_o[at, lanes]), q)
            probs = []
            for h in range(2):
                s = scores[h * rows : (h + 1) * rows] + bias
                e = jnp.exp(s - jnp.max(s, axis=0, keepdims=True))
                probs.append((e * (1.0 / jnp.sum(e, axis=0, keepdims=True))).astype(BF16))
            probs = jnp.concatenate(probs, axis=0)
            if long_at is None:
                ps_o[pair] = probs
            else:
                pl_o[long_at, pair] = probs
            c_o[at, lanes] = tn(probs, two_heads(v_o[at, lanes])).astype(BF16)
    total[...] += nn(c_o[...], wo_all[at_cols, :])

    @pl.when(step == pl.num_programs(0) - 1)
    def _():
        h = x_all[...].astype(F32) + (total[...] + row_of(vecs_o, OB))
        unit, inverse = normalized(h)
        n_o[...] = unit
        r_o[...] = inverse
        keep_all.wait()


def attention_forward(slen, llen, pos, xs, xl, pieces, inner, dims):
    rows, width = xs.shape[0] + xl.shape[0], xs.shape[1]
    short_rows, long_count, long_length, _ = dims
    step = 256
    steps, pairs = width // step, width // PAIR
    per = step // PAIR
    each_all = pieces[0].shape[1]
    cols = pl.BlockSpec((rows, step), lambda g, *_: (0, g))
    return pl.pallas_call(
        functools.partial(attention_forward_body, dims),
        grid_spec=pltpu.PrefetchScalarGridSpec(
            num_scalar_prefetch=3,
            grid=(steps,),
            in_specs=[
                whole(*xs.shape), whole(*xl.shape), *[pl.BlockSpec(memory_space=pl.ANY)] * 8,
            ],
            out_specs=[
                cols, cols, cols, cols,
                pl.BlockSpec((per, 2 * short_rows, short_rows), lambda g, *_: (g, 0, 0)),
                pl.BlockSpec((long_count, per, 2 * long_length, long_length), lambda g, *_: (0, g, 0, 0)),
                whole(rows, width), whole(rows, 1), whole(8, width), whole(1, inner),
                pl.BlockSpec(memory_space=pl.ANY),
            ],
            scratch_shapes=[
                pltpu.VMEM((rows, width), BF16), pltpu.VMEM((rows, width), F32), pltpu.VMEM((width, width), BF16),
                pltpu.VMEM((SHARDS, each_all, width), BF16), pltpu.SemaphoreType.DMA((SHARDS,)),
                pltpu.SemaphoreType.DMA(()),
            ],
        ),
        out_shape=[
            *[jax.ShapeDtypeStruct((rows, width), BF16)] * 4,
            jax.ShapeDtypeStruct((pairs, 2 * short_rows, short_rows), BF16),
            jax.ShapeDtypeStruct((long_count, pairs, 2 * long_length, long_length), BF16),
            jax.ShapeDtypeStruct((rows, width), F32),
            jax.ShapeDtypeStruct((rows, 1), F32),
            jax.ShapeDtypeStruct((8, width), BF16),
            jax.ShapeDtypeStruct((1, inner), BF16),
            jax.ShapeDtypeStruct((SHARDS, each_all, width), BF16),
        ],
        compiler_params=params(58),
        cost_estimate=cost(8 * rows * width * width, 20e6),
        name="attention_forward",
    )(slen, llen, pos, xs, xl, *pieces)


HBM = pl.BlockSpec(memory_space=pl.ANY)
ON_CHIP = pl.BlockSpec(memory_space=pltpu.VMEM)
SCALARS = pl.BlockSpec(memory_space=pltpu.SMEM)


class Copies:
    def __init__(self, sems):
        self.sems, self.used, self.open = sems, 0, []

    def start(self, source, target):
        copy = pltpu.make_async_copy(source, target, self.sems.at[self.used])
        self.used += 1
        copy.start()
        return copy

    def send(self, source, target):
        self.open.append(self.start(source, target))

    def finish(self):
        for copy in self.open:
            copy.wait()


def feed_body(
    dims, slen, llen, pos, unit1, cot_s, cot_l, inv1, ub, vecs, p0, p1, p2, p3, p4, p5, p6, p7,
    keep, give, outs_o, outl_o, gfs_o, gatt_o, sums_o,
    wup, wdown, unit_v, cot_v, low_v, low_t, hidden, gelu_v, grad_v, gffn, out_v, gatt, valid_v,
    keep_dv, give_dv, keep_uv, give_uv, sems, piece_sems, down_sems, up_sems,
):
    short_rows = dims[0]
    rows, width = low_v.shape
    parts, block = hidden.shape[0], hidden.shape[2]
    each, tall = width // SHARDS, block * parts // SHARDS
    owners, lanes, tile = SHARDS // parts, 256, 128
    copies = Copies(sems)
    pieces = (p0, p1, p2, p3, p4, p5, p6, p7)
    unit_here = copies.start(unit1, unit_v)
    groups = [[], [], []]
    for other in range(2):
        for k in range(RING):
            for i in range(RING):
                n = (other * RING + k) * RING + i
                at = gathered_at(pos, other, k, i)
                source = pieces[other * RING + k]
                half = parts // 2
                targets = (wup.at[:half, at], wup.at[half:, at], wdown.at[at])
                sources = (source.at[i, :half], source.at[i, half:parts], source.at[i, parts:])
                for group, sem, src, target in zip(groups, range(3), sources, targets):
                    group.append(pltpu.make_async_copy(src, target, piece_sems.at[sem, n]))
    for copy in groups[0]:
        copy.start()
    valid_v[...] = valid_rows(slen, llen, dims)
    grad_v[...] = jnp.zeros_like(grad_v)
    unit_here.wait()

    @pl.loop(0, rows // tile)
    def _(r):
        at = pl.ds(pl.multiple_of(r * tile, tile), tile)
        low_v[at] = (unit_v[at] * row_of(vecs, G1) + row_of(vecs, S1)).astype(BF16)

    @pl.loop(0, parts)
    def _(j):
        for n in range(2):

            @pl.when(j == n * (parts // 2))
            def _():
                for copy in groups[n]:
                    copy.wait()
                for copy in groups[n + 1]:
                    copy.start()

        bias = ub[:, pl.ds(pl.multiple_of(j * block, block), block)].astype(F32)
        pre = nn(low_v[...], wup[j].reshape(width, block)) + bias
        cdf = 0.5 + 0.5 * lax.erf(pre * (0.5**0.5))
        density = jnp.exp(-0.5 * pre * pre) * (0.5 / jnp.pi) ** 0.5
        hidden[j] = (pre * cdf).astype(BF16)
        gelu_v[j] = (cdf + pre * density).astype(BF16)

    for copy in groups[2]:
        copy.wait()
    cots_here = copies.start(cot_s, cot_v.at[:short_rows]), copies.start(cot_l, cot_v.at[short_rows:])

    @pl.loop(0, parts)
    def _(j):
        grad_v[...] += nn(hidden[j], wdown[pl.ds(j * owners, owners)].reshape(block, width))

    for copy in cots_here:
        copy.wait()
    sums_o[...] = jnp.zeros_like(sums_o)

    @pl.loop(0, rows // tile)
    def _(r):
        at = pl.ds(pl.multiple_of(r * tile, tile), tile)
        first = unit_v[at] * row_of(vecs, G1) + row_of(vecs, S1)
        unit, inverse = normalized(first + (grad_v[at] + row_of(vecs, DB)))
        valid = valid_v[at]
        out_v[at] = ((unit * row_of(vecs, G2) + row_of(vecs, S2)) * valid).astype(BF16)
        cot = cot_v[at].astype(F32) * valid
        back = norm_back(cot * row_of(vecs, G2), unit, inverse)
        grad_v[at] = back
        low_back = back.astype(BF16)
        gffn[at] = low_back
        sums_o[DB : DB + 1] += jnp.sum(low_back.astype(F32), axis=0, keepdims=True)
        sums_o[G2 : G2 + 1] += jnp.sum(cot * unit, axis=0, keepdims=True)
        sums_o[S2 : S2 + 1] += jnp.sum(cot, axis=0, keepdims=True)

    copies.send(out_v.at[:short_rows], outs_o)
    copies.send(out_v.at[short_rows:], outl_o)
    on_first = pos[2] == 0

    def down_copies(at, p0, p1):
        return (
            pltpu.make_async_copy(keep_dv.at[at], keep.at[jnp.where(on_first, p0, p1), :parts], down_sems.at[0, at]),
            pltpu.make_async_copy(give_dv.at[at], give.at[jnp.where(on_first, p1, p0), :parts], down_sems.at[1, at]),
        )

    @pl.loop(0, RING)
    def _(x):
        grad = tn(hidden[x], gffn[...]).astype(BF16)
        for z in range(RING):
            place = x * RING + z
            even, odd = grad[2 * z * tall : (2 * z + 1) * tall], grad[(2 * z + 1) * tall : (2 * z + 2) * tall]
            keep_dv[place] = jnp.where(on_first, even, odd).reshape(parts, each, width)
            give_dv[place] = jnp.where(on_first, odd, even).reshape(parts, each, width)
            for copy in down_copies(place, *places(pos, x, z)):
                copy.start()

    def up_copies(j):
        return (
            pltpu.make_async_copy(keep_uv.at[j], keep.at[:, parts + j], up_sems.at[0, j]),
            pltpu.make_async_copy(give_uv.at[j], give.at[:, parts + j], up_sems.at[1, j]),
        )

    low_t[:width] = low_v[...].T
    low_t[width:] = jnp.ones((16, rows), BF16)

    @pl.loop(0, parts)
    def _(j):
        weight = wdown[pl.ds(j * owners, owners)].reshape(block, width)
        up = (nt(gffn[...], weight) * gelu_v[j].astype(F32)).astype(BF16)
        hidden[j] = up
        grad = nn(low_t[...], hidden[j])
        sums_o[pl.ds(8 + j, 1)] = grad[width : width + 1]
        deal(keep_uv.at[j], give_uv.at[j], pos, grad[:width].astype(BF16), slice(None), each)
        for copy in up_copies(j):
            copy.start()

    @pl.loop(0, parts)
    def _(j):
        grad_v[...] += nt(hidden[j], wup[j].reshape(width, block))

    @pl.loop(0, rows // tile)
    def _(r):
        at = pl.ds(pl.multiple_of(r * tile, tile), tile)
        grad, unit = grad_v[at], unit_v[at]
        back = norm_back(grad * row_of(vecs, G1), unit, inv1[at])
        grad_v[at] = back
        low_back = back.astype(BF16)
        gatt[at] = low_back
        sums_o[OB : OB + 1] += jnp.sum(low_back.astype(F32), axis=0, keepdims=True)
        sums_o[G1 : G1 + 1] += jnp.sum(grad * unit, axis=0, keepdims=True)
        sums_o[S1 : S1 + 1] += jnp.sum(grad, axis=0, keepdims=True)

    copies.send(gatt, gatt_o)
    copies.send(grad_v, gfs_o)
    for at in range(CHIPS):
        for copy in down_copies(at, at, at):
            copy.wait()
    for j in range(parts):
        for copy in up_copies(j):
            copy.wait()
    copies.finish()


def feed(slen, llen, pos, unit1, cot_s, cot_l, inv1, ub, vecs, pieces, dims):
    rows, width = unit1.shape
    inner = ub.shape[1]
    parts = RING
    block, tall, each = inner // parts, inner // SHARDS, width // SHARDS
    down, up = (CHIPS, parts, each, width), (parts, CHIPS, each, width)
    return pl.pallas_call(
        functools.partial(feed_body, dims),
        in_specs=[SCALARS] * 3 + [HBM] * 3 + [ON_CHIP] * 3 + [HBM] * 8,
        out_specs=[HBM] * 6 + [ON_CHIP],
        scratch_shapes=[
            pltpu.VMEM((parts, SHARDS, each, width), BF16), pltpu.VMEM((SHARDS, parts, each, width), BF16),
            pltpu.VMEM((rows, width), F32), pltpu.VMEM((rows, width), BF16), pltpu.VMEM((rows, width), BF16),
            pltpu.VMEM((width + 16, rows), BF16), pltpu.VMEM((parts, rows, block), BF16),
            pltpu.VMEM((parts, rows, block), BF16), pltpu.VMEM((rows, width), F32), pltpu.VMEM((rows, width), BF16),
            pltpu.VMEM((rows, width), BF16), pltpu.VMEM((rows, width), BF16), pltpu.VMEM((rows, 1), F32),
            pltpu.VMEM(down, BF16), pltpu.VMEM(down, BF16), pltpu.VMEM(up, BF16), pltpu.VMEM(up, BF16),
            pltpu.SemaphoreType.DMA((8,)), pltpu.SemaphoreType.DMA((3, SHARDS)),
            pltpu.SemaphoreType.DMA((2, CHIPS)), pltpu.SemaphoreType.DMA((2, parts)),
        ],
        out_shape=[
            *[jax.ShapeDtypeStruct((CHIPS, 2 * parts, each, width), BF16)] * 2,
            jax.ShapeDtypeStruct(cot_s.shape, BF16),
            jax.ShapeDtypeStruct(cot_l.shape, BF16),
            jax.ShapeDtypeStruct((rows, width), F32),
            jax.ShapeDtypeStruct((rows, width), BF16),
            jax.ShapeDtypeStruct((16, width), F32),
        ],
        compiler_params=params(58),
        cost_estimate=cost(12 * rows * width * inner, 30e6),
        name="feed",
    )(slen, llen, pos, unit1, cot_s, cot_l, inv1, ub, vecs, *pieces)


def attention_back_body(dims, first_group, gatt, wo_block, q, k, v, ps, plong, grads, gc, wo_all):
    step = pl.program_id(0) + first_group
    width, cols = gatt.shape[1], q.shape[1]
    at_cols = pl.ds(pl.multiple_of(step * cols, cols), cols)

    @pl.when(step == first_group)
    def _():
        wo_all[...] = wo_block[...].reshape(width, width)

    gc[...] = nt(gatt[...], wo_all[at_cols, :]).astype(BF16)
    scale = HEAD_DIM**-0.5
    for first, rows, long_at in segments(dims):
        at = slice(first, first + rows)
        for pair in range(cols // PAIR):
            lanes = slice(pair * PAIR, (pair + 1) * PAIR)
            probs = ps[pair] if long_at is None else plong[long_at, pair]
            grad = gc[at, lanes]
            dp = nt(two_heads(v[at, lanes]), grad)
            ds = []
            for h in range(2):
                half = slice(h * rows, (h + 1) * rows)
                p = probs[half].astype(F32)
                d = dp[half]
                ds.append((p * (d - jnp.sum(d * p, axis=0, keepdims=True))).astype(BF16))
            ds = jnp.concatenate(ds, axis=0)
            grads[2, at, lanes] = own_lanes(nn(probs, grad)).astype(BF16)
            grads[1, at, lanes] = (own_lanes(nn(ds, q[at, lanes])) * scale).astype(BF16)
            grads[0, at, lanes] = (tn(ds, two_heads(k[at, lanes])) * scale).astype(BF16)


def attention_back(gatt, gathered, q, k, v, ps, plong, dims, groups):
    rows, width = gatt.shape
    short_rows, long_count, long_length, _ = dims
    step = 256
    per = step // PAIR
    low, high = groups
    cols = pl.BlockSpec((rows, step), lambda g: (0, g + low))
    return pl.pallas_call(
        functools.partial(attention_back_body, dims, low),
        grid=(high - low,),
        in_specs=[
            whole(rows, width),
            pl.BlockSpec((SHARDS, width // SHARDS, width), lambda g: (0, 3, 0)),
            cols, cols, cols,
            pl.BlockSpec((per, 2 * short_rows, short_rows), lambda g: (g + low, 0, 0)),
            pl.BlockSpec((long_count, per, 2 * long_length, long_length), lambda g: (0, g + low, 0, 0)),
        ],
        out_specs=pl.BlockSpec((3, rows, step), lambda g: (0, 0, g)),
        scratch_shapes=[pltpu.VMEM((rows, step), BF16), pltpu.VMEM((width, width), BF16)],
        out_shape=jax.ShapeDtypeStruct((3, rows, step * (high - low)), BF16),
        compiler_params=params(BACK_MIB),
        cost_estimate=cost(3 * (high - low) * rows * width * width, 5e6 * (high - low)),
        name="attention_back",
    )(gatt, gathered, q, k, v, ps, plong)


def weight_back_body(
    pos, gatt, gatt_other, c, c_other, d, d_other, d_last, d_last_other, xs, xl, xs_other, xl_other, sums_own, sums_other,
    o0, o1, o2, o3,
    x_t, c_t, grad, sums,
):
    step = pl.program_id(0)
    rows, width = c.shape
    cols = gatt.shape[1]
    each = width // SHARDS
    mine = CHIPS * each
    on_first = pos[2] == 0
    at_cols = pl.ds(pl.multiple_of(step * cols, cols), cols)

    def take(target, first, source):
        turned = source[...].T
        for i in range(CHIPS):
            low = 2 * i * each
            target[i * each : (i + 1) * each, first : first + turned.shape[1]] = jnp.where(
                on_first, turned[low : low + each], turned[low + each : low + 2 * each]
            )

    @pl.when(step == 0)
    def _():
        first = 0
        for source in (xs, xl, xs_other, xl_other):
            take(x_t, first, source)
            first += source.shape[0]
        x_t[mine:] = jnp.ones((16, 2 * rows), BF16)
        take(c_t, 0, c)
        take(c_t, rows, c_other)
        sums[...] = sums_own[...] + sums_other[...]

    def hand_out(value, at):
        n = value.shape[0] // CHIPS
        grad[:, :n] = value.reshape(CHIPS, n, cols)
        for along, out in enumerate((o0, o1, o2, o3)):
            for e in range(RING):
                x0, z0 = (pos[0] + along) & (RING - 1), (pos[1] + e) & (RING - 1)
                x1, z1 = (pos[0] + e) & (RING - 1), (pos[1] + along) & (RING - 1)
                out[e, at : at + n] = grad[jnp.where(on_first, x0 * RING + z0, x1 * RING + z1), :n]

    both = jnp.concatenate([gatt[...], gatt_other[...]], axis=0)
    hand_out(nn(c_t[...], both).astype(BF16), 3 * each)
    for i in range(3):
        last = step == pl.num_programs(0) - 1
        both = jnp.concatenate(
            [jnp.where(last, d_last[i], d[i]), jnp.where(last, d_last_other[i], d_other[i])], axis=0
        )
        total = nn(x_t[...], both)
        hand_out(total[:mine].astype(BF16), i * each)
        if i != 1:
            at = QB if i == 0 else VB
            sums[at : at + 1, at_cols] = total[mine : mine + 1]
    for out in (o0, o1, o2, o3):
        out[:, 4 * each :] = jnp.zeros((RING, 8, cols), BF16)

    @pl.when(step == pl.num_programs(0) - 1)
    def _():
        owned = spread(SHARDS, width)
        rest = column_rest(cols, width, each)
        line = jnp.zeros((SHARDS, cols), F32)
        for i in range(8):
            put = (iota(rest.shape, 0) == rest + i * each).astype(BF16)
            line += nt(jnp.where(owned, sums[i : i + 1], 0.0).astype(BF16), put)
        parts = RING
        place = width * parts // SHARDS
        wide_owned = spread(SHARDS // parts, width)
        put = (iota((cols, width), 0) == column_rest(cols, width, place)).astype(BF16)
        wide = jnp.concatenate(
            [nt(jnp.where(wide_owned, sums[8 + j : 9 + j], 0.0).astype(BF16), put) for j in range(parts)], axis=0
        )
        small = jnp.concatenate([line[:, None], wide[:, None], jnp.zeros((SHARDS, 6, cols), F32)], axis=1)
        small = small.reshape(CHIPS, 2, 8, cols)
        small = jnp.where(on_first, small[:, 0], small[:, 1])
        hand_out(small.reshape(CHIPS * 8, cols).astype(BF16), 4 * each)


def weight_back(pos, gatt, c, d, d_last, xs, xl, sums, others):
    gatt_other, c_other, d_other, d_last_other, xs_other, xl_other, sums_other = others
    rows, width = gatt.shape
    each = width // SHARDS
    step = 256
    cols = pl.BlockSpec((rows, step), lambda g, *_: (0, g))
    three = pl.BlockSpec((3, rows, step), lambda g, *_: (0, 0, jnp.minimum(g, width // step - 2)))
    out = pl.BlockSpec((RING, 4 * each + 8, step), lambda g, *_: (0, 0, g))
    return pl.pallas_call(
        weight_back_body,
        grid_spec=pltpu.PrefetchScalarGridSpec(
            num_scalar_prefetch=1,
            grid=(width // step,),
            in_specs=[
                cols, cols, whole(rows, width), whole(rows, width), three, three,
                whole(3, rows, step), whole(3, rows, step),
                whole(*xs.shape), whole(*xl.shape), whole(*xs.shape), whole(*xl.shape),
                whole(16, width), whole(16, width),
            ],
            out_specs=[out] * RING,
            scratch_shapes=[
                pltpu.VMEM((width // 2 + 16, 2 * rows), BF16), pltpu.VMEM((width // 2, 2 * rows), BF16),
                pltpu.VMEM((CHIPS, each, step), BF16), pltpu.VMEM((16, width), F32),
            ],
        ),
        out_shape=[jax.ShapeDtypeStruct((RING, 4 * each + 8, width), BF16)] * RING,
        compiler_params=params(BACK_MIB),
        cost_estimate=cost(8 * rows * width * width, 12e6),
        name="weight_back",
    )(pos, gatt, gatt_other, c, c_other, d, d_other, d_last, d_last_other, xs, xl, xs_other, xl_other, sums, sums_other)


def input_back_body(dims, gfs, d, d_last, wq, wk, wv, gs_o, gl_o, total):
    step = pl.program_id(0)
    short_rows, width, cols = dims[0], gfs.shape[1], d.shape[2]
    last = step == pl.num_programs(0) - 1
    dq, dk, dv = (jnp.where(last, d_last[i], d[i]) for i in range(3))
    part = (
        nt(dq, wq[...].reshape(width, cols))
        + nt(dk, wk[...].reshape(width, cols))
        + nt(dv, wv[...].reshape(width, cols))
    )

    @pl.when(step == 0)
    def _():
        total[...] = gfs[...] + part

    @pl.when(step > 0)
    def _():
        total[...] += part

    @pl.when(step == pl.num_programs(0) - 1)
    def _():
        gs_o[...] = total[:short_rows]
        gl_o[...] = total[short_rows:]


def input_back(gfs, d, d_last, gathered, dims):
    rows, width = gfs.shape
    each = width // SHARDS
    step = 256
    short_rows = dims[0]
    slab = lambda i: pl.BlockSpec((SHARDS, each, step), lambda g: (0, i, g))
    return pl.pallas_call(
        functools.partial(input_back_body, dims),
        grid=(width // step,),
        in_specs=[
            whole(rows, width), pl.BlockSpec((3, rows, step), lambda g: (0, 0, jnp.minimum(g, width // step - 2))),
            whole(3, rows, step), slab(0), slab(1), slab(2),
        ],
        out_specs=[whole(short_rows, width), whole(rows - short_rows, width)],
        scratch_shapes=[pltpu.VMEM((rows, width), F32)],
        out_shape=[
            jax.ShapeDtypeStruct((short_rows, width), F32),
            jax.ShapeDtypeStruct((rows - short_rows, width), F32),
        ],
        compiler_params=params(16),
        cost_estimate=cost(6 * rows * width * width, 12e6),
        name="input_back",
    )(gfs, d, d_last, gathered, gathered, gathered)


def pair_sum(keep, got):
    parts = []
    for d in range(RING):
        at = slice(d * RING, (d + 1) * RING)
        parts.append((keep[at].astype(F32) + got[at].astype(F32)).astype(BF16))
    return parts


def four_sum(own, left, right, far):
    return (own.astype(F32) + far.astype(F32)) + (left.astype(F32) + right.astype(F32))


def turn(delta, stage):
    moves = []
    for x in range(RING):
        for z in range(RING):
            for core in range(2):
                to_x, to_z = x, z
                if (core == 0) == (stage == 0):
                    to_x = (x + delta) % RING
                else:
                    to_z = (z + delta) % RING
                moves.append(((x * RING + z) * 2 + core, (to_x * RING + to_z) * 2 + core))
    return moves


def swap_cores(v):
    return lax.ppermute(v, "shard", [(i, i ^ 1) for i in range(SHARDS)])


def around(v, stage):
    return tuple(lax.ppermute(v[d] if isinstance(v, (list, tuple)) else v, "shard", turn(d, stage)) for d in (1, 3, 2))


def both_cores(pieces):
    return (*pieces, *(swap_cores(p) for p in pieces))


def second_turn(own, left, right, far):
    parts = [four_sum(own[d], left[d], right[d], far[d]).astype(BF16) for d in range(RING)]
    own = four_sum(parts[0], *around(parts, 1)).astype(BF16)
    return own, *(lax.ppermute(own, "rep", [(i, (i + d) % RING) for i in range(RING)]) for d in (1, 3, 2))


def replica_sum(own, left, right, far, at):
    return (own[at].astype(F32) + far[at].astype(F32)) + (left[at].astype(F32) + right[at].astype(F32))


def finish_attention_body(own, left, right, far, wqkv_o, wo_o, *vector_os):
    each, width = wo_o.shape
    for j in range(wqkv_o.shape[1] // width):
        at = slice(j * each, (j + 1) * each)
        wqkv_o[:, j * width : (j + 1) * width] = replica_sum(own, left, right, far, at)
    wo_o[...] = replica_sum(own, left, right, far, slice(3 * each, 4 * each))
    last = replica_sum(own, left, right, far, slice(4 * each, 4 * each + 8))[:, width - 256 :]
    for i, o in enumerate(vector_os[:-1]):
        o[...] = last[0:1, i * each : (i + 1) * each]
    o = vector_os[-1]
    o[...] = last[1:2, : o.shape[1]]


def finish_attention(arrays, tall):
    width = arrays[0].shape[1]
    each = width // SHARDS
    return pl.pallas_call(
        finish_attention_body,
        out_shape=[
            jax.ShapeDtypeStruct((each, 3 * width), F32),
            jax.ShapeDtypeStruct((each, width), F32),
            *[jax.ShapeDtypeStruct((1, each), F32)] * 8,
            jax.ShapeDtypeStruct((1, tall), F32),
        ],
        compiler_params=params(4),
        name="finish_attention",
    )(*arrays)


def finish_feed_body(own, left, right, far, up_o, down_o):
    parts = own.shape[0] // 2
    each, width = own.shape[1:]
    for j in range(parts):
        down_o[j * each : (j + 1) * each] = replica_sum(own, left, right, far, j)
        up_o[:, j * width : (j + 1) * width] = replica_sum(own, left, right, far, parts + j)


def finish_feed(arrays, each, inner, tall):
    width = arrays[0].shape[2]
    return pl.pallas_call(
        finish_feed_body,
        out_shape=[jax.ShapeDtypeStruct((each, inner), F32), jax.ShapeDtypeStruct((tall, width), F32)],
        compiler_params=params(4),
        name="finish_feed",
    )(*arrays)


def on_device(
    short_tokens, long_tokens, short_lengths, long_lengths, short_cotangent, long_cotangent,
    input_weight, query_bias, value_bias, output_weight, output_bias, first_gain, first_shift,
    up_weight, up_bias, down_weight, down_bias, second_gain, second_shift,
):
    short_count, short_length, width = short_tokens.shape
    long_count, long_length, _ = long_tokens.shape
    dims = (short_count * short_length, long_count, long_length, short_length)
    each, inner, tall = width // SHARDS, up_weight.shape[1], down_weight.shape[0]
    xs, xl = short_tokens.reshape(-1, width), long_tokens.reshape(-1, width)
    cs, cl = short_cotangent.reshape(-1, width), long_cotangent.reshape(-1, width)
    index = lax.axis_index("shard")
    pos = jnp.stack([index // 8, (index // 2) % 4, index % 2]).astype(jnp.int32)

    packed = pack(
        input_weight, output_weight, up_weight, down_weight,
        (query_bias, value_bias, output_bias, first_gain, first_shift, down_bias, second_gain, second_shift),
        up_bias,
    )
    *near, xs_other, xl_other = lax.optimization_barrier(
        (packed, *around(packed, 1), swap_cores(xs), swap_cores(xl))
    )
    cut = 4 * each + 8
    near_a = jnp.stack([n[:cut] for n in near])
    near_f = jnp.stack([n[cut:].reshape(-1, each, width) for n in near])
    around_a = around(near_a, 0)
    far_f = around(near_f, 0)
    pieces_a = both_cores((near_a, *around_a))
    xs, near_f = lax.optimization_barrier((xs, near_f))
    q, k, v, c, ps, plong, unit1, inv1, vecs, ub, gathered_a = attention_forward(
        short_lengths, long_lengths, pos, xs, xl, pieces_a, inner, dims
    )
    unit1, *far_f = lax.optimization_barrier((unit1, *far_f))
    ub, c_other = lax.optimization_barrier((ub, swap_cores(c)))
    keep_f, give_f, out_s, out_l, gfs, gatt, sums = feed(
        short_lengths, long_lengths, pos, unit1, cs, cl, inv1, ub, vecs, both_cores((near_f, *far_f)), dims
    )
    groups = width // 256
    grads = attention_back(gatt, gathered_a, q, k, v, ps, plong, dims, (0, groups - 1))
    got_f, gatt_other, sums_other, grads = lax.optimization_barrier(
        (swap_cores(give_f), swap_cores(gatt), swap_cores(sums), grads)
    )
    grads_other = swap_cores(grads)
    parts_f = pair_sum(keep_f, got_f)
    gatt, *parts_f = lax.optimization_barrier((gatt, *parts_f))
    around_f = around(parts_f, 0)
    grads_last = attention_back(gatt, gathered_a, q, k, v, ps, plong, dims, (groups - 1, groups))
    others = (gatt_other, c_other, grads_other, swap_cores(grads_last), xs_other, xl_other, sums_other)
    parts_a = weight_back(pos, gatt, c, grads, grads_last, xs, xl, sums, others)
    gfs, *both = lax.optimization_barrier((gfs, *parts_a, *around_f[:2]))
    parts_a, around_f = both[:RING], (*both[RING:], around_f[2])
    around_a = around(parts_a, 0)
    grad_s, grad_l = input_back(gfs, grads, grads_last, gathered_a, dims)
    grad_s, *around_a = lax.optimization_barrier((grad_s, *around_a))
    up, down = finish_feed(second_turn(parts_f[0], *around_f), each, inner, tall)
    w_in, w_out, *vectors = finish_attention(second_turn(parts_a[0], *around_a), tall)
    vectors = [x.reshape(-1) for x in vectors]
    return (
        out_s.reshape(short_tokens.shape), out_l.reshape(long_tokens.shape),
        grad_s.reshape(short_tokens.shape), grad_l.reshape(long_tokens.shape),
        w_in, vectors[QB], vectors[VB], w_out, vectors[OB], vectors[G1], vectors[S1],
        up, vectors[8], down, vectors[DB], vectors[G2], vectors[S2],
    )


def solution(mesh):
    rows, flat = P(("rep", "shard"), None, None), P("shard")
    tall = P("shard", None)
    return jax.shard_map(
        on_device,
        mesh=mesh,
        in_specs=(
            rows, rows, P(("rep", "shard")), P(("rep", "shard")), rows, rows,
            tall, flat, flat, tall, flat, flat, flat, tall, flat, tall, flat, flat, flat,
        ),
        out_specs=(
            rows, rows, rows, rows,
            tall, flat, flat, tall, flat, flat, flat, tall, flat, tall, flat, flat, flat,
        ),
        check_vma=False,
    )
```

```python
import functools

import jax
import jax.numpy as jnp
from jax import lax
from jax.experimental import pallas as pl
from jax.experimental.pallas import tpu as pltpu
from jax.sharding import PartitionSpec as P

F32 = jnp.float32
BF16 = jnp.bfloat16
HEAD_DIM = 64
PAIR = 128
EPSILON = 1e-06
BACK_MIB = 58
QB, VB, OB, G1, S1, DB, G2, S2 = range(8)
RING = 4
CHIPS = RING * RING
SHARDS = 2 * CHIPS


def nn(a, b):
    return lax.dot_general(a, b, (((1,), (0,)), ((), ())), preferred_element_type=F32)


def nt(a, b):
    return lax.dot_general(a, b, (((1,), (1,)), ((), ())), preferred_element_type=F32)


def tn(a, b):
    return lax.dot_general(a, b, (((0,), (0,)), ((), ())), preferred_element_type=F32)


def iota(shape, dim):
    return lax.broadcasted_iota(jnp.int32, shape, dim)


def row_of(ref, i):
    return ref[i : i + 1, :].astype(F32)


def whole(*shape):
    return pl.BlockSpec(shape, lambda g, *_: (0,) * len(shape))


def params(mebibytes):
    return pltpu.CompilerParams(vmem_limit_bytes=mebibytes * 1024 * 1024)


def cost(flops, moved):
    return pl.CostEstimate(flops=int(flops), bytes_accessed=int(moved), transcendentals=0)


def places(pos, x, z):
    along_x, along_z = (x - pos[0]) & (RING - 1), (z - pos[1]) & (RING - 1)
    return along_x * RING + along_z, along_z * RING + along_x


def deal(keep, give, pos, value, at, each):
    first = pos[2] == 0
    for x in range(RING):
        for z in range(RING):
            p0, p1 = places(pos, x, z)
            low = 2 * (x * RING + z) * each
            even, odd = value[low : low + each], value[low + each : low + 2 * each]
            keep[jnp.where(first, p0, p1), at] = jnp.where(first, even, odd)
            give[jnp.where(first, p1, p0), at] = jnp.where(first, odd, even)


def spread(owners, width):
    each = width // owners
    at = iota((owners, width), 1)
    low = iota((owners, width), 0) * each
    return (at >= low) & (at < low + each)


def column_rest(rows, width, each):
    at = iota((1, width), 1)
    return jnp.broadcast_to(at - (at // each) * each, (rows, width))


def two_heads(pair):
    low_half = iota(pair.shape, 1) < HEAD_DIM
    zero = jnp.zeros_like(pair)
    return jnp.concatenate([jnp.where(low_half, pair, zero), jnp.where(low_half, zero, pair)], axis=0)


def own_lanes(stack):
    half = stack.shape[0] // 2
    return jnp.where(iota((half, stack.shape[1]), 1) < HEAD_DIM, stack[:half], stack[half:])


def normalized(hidden):
    center = hidden - jnp.mean(hidden, axis=-1, keepdims=True)
    spread_of = jnp.mean(center * center, axis=-1, keepdims=True)
    inverse = lax.rsqrt(spread_of + EPSILON)
    return center * inverse, inverse


def norm_back(scaled, unit, inverse):
    return inverse * (
        scaled
        - jnp.mean(scaled, axis=-1, keepdims=True)
        - unit * jnp.mean(scaled * unit, axis=-1, keepdims=True)
    )


def segments(dims):
    short_rows, long_count, long_length, _ = dims
    return [(0, short_rows, None)] + [
        (short_rows + i * long_length, long_length, i) for i in range(long_count)
    ]


def key_bias(slen, llen, short_length, rows, long_at):
    key = iota((rows, rows), 0)
    if long_at is not None:
        return jnp.where(key < llen[long_at], 0.0, -1e9).astype(F32)
    query = iota((rows, rows), 1)
    keep = jnp.zeros((rows, rows), jnp.bool_)
    for p in range(rows // short_length):
        low, high = p * short_length, (p + 1) * short_length
        keep = keep | ((key >= low) & (key < low + slen[p]) & (query >= low) & (query < high))
    return jnp.where(keep, 0.0, -1e9).astype(F32)


def valid_rows(slen, llen, dims):
    short_rows, long_count, long_length, short_length = dims
    parts = []
    at = iota((short_length, 1), 0)
    for p in range(short_rows // short_length):
        parts.append((at < slen[p]).astype(F32))
    at = iota((long_length, 1), 0)
    for p in range(long_count):
        parts.append((at < llen[p]).astype(F32))
    return jnp.concatenate(parts, axis=0)


def slabs_of(out, base, source, each, width):
    for j in range(source.shape[1] // width):
        out[base + j * each : base + (j + 1) * each] = source[:, j * width : (j + 1) * width]
    return base + source.shape[1] // width * each


def pack_body(wqkv, wo, wup, wdown, *rest):
    vectors, out = rest[:-1], rest[-1]
    each, width = wo.shape
    base = slabs_of(out, 0, wqkv, each, width)
    base = slabs_of(out, base, wo, each, width)
    out[base : base + 8] = jnp.zeros((8, width), BF16)
    for i, v in enumerate(vectors[:-1]):
        out[base : base + 1, i * each : (i + 1) * each] = v[...]
    out[base + 1 : base + 2, : vectors[-1].shape[1]] = vectors[-1][...]
    base = slabs_of(out, base + 8, wup, each, width)
    out[base:] = wdown[...]


def pack(wqkv, wo, wup, wdown, vectors, ub):
    each, width = wo.shape
    rows = wqkv.shape[1] // width * each + each + 8 + 2 * wdown.shape[0]
    return pl.pallas_call(
        pack_body,
        out_shape=jax.ShapeDtypeStruct((rows, width), BF16),
        compiler_params=params(58),
        name="pack",
    )(wqkv, wo, wup, wdown, *[v[None] for v in vectors], ub[None])


STEPS = (0, -1, 1, 2)


def gathered_at(pos, other, k, i):
    core = pos[2] ^ other
    x0, z0 = (pos[0] + STEPS[k]) & (RING - 1), (pos[1] + STEPS[i]) & (RING - 1)
    x1, z1 = (pos[0] + STEPS[i]) & (RING - 1), (pos[1] + STEPS[k]) & (RING - 1)
    return jnp.where(core == 0, (x0 * RING + z0) * 2, (x1 * RING + z1) * 2 + 1)


def arrivals(pos, pieces, target, sems, at):
    copies = []
    for other in range(2):
        for k in range(RING):
            for i in range(RING):
                n = (other * RING + k) * RING + i
                copies.append(
                    pltpu.make_async_copy(
                        pieces[other * RING + k].at[i, at], target.at[gathered_at(pos, other, k, i), at], sems.at[n]
                    )
                )
    return copies


def attention_forward_body(
    dims, slen, llen, pos, xs, xl, p0, p1, p2, p3, p4, p5, p6, p7,
    q_o, k_o, v_o, c_o, ps_o, pl_o, n_o, r_o, vecs_o, ub_o, gathered_o,
    x_all, total, wo_all, gathered, sems, out_sem,
):
    step = pl.program_id(0)
    short_rows, width = dims[0], x_all.shape[1]
    cols = q_o.shape[1]
    each = width // SHARDS
    keep_all = pltpu.make_async_copy(gathered, gathered_o, out_sem)

    @pl.when(step == 0)
    def _():
        copies = arrivals(pos, (p0, p1, p2, p3, p4, p5, p6, p7), gathered, sems, slice(None))
        for copy in copies:
            copy.start()
        x_all[:short_rows, :] = xs[...]
        x_all[short_rows:, :] = xl[...]
        total[...] = jnp.zeros_like(total)
        for copy in copies:
            copy.wait()
        keep_all.start()
        wo_all[...] = gathered[:, 3 * each : 4 * each].reshape(width, width)
        packed = gathered[:, 4 * each :]
        line = packed[:, 0, : 8 * each + 64]
        rest = column_rest(line.shape[1], width, each)
        mine = spread(SHARDS, width)
        for i in range(8):
            pick = (iota(rest.shape, 0) == rest + i * each).astype(BF16)
            row = jnp.sum(jnp.where(mine, nn(line, pick), 0.0), axis=0, keepdims=True)
            vecs_o[i : i + 1] = row.astype(BF16)
        inner = ub_o.shape[1]
        line = packed[:, 1, :128]
        pick = (iota((128, inner), 0) == column_rest(128, inner, inner // SHARDS)).astype(BF16)
        row = jnp.sum(jnp.where(spread(SHARDS, inner), nn(line, pick), 0.0), axis=0, keepdims=True)
        ub_o[...] = row.astype(BF16)

    x = x_all[...]
    at_cols = pl.ds(pl.multiple_of(step * cols, cols), cols)
    wq, wk, wv = (gathered[:, i * each : (i + 1) * each, at_cols].reshape(width, cols) for i in range(3))
    q_o[...] = (nn(x, wq) + vecs_o[QB : QB + 1, at_cols].astype(F32)).astype(BF16)
    k_o[...] = nn(x, wk).astype(BF16)
    v_o[...] = (nn(x, wv) + vecs_o[VB : VB + 1, at_cols].astype(F32)).astype(BF16)
    for first, rows, long_at in segments(dims):
        bias = key_bias(slen, llen, dims[3], rows, long_at)
        at = slice(first, first + rows)
        for pair in range(cols // PAIR):
            lanes = slice(pair * PAIR, (pair + 1) * PAIR)
            q = q_o[at, lanes] * jnp.asarray(HEAD_DIM**-0.5, BF16)
            scores = nt(two_heads(k_o[at, lanes]), q)
            probs = []
            for h in range(2):
                s = scores[h * rows : (h + 1) * rows] + bias
                e = jnp.exp(s - jnp.max(s, axis=0, keepdims=True))
                probs.append((e * (1.0 / jnp.sum(e, axis=0, keepdims=True))).astype(BF16))
            probs = jnp.concatenate(probs, axis=0)
            if long_at is None:
                ps_o[pair] = probs
            else:
                pl_o[long_at, pair] = probs
            c_o[at, lanes] = tn(probs, two_heads(v_o[at, lanes])).astype(BF16)
    total[...] += nn(c_o[...], wo_all[at_cols, :])

    @pl.when(step == pl.num_programs(0) - 1)
    def _():
        h = x_all[...].astype(F32) + (total[...] + row_of(vecs_o, OB))
        unit, inverse = normalized(h)
        n_o[...] = unit
        r_o[...] = inverse
        keep_all.wait()


def attention_forward(slen, llen, pos, xs, xl, pieces, inner, dims):
    rows, width = xs.shape[0] + xl.shape[0], xs.shape[1]
    short_rows, long_count, long_length, _ = dims
    step = 256
    steps, pairs = width // step, width // PAIR
    per = step // PAIR
    each_all = pieces[0].shape[1]
    cols = pl.BlockSpec((rows, step), lambda g, *_: (0, g))
    return pl.pallas_call(
        functools.partial(attention_forward_body, dims),
        grid_spec=pltpu.PrefetchScalarGridSpec(
            num_scalar_prefetch=3,
            grid=(steps,),
            in_specs=[
                whole(*xs.shape), whole(*xl.shape), *[pl.BlockSpec(memory_space=pl.ANY)] * 8,
            ],
            out_specs=[
                cols, cols, cols, cols,
                pl.BlockSpec((per, 2 * short_rows, short_rows), lambda g, *_: (g, 0, 0)),
                pl.BlockSpec((long_count, per, 2 * long_length, long_length), lambda g, *_: (0, g, 0, 0)),
                whole(rows, width), whole(rows, 1), whole(8, width), whole(1, inner),
                pl.BlockSpec(memory_space=pl.ANY),
            ],
            scratch_shapes=[
                pltpu.VMEM((rows, width), BF16), pltpu.VMEM((rows, width), F32), pltpu.VMEM((width, width), BF16),
                pltpu.VMEM((SHARDS, each_all, width), BF16), pltpu.SemaphoreType.DMA((SHARDS,)),
                pltpu.SemaphoreType.DMA(()),
            ],
        ),
        out_shape=[
            *[jax.ShapeDtypeStruct((rows, width), BF16)] * 4,
            jax.ShapeDtypeStruct((pairs, 2 * short_rows, short_rows), BF16),
            jax.ShapeDtypeStruct((long_count, pairs, 2 * long_length, long_length), BF16),
            jax.ShapeDtypeStruct((rows, width), F32),
            jax.ShapeDtypeStruct((rows, 1), F32),
            jax.ShapeDtypeStruct((8, width), BF16),
            jax.ShapeDtypeStruct((1, inner), BF16),
            jax.ShapeDtypeStruct((SHARDS, each_all, width), BF16),
        ],
        compiler_params=params(58),
        cost_estimate=cost(8 * rows * width * width, 20e6),
        name="attention_forward",
    )(slen, llen, pos, xs, xl, *pieces)


HBM = pl.BlockSpec(memory_space=pl.ANY)
ON_CHIP = pl.BlockSpec(memory_space=pltpu.VMEM)
SCALARS = pl.BlockSpec(memory_space=pltpu.SMEM)


class Copies:
    def __init__(self, sems):
        self.sems, self.used, self.open = sems, 0, []

    def start(self, source, target):
        copy = pltpu.make_async_copy(source, target, self.sems.at[self.used])
        self.used += 1
        copy.start()
        return copy

    def send(self, source, target):
        self.open.append(self.start(source, target))

    def finish(self):
        for copy in self.open:
            copy.wait()


def feed_body(
    dims, slen, llen, pos, unit1, cot_s, cot_l, inv1, ub, vecs, p0, p1, p2, p3, p4, p5, p6, p7,
    keep, give, outs_o, outl_o, gfs_o, gatt_o, sums_o,
    wup, wdown, unit_v, cot_v, low_v, low_t, hidden, gelu_v, grad_v, gffn, out_v, gatt, valid_v,
    keep_dv, give_dv, keep_uv, give_uv, sems, piece_sems, down_sems, up_sems,
):
    short_rows = dims[0]
    rows, width = low_v.shape
    parts, block = hidden.shape[0], hidden.shape[2]
    each, tall = width // SHARDS, block * parts // SHARDS
    owners, lanes, tile = SHARDS // parts, 256, 128
    copies = Copies(sems)
    pieces = (p0, p1, p2, p3, p4, p5, p6, p7)
    unit_here = copies.start(unit1, unit_v)
    groups = [[], [], []]
    for other in range(2):
        for k in range(RING):
            for i in range(RING):
                n = (other * RING + k) * RING + i
                at = gathered_at(pos, other, k, i)
                source = pieces[other * RING + k]
                half = parts // 2
                targets = (wup.at[:half, at], wup.at[half:, at], wdown.at[at])
                sources = (source.at[i, :half], source.at[i, half:parts], source.at[i, parts:])
                for group, sem, src, target in zip(groups, range(3), sources, targets):
                    group.append(pltpu.make_async_copy(src, target, piece_sems.at[sem, n]))
    for copy in groups[0]:
        copy.start()
    valid_v[...] = valid_rows(slen, llen, dims)
    grad_v[...] = jnp.zeros_like(grad_v)
    unit_here.wait()

    @pl.loop(0, rows // tile)
    def _(r):
        at = pl.ds(pl.multiple_of(r * tile, tile), tile)
        low_v[at] = (unit_v[at] * row_of(vecs, G1) + row_of(vecs, S1)).astype(BF16)

    @pl.loop(0, parts)
    def _(j):
        for n in range(2):

            @pl.when(j == n * (parts // 2))
            def _():
                for copy in groups[n]:
                    copy.wait()
                for copy in groups[n + 1]:
                    copy.start()

        bias = ub[:, pl.ds(pl.multiple_of(j * block, block), block)].astype(F32)
        pre = nn(low_v[...], wup[j].reshape(width, block)) + bias
        cdf = 0.5 + 0.5 * lax.erf(pre * (0.5**0.5))
        density = jnp.exp(-0.5 * pre * pre) * (0.5 / jnp.pi) ** 0.5
        hidden[j] = (pre * cdf).astype(BF16)
        gelu_v[j] = (cdf + pre * density).astype(BF16)

    for copy in groups[2]:
        copy.wait()
    cots_here = copies.start(cot_s, cot_v.at[:short_rows]), copies.start(cot_l, cot_v.at[short_rows:])

    @pl.loop(0, parts)
    def _(j):
        grad_v[...] += nn(hidden[j], wdown[pl.ds(j * owners, owners)].reshape(block, width))

    for copy in cots_here:
        copy.wait()
    sums_o[...] = jnp.zeros_like(sums_o)

    @pl.loop(0, rows // tile)
    def _(r):
        at = pl.ds(pl.multiple_of(r * tile, tile), tile)
        first = unit_v[at] * row_of(vecs, G1) + row_of(vecs, S1)
        unit, inverse = normalized(first + (grad_v[at] + row_of(vecs, DB)))
        valid = valid_v[at]
        out_v[at] = ((unit * row_of(vecs, G2) + row_of(vecs, S2)) * valid).astype(BF16)
        cot = cot_v[at].astype(F32) * valid
        back = norm_back(cot * row_of(vecs, G2), unit, inverse)
        grad_v[at] = back
        low_back = back.astype(BF16)
        gffn[at] = low_back
        sums_o[DB : DB + 1] += jnp.sum(low_back.astype(F32), axis=0, keepdims=True)
        sums_o[G2 : G2 + 1] += jnp.sum(cot * unit, axis=0, keepdims=True)
        sums_o[S2 : S2 + 1] += jnp.sum(cot, axis=0, keepdims=True)

    copies.send(out_v.at[:short_rows], outs_o)
    copies.send(out_v.at[short_rows:], outl_o)
    on_first = pos[2] == 0

    def down_copies(at, p0, p1):
        return (
            pltpu.make_async_copy(keep_dv.at[at], keep.at[jnp.where(on_first, p0, p1), :parts], down_sems.at[0, at]),
            pltpu.make_async_copy(give_dv.at[at], give.at[jnp.where(on_first, p1, p0), :parts], down_sems.at[1, at]),
        )

    @pl.loop(0, RING)
    def _(x):
        grad = tn(hidden[x], gffn[...]).astype(BF16)
        for z in range(RING):
            place = x * RING + z
            even, odd = grad[2 * z * tall : (2 * z + 1) * tall], grad[(2 * z + 1) * tall : (2 * z + 2) * tall]
            keep_dv[place] = jnp.where(on_first, even, odd).reshape(parts, each, width)
            give_dv[place] = jnp.where(on_first, odd, even).reshape(parts, each, width)
            for copy in down_copies(place, *places(pos, x, z)):
                copy.start()

    def up_copies(j):
        return (
            pltpu.make_async_copy(keep_uv.at[j], keep.at[:, parts + j], up_sems.at[0, j]),
            pltpu.make_async_copy(give_uv.at[j], give.at[:, parts + j], up_sems.at[1, j]),
        )

    low_t[:width] = low_v[...].T
    low_t[width:] = jnp.ones((16, rows), BF16)

    @pl.loop(0, parts)
    def _(j):
        weight = wdown[pl.ds(j * owners, owners)].reshape(block, width)
        up = (nt(gffn[...], weight) * gelu_v[j].astype(F32)).astype(BF16)
        hidden[j] = up
        grad = nn(low_t[...], hidden[j])
        sums_o[pl.ds(8 + j, 1)] = grad[width : width + 1]
        deal(keep_uv.at[j], give_uv.at[j], pos, grad[:width].astype(BF16), slice(None), each)
        for copy in up_copies(j):
            copy.start()

    @pl.loop(0, parts)
    def _(j):
        grad_v[...] += nt(hidden[j], wup[j].reshape(width, block))

    @pl.loop(0, rows // tile)
    def _(r):
        at = pl.ds(pl.multiple_of(r * tile, tile), tile)
        grad, unit = grad_v[at], unit_v[at]
        back = norm_back(grad * row_of(vecs, G1), unit, inv1[at])
        grad_v[at] = back
        low_back = back.astype(BF16)
        gatt[at] = low_back
        sums_o[OB : OB + 1] += jnp.sum(low_back.astype(F32), axis=0, keepdims=True)
        sums_o[G1 : G1 + 1] += jnp.sum(grad * unit, axis=0, keepdims=True)
        sums_o[S1 : S1 + 1] += jnp.sum(grad, axis=0, keepdims=True)

    copies.send(gatt, gatt_o)
    copies.send(grad_v, gfs_o)
    for at in range(CHIPS):
        for copy in down_copies(at, at, at):
            copy.wait()
    for j in range(parts):
        for copy in up_copies(j):
            copy.wait()
    copies.finish()


def feed(slen, llen, pos, unit1, cot_s, cot_l, inv1, ub, vecs, pieces, dims):
    rows, width = unit1.shape
    inner = ub.shape[1]
    parts = RING
    block, tall, each = inner // parts, inner // SHARDS, width // SHARDS
    down, up = (CHIPS, parts, each, width), (parts, CHIPS, each, width)
    return pl.pallas_call(
        functools.partial(feed_body, dims),
        in_specs=[SCALARS] * 3 + [HBM] * 3 + [ON_CHIP] * 3 + [HBM] * 8,
        out_specs=[HBM] * 6 + [ON_CHIP],
        scratch_shapes=[
            pltpu.VMEM((parts, SHARDS, each, width), BF16), pltpu.VMEM((SHARDS, parts, each, width), BF16),
            pltpu.VMEM((rows, width), F32), pltpu.VMEM((rows, width), BF16), pltpu.VMEM((rows, width), BF16),
            pltpu.VMEM((width + 16, rows), BF16), pltpu.VMEM((parts, rows, block), BF16),
            pltpu.VMEM((parts, rows, block), BF16), pltpu.VMEM((rows, width), F32), pltpu.VMEM((rows, width), BF16),
            pltpu.VMEM((rows, width), BF16), pltpu.VMEM((rows, width), BF16), pltpu.VMEM((rows, 1), F32),
            pltpu.VMEM(down, BF16), pltpu.VMEM(down, BF16), pltpu.VMEM(up, BF16), pltpu.VMEM(up, BF16),
            pltpu.SemaphoreType.DMA((8,)), pltpu.SemaphoreType.DMA((3, SHARDS)),
            pltpu.SemaphoreType.DMA((2, CHIPS)), pltpu.SemaphoreType.DMA((2, parts)),
        ],
        out_shape=[
            *[jax.ShapeDtypeStruct((CHIPS, 2 * parts, each, width), BF16)] * 2,
            jax.ShapeDtypeStruct(cot_s.shape, BF16),
            jax.ShapeDtypeStruct(cot_l.shape, BF16),
            jax.ShapeDtypeStruct((rows, width), F32),
            jax.ShapeDtypeStruct((rows, width), BF16),
            jax.ShapeDtypeStruct((16, width), F32),
        ],
        compiler_params=params(58),
        cost_estimate=cost(12 * rows * width * inner, 30e6),
        name="feed",
    )(slen, llen, pos, unit1, cot_s, cot_l, inv1, ub, vecs, *pieces)


def attention_back_body(dims, gatt, wo_block, q, k, v, ps, plong, grads, gc, wo_all):
    step = pl.program_id(0)
    width, cols = gatt.shape[1], q.shape[1]
    at_cols = pl.ds(pl.multiple_of(step * cols, cols), cols)

    @pl.when(step == 0)
    def _():
        wo_all[...] = wo_block[...].reshape(width, width)

    gc[...] = nt(gatt[...], wo_all[at_cols, :]).astype(BF16)
    scale = HEAD_DIM**-0.5
    for first, rows, long_at in segments(dims):
        at = slice(first, first + rows)
        for pair in range(cols // PAIR):
            lanes = slice(pair * PAIR, (pair + 1) * PAIR)
            probs = ps[pair] if long_at is None else plong[long_at, pair]
            grad = gc[at, lanes]
            dp = nt(two_heads(v[at, lanes]), grad)
            ds = []
            for h in range(2):
                half = slice(h * rows, (h + 1) * rows)
                p = probs[half].astype(F32)
                d = dp[half]
                ds.append((p * (d - jnp.sum(d * p, axis=0, keepdims=True))).astype(BF16))
            ds = jnp.concatenate(ds, axis=0)
            grads[2, at, lanes] = own_lanes(nn(probs, grad)).astype(BF16)
            grads[1, at, lanes] = (own_lanes(nn(ds, q[at, lanes])) * scale).astype(BF16)
            grads[0, at, lanes] = (tn(ds, two_heads(k[at, lanes])) * scale).astype(BF16)


def attention_back(gatt, gathered, q, k, v, ps, plong, dims):
    rows, width = gatt.shape
    short_rows, long_count, long_length, _ = dims
    step = 256
    per = step // PAIR
    cols = pl.BlockSpec((rows, step), lambda g: (0, g))
    return pl.pallas_call(
        functools.partial(attention_back_body, dims),
        grid=(width // step,),
        in_specs=[
            whole(rows, width),
            pl.BlockSpec((SHARDS, width // SHARDS, width), lambda g: (0, 3, 0)),
            cols, cols, cols,
            pl.BlockSpec((per, 2 * short_rows, short_rows), lambda g: (g, 0, 0)),
            pl.BlockSpec((long_count, per, 2 * long_length, long_length), lambda g: (0, g, 0, 0)),
        ],
        out_specs=pl.BlockSpec((3, rows, step), lambda g: (0, 0, g)),
        scratch_shapes=[pltpu.VMEM((rows, step), BF16), pltpu.VMEM((width, width), BF16)],
        out_shape=jax.ShapeDtypeStruct((3, rows, width), BF16),
        compiler_params=params(BACK_MIB),
        cost_estimate=cost(8 * rows * width * width, 15e6),
        name="attention_back",
    )(gatt, gathered, q, k, v, ps, plong)


def weight_back_body(
    pos, gatt, gatt_other, c, c_other, d, d_other, xs, xl, xs_other, xl_other, sums_own, sums_other,
    o0, o1, o2, o3,
    x_t, c_t, grad, sums,
):
    step = pl.program_id(0)
    rows, width = c.shape
    cols = gatt.shape[1]
    each = width // SHARDS
    mine = CHIPS * each
    on_first = pos[2] == 0
    at_cols = pl.ds(pl.multiple_of(step * cols, cols), cols)

    def take(target, first, source):
        turned = source[...].T
        for i in range(CHIPS):
            low = 2 * i * each
            target[i * each : (i + 1) * each, first : first + turned.shape[1]] = jnp.where(
                on_first, turned[low : low + each], turned[low + each : low + 2 * each]
            )

    @pl.when(step == 0)
    def _():
        first = 0
        for source in (xs, xl, xs_other, xl_other):
            take(x_t, first, source)
            first += source.shape[0]
        x_t[mine:] = jnp.ones((16, 2 * rows), BF16)
        take(c_t, 0, c)
        take(c_t, rows, c_other)
        sums[...] = sums_own[...] + sums_other[...]

    def hand_out(value, at):
        n = value.shape[0] // CHIPS
        grad[:, :n] = value.reshape(CHIPS, n, cols)
        for along, out in enumerate((o0, o1, o2, o3)):
            for e in range(RING):
                x0, z0 = (pos[0] + along) & (RING - 1), (pos[1] + e) & (RING - 1)
                x1, z1 = (pos[0] + e) & (RING - 1), (pos[1] + along) & (RING - 1)
                out[e, at : at + n] = grad[jnp.where(on_first, x0 * RING + z0, x1 * RING + z1), :n]

    both = jnp.concatenate([gatt[...], gatt_other[...]], axis=0)
    hand_out(nn(c_t[...], both).astype(BF16), 3 * each)
    for i in range(3):
        both = jnp.concatenate([d[i], d_other[i]], axis=0)
        total = nn(x_t[...], both)
        hand_out(total[:mine].astype(BF16), i * each)
        if i != 1:
            at = QB if i == 0 else VB
            sums[at : at + 1, at_cols] = total[mine : mine + 1]
    for out in (o0, o1, o2, o3):
        out[:, 4 * each :] = jnp.zeros((RING, 8, cols), BF16)

    @pl.when(step == pl.num_programs(0) - 1)
    def _():
        owned = spread(SHARDS, width)
        rest = column_rest(cols, width, each)
        line = jnp.zeros((SHARDS, cols), F32)
        for i in range(8):
            put = (iota(rest.shape, 0) == rest + i * each).astype(BF16)
            line += nt(jnp.where(owned, sums[i : i + 1], 0.0).astype(BF16), put)
        parts = RING
        place = width * parts // SHARDS
        wide_owned = spread(SHARDS // parts, width)
        put = (iota((cols, width), 0) == column_rest(cols, width, place)).astype(BF16)
        wide = jnp.concatenate(
            [nt(jnp.where(wide_owned, sums[8 + j : 9 + j], 0.0).astype(BF16), put) for j in range(parts)], axis=0
        )
        small = jnp.concatenate([line[:, None], wide[:, None], jnp.zeros((SHARDS, 6, cols), F32)], axis=1)
        small = small.reshape(CHIPS, 2, 8, cols)
        small = jnp.where(on_first, small[:, 0], small[:, 1])
        hand_out(small.reshape(CHIPS * 8, cols).astype(BF16), 4 * each)


def weight_back(pos, gatt, c, d, xs, xl, sums, others):
    gatt_other, c_other, d_other, xs_other, xl_other, sums_other = others
    rows, width = gatt.shape
    each = width // SHARDS
    step = 256
    cols = pl.BlockSpec((rows, step), lambda g, *_: (0, g))
    three = pl.BlockSpec((3, rows, step), lambda g, *_: (0, 0, g))
    out = pl.BlockSpec((RING, 4 * each + 8, step), lambda g, *_: (0, 0, g))
    return pl.pallas_call(
        weight_back_body,
        grid_spec=pltpu.PrefetchScalarGridSpec(
            num_scalar_prefetch=1,
            grid=(width // step,),
            in_specs=[
                cols, cols, whole(rows, width), whole(rows, width), three, three,
                whole(*xs.shape), whole(*xl.shape), whole(*xs.shape), whole(*xl.shape),
                whole(16, width), whole(16, width),
            ],
            out_specs=[out] * RING,
            scratch_shapes=[
                pltpu.VMEM((width // 2 + 16, 2 * rows), BF16), pltpu.VMEM((width // 2, 2 * rows), BF16),
                pltpu.VMEM((CHIPS, each, step), BF16), pltpu.VMEM((16, width), F32),
            ],
        ),
        out_shape=[jax.ShapeDtypeStruct((RING, 4 * each + 8, width), BF16)] * RING,
        compiler_params=params(BACK_MIB),
        cost_estimate=cost(8 * rows * width * width, 12e6),
        name="weight_back",
    )(pos, gatt, gatt_other, c, c_other, d, d_other, xs, xl, xs_other, xl_other, sums, sums_other)


def input_back_body(dims, gfs, d, wq, wk, wv, gs_o, gl_o, total):
    step = pl.program_id(0)
    short_rows, width, cols = dims[0], gfs.shape[1], d.shape[2]
    part = (
        nt(d[0], wq[...].reshape(width, cols))
        + nt(d[1], wk[...].reshape(width, cols))
        + nt(d[2], wv[...].reshape(width, cols))
    )

    @pl.when(step == 0)
    def _():
        total[...] = gfs[...] + part

    @pl.when(step > 0)
    def _():
        total[...] += part

    @pl.when(step == pl.num_programs(0) - 1)
    def _():
        gs_o[...] = total[:short_rows]
        gl_o[...] = total[short_rows:]


def input_back(gfs, d, gathered, dims):
    rows, width = gfs.shape
    each = width // SHARDS
    step = 256
    short_rows = dims[0]
    slab = lambda i: pl.BlockSpec((SHARDS, each, step), lambda g: (0, i, g))
    return pl.pallas_call(
        functools.partial(input_back_body, dims),
        grid=(width // step,),
        in_specs=[whole(rows, width), pl.BlockSpec((3, rows, step), lambda g: (0, 0, g)), slab(0), slab(1), slab(2)],
        out_specs=[whole(short_rows, width), whole(rows - short_rows, width)],
        scratch_shapes=[pltpu.VMEM((rows, width), F32)],
        out_shape=[
            jax.ShapeDtypeStruct((short_rows, width), F32),
            jax.ShapeDtypeStruct((rows - short_rows, width), F32),
        ],
        compiler_params=params(16),
        cost_estimate=cost(6 * rows * width * width, 12e6),
        name="input_back",
    )(gfs, d, gathered, gathered, gathered)


def pair_sum(keep, got):
    parts = []
    for d in range(RING):
        at = slice(d * RING, (d + 1) * RING)
        parts.append((keep[at].astype(F32) + got[at].astype(F32)).astype(BF16))
    return parts


def four_sum(own, left, right, far):
    return (own.astype(F32) + far.astype(F32)) + (left.astype(F32) + right.astype(F32))


def turn(delta, stage):
    moves = []
    for x in range(RING):
        for z in range(RING):
            for core in range(2):
                to_x, to_z = x, z
                if (core == 0) == (stage == 0):
                    to_x = (x + delta) % RING
                else:
                    to_z = (z + delta) % RING
                moves.append(((x * RING + z) * 2 + core, (to_x * RING + to_z) * 2 + core))
    return moves


def swap_cores(v):
    return lax.ppermute(v, "shard", [(i, i ^ 1) for i in range(SHARDS)])


def around(v, stage):
    return tuple(lax.ppermute(v[d] if isinstance(v, (list, tuple)) else v, "shard", turn(d, stage)) for d in (1, 3, 2))


def both_cores(pieces):
    return (*pieces, *(swap_cores(p) for p in pieces))


def across_replicas(v):
    return tuple(
        lax.ppermute(v[d] if isinstance(v, (list, tuple)) else v, "rep", [(i, (i + d) % RING) for i in range(RING)])
        for d in (1, 3, 2)
    )


def second_turn(parts):
    own = four_sum(parts[0], *around(parts, 1)).astype(BF16)
    return own, *across_replicas(own)


def first_sums(own, left, right, far):
    return [four_sum(own[d], left[d], right[d], far[d]).astype(BF16) for d in range(RING)]


def far_pieces(keep, got, replica):
    at, share = slice(2 * RING, 3 * RING), keep.shape[1] // RING
    pieces = []
    for d in range(RING):
        low = ((replica + d) % RING) * share
        cut = lambda v: lax.dynamic_slice_in_dim(v[at], low, share, axis=1).astype(F32)
        pieces.append((cut(keep) + cut(got)).astype(BF16))
    return pieces


def first_sums_shared(own, left, right, far, replica):
    share = far.shape[1]
    sums = []
    for d in range(RING):
        near = own[d].astype(F32) + (left[d].astype(F32) + right[d].astype(F32))
        near = near.reshape(RING, share, *near.shape[1:])
        mine = lax.broadcasted_iota(jnp.int32, near.shape, 0) == replica
        total = near + jnp.where(mine, far[d].astype(F32)[None], 0.0)
        sums.append(total.reshape(own.shape[1:]).astype(BF16))
    return sums


def replica_sum(own, left, right, far, at):
    return (own[at].astype(F32) + far[at].astype(F32)) + (left[at].astype(F32) + right[at].astype(F32))


def finish_attention_body(own, left, right, far, wqkv_o, wo_o, *vector_os):
    each, width = wo_o.shape
    for j in range(wqkv_o.shape[1] // width):
        at = slice(j * each, (j + 1) * each)
        wqkv_o[:, j * width : (j + 1) * width] = replica_sum(own, left, right, far, at)
    wo_o[...] = replica_sum(own, left, right, far, slice(3 * each, 4 * each))
    last = replica_sum(own, left, right, far, slice(4 * each, 4 * each + 8))[:, width - 256 :]
    for i, o in enumerate(vector_os[:-1]):
        o[...] = last[0:1, i * each : (i + 1) * each]
    o = vector_os[-1]
    o[...] = last[1:2, : o.shape[1]]


def finish_attention(arrays, tall):
    width = arrays[0].shape[1]
    each = width // SHARDS
    return pl.pallas_call(
        finish_attention_body,
        out_shape=[
            jax.ShapeDtypeStruct((each, 3 * width), F32),
            jax.ShapeDtypeStruct((each, width), F32),
            *[jax.ShapeDtypeStruct((1, each), F32)] * 8,
            jax.ShapeDtypeStruct((1, tall), F32),
        ],
        compiler_params=params(4),
        name="finish_attention",
    )(*arrays)


def finish_feed_body(own, left, right, far, up_o, down_o):
    parts = own.shape[0] // 2
    each, width = own.shape[1:]
    for j in range(parts):
        down_o[j * each : (j + 1) * each] = replica_sum(own, left, right, far, j)
        up_o[:, j * width : (j + 1) * width] = replica_sum(own, left, right, far, parts + j)


def finish_feed(arrays, each, inner, tall):
    width = arrays[0].shape[2]
    return pl.pallas_call(
        finish_feed_body,
        out_shape=[jax.ShapeDtypeStruct((each, inner), F32), jax.ShapeDtypeStruct((tall, width), F32)],
        compiler_params=params(4),
        name="finish_feed",
    )(*arrays)


def on_device(
    short_tokens, long_tokens, short_lengths, long_lengths, short_cotangent, long_cotangent,
    input_weight, query_bias, value_bias, output_weight, output_bias, first_gain, first_shift,
    up_weight, up_bias, down_weight, down_bias, second_gain, second_shift,
):
    short_count, short_length, width = short_tokens.shape
    long_count, long_length, _ = long_tokens.shape
    dims = (short_count * short_length, long_count, long_length, short_length)
    each, inner, tall = width // SHARDS, up_weight.shape[1], down_weight.shape[0]
    xs, xl = short_tokens.reshape(-1, width), long_tokens.reshape(-1, width)
    cs, cl = short_cotangent.reshape(-1, width), long_cotangent.reshape(-1, width)
    index = lax.axis_index("shard")
    pos = jnp.stack([index // 8, (index // 2) % 4, index % 2]).astype(jnp.int32)

    packed = pack(
        input_weight, output_weight, up_weight, down_weight,
        (query_bias, value_bias, output_bias, first_gain, first_shift, down_bias, second_gain, second_shift),
        up_bias,
    )
    *near, xs_other, xl_other = lax.optimization_barrier(
        (packed, *around(packed, 1), swap_cores(xs), swap_cores(xl))
    )
    cut = 4 * each + 8
    near_a = jnp.stack([n[:cut] for n in near])
    near_f = jnp.stack([n[cut:].reshape(-1, each, width) for n in near])
    around_a = around(near_a, 0)
    far_f = around(near_f, 0)
    pieces_a = both_cores((near_a, *around_a))
    xs, near_f = lax.optimization_barrier((xs, near_f))
    q, k, v, c, ps, plong, unit1, inv1, vecs, ub, gathered_a = attention_forward(
        short_lengths, long_lengths, pos, xs, xl, pieces_a, inner, dims
    )
    unit1, *far_f = lax.optimization_barrier((unit1, *far_f))
    ub, c_other = lax.optimization_barrier((ub, swap_cores(c)))
    keep_f, give_f, out_s, out_l, gfs, gatt, sums = feed(
        short_lengths, long_lengths, pos, unit1, cs, cl, inv1, ub, vecs, both_cores((near_f, *far_f)), dims
    )
    grads = attention_back(gatt, gathered_a, q, k, v, ps, plong, dims)
    got_f, gatt_other, sums_other, grads = lax.optimization_barrier(
        (swap_cores(give_f), swap_cores(gatt), swap_cores(sums), grads)
    )
    grads_other = swap_cores(grads)
    replica = lax.axis_index("rep")
    parts_f = pair_sum(keep_f, got_f)
    shares = far_pieces(keep_f, got_f, replica)
    parts_f[2] = shares[0]
    grads_other, *parts_f = lax.optimization_barrier((grads_other, *parts_f, *shares[1:]))
    parts_f, shares = parts_f[:RING], [parts_f[2], *parts_f[RING:]]
    near_sums = [lax.ppermute(parts_f[d], "shard", turn(d, 0)) for d in (1, 3)]
    far_sum = four_sum(shares[0], *across_replicas(shares)).astype(BF16)
    others = (gatt_other, c_other, grads_other, xs_other, xl_other, sums_other)
    parts_a = weight_back(pos, gatt, c, grads, xs, xl, sums, others)
    gfs, *both = lax.optimization_barrier((gfs, *parts_a, *near_sums, far_sum))
    parts_a, near_sums, far_sum = both[:RING], both[RING:-1], both[-1]
    far_f = lax.ppermute(far_sum, "shard", turn(2, 0))
    around_a = around(parts_a, 0)
    grad_s, grad_l = input_back(gfs, grads, gathered_a, dims)
    grad_s, *around_a = lax.optimization_barrier((grad_s, *around_a))
    up, down = finish_feed(second_turn(first_sums_shared(parts_f[0], *near_sums, far_f, replica)), each, inner, tall)
    w_in, w_out, *vectors = finish_attention(second_turn(first_sums(parts_a[0], *around_a)), tall)
    vectors = [x.reshape(-1) for x in vectors]
    return (
        out_s.reshape(short_tokens.shape), out_l.reshape(long_tokens.shape),
        grad_s.reshape(short_tokens.shape), grad_l.reshape(long_tokens.shape),
        w_in, vectors[QB], vectors[VB], w_out, vectors[OB], vectors[G1], vectors[S1],
        up, vectors[8], down, vectors[DB], vectors[G2], vectors[S2],
    )


def solution(mesh):
    rows, flat = P(("rep", "shard"), None, None), P("shard")
    tall = P("shard", None)
    return jax.shard_map(
        on_device,
        mesh=mesh,
        in_specs=(
            rows, rows, P(("rep", "shard")), P(("rep", "shard")), rows, rows,
            tall, flat, flat, tall, flat, flat, flat, tall, flat, tall, flat, flat, flat,
        ),
        out_specs=(
            rows, rows, rows, rows,
            tall, flat, flat, tall, flat, flat, flat, tall, flat, tall, flat, flat, flat,
        ),
        check_vma=False,
    )
```

```python
import functools

import jax
import jax.numpy as jnp
from jax import lax
from jax.experimental import pallas as pl
from jax.experimental.pallas import tpu as pltpu
from jax.sharding import PartitionSpec as P

F32 = jnp.float32
BF16 = jnp.bfloat16
HEAD_DIM = 64
PAIR = 128
EPSILON = 1e-06
BACK_MIB = 58
QB, VB, OB, G1, S1, DB, G2, S2 = range(8)
RING = 4
CHIPS = RING * RING
SHARDS = 2 * CHIPS


def nn(a, b):
    return lax.dot_general(a, b, (((1,), (0,)), ((), ())), preferred_element_type=F32)


def nt(a, b):
    return lax.dot_general(a, b, (((1,), (1,)), ((), ())), preferred_element_type=F32)


def tn(a, b):
    return lax.dot_general(a, b, (((0,), (0,)), ((), ())), preferred_element_type=F32)


def iota(shape, dim):
    return lax.broadcasted_iota(jnp.int32, shape, dim)


def row_of(ref, i):
    return ref[i : i + 1, :].astype(F32)


def whole(*shape):
    return pl.BlockSpec(shape, lambda g, *_: (0,) * len(shape))


def params(mebibytes):
    return pltpu.CompilerParams(vmem_limit_bytes=mebibytes * 1024 * 1024)


def cost(flops, moved):
    return pl.CostEstimate(flops=int(flops), bytes_accessed=int(moved), transcendentals=0)


def places(pos, x, z):
    along_x, along_z = (x - pos[0]) & (RING - 1), (z - pos[1]) & (RING - 1)
    return along_x * RING + along_z, along_z * RING + along_x


def deal(keep, give, pos, value, at, each):
    first = pos[2] == 0
    for x in range(RING):
        for z in range(RING):
            p0, p1 = places(pos, x, z)
            low = 2 * (x * RING + z) * each
            even, odd = value[low : low + each], value[low + each : low + 2 * each]
            keep[jnp.where(first, p0, p1), at] = jnp.where(first, even, odd)
            give[jnp.where(first, p1, p0), at] = jnp.where(first, odd, even)


def deal_apart(keep, gives, spare, pos, value, at, each):
    first = pos[2] == 0
    for x in range(RING):
        for z in range(RING):
            p0, p1 = places(pos, x, z)
            low = 2 * (x * RING + z) * each
            even, odd = value[low : low + each], value[low + each : low + 2 * each]
            keep[jnp.where(first, p0, p1), at] = jnp.where(first, even, odd)
            spare[x * RING + z, :each] = jnp.where(first, odd, even)
    for a, give in enumerate(gives):
        for b in range(RING):
            xa, zb = (pos[0] + a) & (RING - 1), (pos[1] + b) & (RING - 1)
            xb, za = (pos[0] + b) & (RING - 1), (pos[1] + a) & (RING - 1)
            give[b, at] = spare[jnp.where(first, xb * RING + za, xa * RING + zb), :each]


def spread(owners, width):
    each = width // owners
    at = iota((owners, width), 1)
    low = iota((owners, width), 0) * each
    return (at >= low) & (at < low + each)


def column_rest(rows, width, each):
    at = iota((1, width), 1)
    return jnp.broadcast_to(at - (at // each) * each, (rows, width))


def two_heads(pair):
    low_half = iota(pair.shape, 1) < HEAD_DIM
    zero = jnp.zeros_like(pair)
    return jnp.concatenate([jnp.where(low_half, pair, zero), jnp.where(low_half, zero, pair)], axis=0)


def own_lanes(stack):
    half = stack.shape[0] // 2
    return jnp.where(iota((half, stack.shape[1]), 1) < HEAD_DIM, stack[:half], stack[half:])


def normalized(hidden):
    center = hidden - jnp.mean(hidden, axis=-1, keepdims=True)
    spread_of = jnp.mean(center * center, axis=-1, keepdims=True)
    inverse = lax.rsqrt(spread_of + EPSILON)
    return center * inverse, inverse


def norm_back(scaled, unit, inverse):
    return inverse * (
        scaled
        - jnp.mean(scaled, axis=-1, keepdims=True)
        - unit * jnp.mean(scaled * unit, axis=-1, keepdims=True)
    )


def segments(dims):
    short_rows, long_count, long_length, _ = dims
    return [(0, short_rows, None)] + [
        (short_rows + i * long_length, long_length, i) for i in range(long_count)
    ]


def key_bias(slen, llen, short_length, rows, long_at):
    key = iota((rows, rows), 0)
    if long_at is not None:
        return jnp.where(key < llen[long_at], 0.0, -1e9).astype(F32)
    query = iota((rows, rows), 1)
    keep = jnp.zeros((rows, rows), jnp.bool_)
    for p in range(rows // short_length):
        low, high = p * short_length, (p + 1) * short_length
        keep = keep | ((key >= low) & (key < low + slen[p]) & (query >= low) & (query < high))
    return jnp.where(keep, 0.0, -1e9).astype(F32)


def valid_rows(slen, llen, dims):
    short_rows, long_count, long_length, short_length = dims
    parts = []
    at = iota((short_length, 1), 0)
    for p in range(short_rows // short_length):
        parts.append((at < slen[p]).astype(F32))
    at = iota((long_length, 1), 0)
    for p in range(long_count):
        parts.append((at < llen[p]).astype(F32))
    return jnp.concatenate(parts, axis=0)


def slabs_of(out, base, source, each, width):
    for j in range(source.shape[1] // width):
        out[base + j * each : base + (j + 1) * each] = source[:, j * width : (j + 1) * width]
    return base + source.shape[1] // width * each


def pack_body(wqkv, wo, wup, wdown, *rest):
    vectors, out = rest[:-1], rest[-1]
    each, width = wo.shape
    base = slabs_of(out, 0, wqkv, each, width)
    base = slabs_of(out, base, wo, each, width)
    out[base : base + 8] = jnp.zeros((8, width), BF16)
    for i, v in enumerate(vectors[:-1]):
        out[base : base + 1, i * each : (i + 1) * each] = v[...]
    out[base + 1 : base + 2, : vectors[-1].shape[1]] = vectors[-1][...]
    base = slabs_of(out, base + 8, wup, each, width)
    out[base:] = wdown[...]


def pack(wqkv, wo, wup, wdown, vectors, ub):
    each, width = wo.shape
    rows = wqkv.shape[1] // width * each + each + 8 + 2 * wdown.shape[0]
    return pl.pallas_call(
        pack_body,
        out_shape=jax.ShapeDtypeStruct((rows, width), BF16),
        compiler_params=params(58),
        name="pack",
    )(wqkv, wo, wup, wdown, *[v[None] for v in vectors], ub[None])


STEPS = (0, -1, 1, 2)


def gathered_at(pos, other, k, i):
    core = pos[2] ^ other
    x0, z0 = (pos[0] + STEPS[k]) & (RING - 1), (pos[1] + STEPS[i]) & (RING - 1)
    x1, z1 = (pos[0] + STEPS[i]) & (RING - 1), (pos[1] + STEPS[k]) & (RING - 1)
    return jnp.where(core == 0, (x0 * RING + z0) * 2, (x1 * RING + z1) * 2 + 1)


def arrivals(pos, pieces, target, sems, at):
    copies = []
    for other in range(2):
        for k in range(RING):
            for i in range(RING):
                n = (other * RING + k) * RING + i
                copies.append(
                    pltpu.make_async_copy(
                        pieces[other * RING + k].at[i, at], target.at[gathered_at(pos, other, k, i), at], sems.at[n]
                    )
                )
    return copies


def attention_forward_body(
    dims, slen, llen, pos, xs, xl, p0, p1, p2, p3, p4, p5, p6, p7,
    q_o, k_o, v_o, c_o, ps_o, pl_o, n_o, r_o, vecs_o, ub_o, gathered_o,
    x_all, total, wo_all, gathered, sems, out_sem,
):
    step = pl.program_id(0)
    short_rows, width = dims[0], x_all.shape[1]
    cols = q_o.shape[1]
    each = width // SHARDS
    keep_all = pltpu.make_async_copy(gathered, gathered_o, out_sem)

    @pl.when(step == 0)
    def _():
        copies = arrivals(pos, (p0, p1, p2, p3, p4, p5, p6, p7), gathered, sems, slice(None))
        for copy in copies:
            copy.start()
        x_all[:short_rows, :] = xs[...]
        x_all[short_rows:, :] = xl[...]
        total[...] = jnp.zeros_like(total)
        for copy in copies:
            copy.wait()
        keep_all.start()
        wo_all[...] = gathered[:, 3 * each : 4 * each].reshape(width, width)
        packed = gathered[:, 4 * each :]
        line = packed[:, 0, : 8 * each + 64]
        rest = column_rest(line.shape[1], width, each)
        mine = spread(SHARDS, width)
        for i in range(8):
            pick = (iota(rest.shape, 0) == rest + i * each).astype(BF16)
            row = jnp.sum(jnp.where(mine, nn(line, pick), 0.0), axis=0, keepdims=True)
            vecs_o[i : i + 1] = row.astype(BF16)
        inner = ub_o.shape[1]
        line = packed[:, 1, :128]
        pick = (iota((128, inner), 0) == column_rest(128, inner, inner // SHARDS)).astype(BF16)
        row = jnp.sum(jnp.where(spread(SHARDS, inner), nn(line, pick), 0.0), axis=0, keepdims=True)
        ub_o[...] = row.astype(BF16)

    x = x_all[...]
    at_cols = pl.ds(pl.multiple_of(step * cols, cols), cols)
    wq, wk, wv = (gathered[:, i * each : (i + 1) * each, at_cols].reshape(width, cols) for i in range(3))
    q_o[...] = (nn(x, wq) + vecs_o[QB : QB + 1, at_cols].astype(F32)).astype(BF16)
    k_o[...] = nn(x, wk).astype(BF16)
    v_o[...] = (nn(x, wv) + vecs_o[VB : VB + 1, at_cols].astype(F32)).astype(BF16)
    for first, rows, long_at in segments(dims):
        bias = key_bias(slen, llen, dims[3], rows, long_at)
        at = slice(first, first + rows)
        for pair in range(cols // PAIR):
            lanes = slice(pair * PAIR, (pair + 1) * PAIR)
            q = q_o[at, lanes] * jnp.asarray(HEAD_DIM**-0.5, BF16)
            scores = nt(two_heads(k_o[at, lanes]), q)
            probs = []
            for h in range(2):
                s = scores[h * rows : (h + 1) * rows] + bias
                e = jnp.exp(s - jnp.max(s, axis=0, keepdims=True))
                probs.append((e * (1.0 / jnp.sum(e, axis=0, keepdims=True))).astype(BF16))
            probs = jnp.concatenate(probs, axis=0)
            if long_at is None:
                ps_o[pair] = probs
            else:
                pl_o[long_at, pair] = probs
            c_o[at, lanes] = tn(probs, two_heads(v_o[at, lanes])).astype(BF16)
    total[...] += nn(c_o[...], wo_all[at_cols, :])

    @pl.when(step == pl.num_programs(0) - 1)
    def _():
        h = x_all[...].astype(F32) + (total[...] + row_of(vecs_o, OB))
        unit, inverse = normalized(h)
        n_o[...] = unit
        r_o[...] = inverse
        keep_all.wait()


def attention_forward(slen, llen, pos, xs, xl, pieces, inner, dims):
    rows, width = xs.shape[0] + xl.shape[0], xs.shape[1]
    short_rows, long_count, long_length, _ = dims
    step = 256
    steps, pairs = width // step, width // PAIR
    per = step // PAIR
    each_all = pieces[0].shape[1]
    cols = pl.BlockSpec((rows, step), lambda g, *_: (0, g))
    return pl.pallas_call(
        functools.partial(attention_forward_body, dims),
        grid_spec=pltpu.PrefetchScalarGridSpec(
            num_scalar_prefetch=3,
            grid=(steps,),
            in_specs=[
                whole(*xs.shape), whole(*xl.shape), *[pl.BlockSpec(memory_space=pl.ANY)] * 8,
            ],
            out_specs=[
                cols, cols, cols, cols,
                pl.BlockSpec((per, 2 * short_rows, short_rows), lambda g, *_: (g, 0, 0)),
                pl.BlockSpec((long_count, per, 2 * long_length, long_length), lambda g, *_: (0, g, 0, 0)),
                whole(rows, width), whole(rows, 1), whole(8, width), whole(1, inner),
                pl.BlockSpec(memory_space=pl.ANY),
            ],
            scratch_shapes=[
                pltpu.VMEM((rows, width), BF16), pltpu.VMEM((rows, width), F32), pltpu.VMEM((width, width), BF16),
                pltpu.VMEM((SHARDS, each_all, width), BF16), pltpu.SemaphoreType.DMA((SHARDS,)),
                pltpu.SemaphoreType.DMA(()),
            ],
        ),
        out_shape=[
            *[jax.ShapeDtypeStruct((rows, width), BF16)] * 4,
            jax.ShapeDtypeStruct((pairs, 2 * short_rows, short_rows), BF16),
            jax.ShapeDtypeStruct((long_count, pairs, 2 * long_length, long_length), BF16),
            jax.ShapeDtypeStruct((rows, width), F32),
            jax.ShapeDtypeStruct((rows, 1), F32),
            jax.ShapeDtypeStruct((8, width), BF16),
            jax.ShapeDtypeStruct((1, inner), BF16),
            jax.ShapeDtypeStruct((SHARDS, each_all, width), BF16),
        ],
        compiler_params=params(58),
        cost_estimate=cost(8 * rows * width * width, 20e6),
        name="attention_forward",
    )(slen, llen, pos, xs, xl, *pieces)


HBM = pl.BlockSpec(memory_space=pl.ANY)
ON_CHIP = pl.BlockSpec(memory_space=pltpu.VMEM)
SCALARS = pl.BlockSpec(memory_space=pltpu.SMEM)


class Copies:
    def __init__(self, sems):
        self.sems, self.used, self.open = sems, 0, []

    def start(self, source, target):
        copy = pltpu.make_async_copy(source, target, self.sems.at[self.used])
        self.used += 1
        copy.start()
        return copy

    def send(self, source, target):
        self.open.append(self.start(source, target))

    def finish(self):
        for copy in self.open:
            copy.wait()


def feed_body(
    dims, slen, llen, pos, unit1, cot_s, cot_l, inv1, ub, vecs, p0, p1, p2, p3, p4, p5, p6, p7,
    keep, give, outs_o, outl_o, gfs_o, gatt_o, sums_o, dub_o,
    wup, wdown, unit_v, cot_v, low_v, low_t, hidden, gelu_v, grad_v, gffn, out_v, gatt, valid_v,
    keep_dv, give_dv, keep_uv, give_uv, sems, piece_sems, down_sems, up_sems,
):
    short_rows = dims[0]
    rows, width = low_v.shape
    parts, block = hidden.shape[0], hidden.shape[2]
    each, tall = width // SHARDS, block * parts // SHARDS
    owners, lanes, tile = SHARDS // parts, 256, 128
    copies = Copies(sems)
    pieces = (p0, p1, p2, p3, p4, p5, p6, p7)
    unit_here = copies.start(unit1, unit_v)
    groups = [[], [], []]
    for other in range(2):
        for k in range(RING):
            for i in range(RING):
                n = (other * RING + k) * RING + i
                at = gathered_at(pos, other, k, i)
                source = pieces[other * RING + k]
                half = parts // 2
                targets = (wup.at[:half, at], wup.at[half:, at], wdown.at[at])
                sources = (source.at[i, :half], source.at[i, half:parts], source.at[i, parts:])
                for group, sem, src, target in zip(groups, range(3), sources, targets):
                    group.append(pltpu.make_async_copy(src, target, piece_sems.at[sem, n]))
    for copy in groups[0]:
        copy.start()
    valid_v[...] = valid_rows(slen, llen, dims)
    grad_v[...] = jnp.zeros_like(grad_v)
    unit_here.wait()

    @pl.loop(0, rows // tile)
    def _(r):
        at = pl.ds(pl.multiple_of(r * tile, tile), tile)
        low_v[at] = (unit_v[at] * row_of(vecs, G1) + row_of(vecs, S1)).astype(BF16)

    @pl.loop(0, parts)
    def _(j):
        for n in range(2):

            @pl.when(j == n * (parts // 2))
            def _():
                for copy in groups[n]:
                    copy.wait()
                for copy in groups[n + 1]:
                    copy.start()

        bias = ub[:, pl.ds(pl.multiple_of(j * block, block), block)].astype(F32)
        pre = nn(low_v[...], wup[j].reshape(width, block)) + bias
        cdf = 0.5 + 0.5 * lax.erf(pre * (0.5**0.5))
        density = jnp.exp(-0.5 * pre * pre) * (0.5 / jnp.pi) ** 0.5
        hidden[j] = (pre * cdf).astype(BF16)
        gelu_v[j] = (cdf + pre * density).astype(BF16)

    for copy in groups[2]:
        copy.wait()
    cots_here = copies.start(cot_s, cot_v.at[:short_rows]), copies.start(cot_l, cot_v.at[short_rows:])

    @pl.loop(0, parts)
    def _(j):
        grad_v[...] += nn(hidden[j], wdown[pl.ds(j * owners, owners)].reshape(block, width))

    for copy in cots_here:
        copy.wait()
    sums_o[...] = jnp.zeros_like(sums_o)

    @pl.loop(0, rows // tile)
    def _(r):
        at = pl.ds(pl.multiple_of(r * tile, tile), tile)
        first = unit_v[at] * row_of(vecs, G1) + row_of(vecs, S1)
        unit, inverse = normalized(first + (grad_v[at] + row_of(vecs, DB)))
        valid = valid_v[at]
        out_v[at] = ((unit * row_of(vecs, G2) + row_of(vecs, S2)) * valid).astype(BF16)
        cot = cot_v[at].astype(F32) * valid
        back = norm_back(cot * row_of(vecs, G2), unit, inverse)
        grad_v[at] = back
        low_back = back.astype(BF16)
        gffn[at] = low_back
        sums_o[DB : DB + 1] += jnp.sum(low_back.astype(F32), axis=0, keepdims=True)
        sums_o[G2 : G2 + 1] += jnp.sum(cot * unit, axis=0, keepdims=True)
        sums_o[S2 : S2 + 1] += jnp.sum(cot, axis=0, keepdims=True)

    copies.send(out_v.at[:short_rows], outs_o)
    copies.send(out_v.at[short_rows:], outl_o)
    on_first = pos[2] == 0

    def down_copies(at, p0, p1):
        return (
            pltpu.make_async_copy(keep_dv.at[at], keep.at[jnp.where(on_first, p0, p1), :parts], down_sems.at[0, at]),
            pltpu.make_async_copy(give_dv.at[at], give.at[jnp.where(on_first, p1, p0), :parts], down_sems.at[1, at]),
        )

    @pl.loop(0, RING)
    def _(x):
        grad = tn(hidden[x], gffn[...]).astype(BF16)
        for z in range(RING):
            place = x * RING + z
            even, odd = grad[2 * z * tall : (2 * z + 1) * tall], grad[(2 * z + 1) * tall : (2 * z + 2) * tall]
            keep_dv[place] = jnp.where(on_first, even, odd).reshape(parts, each, width)
            give_dv[place] = jnp.where(on_first, odd, even).reshape(parts, each, width)
            for copy in down_copies(place, *places(pos, x, z)):
                copy.start()

    def up_copies(j):
        return (
            pltpu.make_async_copy(keep_uv.at[j], keep.at[:, parts + j], up_sems.at[0, j]),
            pltpu.make_async_copy(give_uv.at[j], give.at[:, parts + j], up_sems.at[1, j]),
        )

    low_t[:width] = low_v[...].T
    low_t[width:] = jnp.ones((16, rows), BF16)

    @pl.loop(0, parts)
    def _(j):
        weight = wdown[pl.ds(j * owners, owners)].reshape(block, width)
        up = (nt(gffn[...], weight) * gelu_v[j].astype(F32)).astype(BF16)
        hidden[j] = up
        grad = nn(low_t[...], hidden[j])
        dub_o[:, pl.ds(pl.multiple_of(j * block, block), block)] = grad[width : width + 1]
        deal(keep_uv.at[j], give_uv.at[j], pos, grad[:width].astype(BF16), slice(None), each)
        for copy in up_copies(j):
            copy.start()

    @pl.loop(0, parts)
    def _(j):
        grad_v[...] += nt(hidden[j], wup[j].reshape(width, block))

    @pl.loop(0, rows // tile)
    def _(r):
        at = pl.ds(pl.multiple_of(r * tile, tile), tile)
        grad, unit = grad_v[at], unit_v[at]
        back = norm_back(grad * row_of(vecs, G1), unit, inv1[at])
        grad_v[at] = back
        low_back = back.astype(BF16)
        gatt[at] = low_back
        sums_o[OB : OB + 1] += jnp.sum(low_back.astype(F32), axis=0, keepdims=True)
        sums_o[G1 : G1 + 1] += jnp.sum(grad * unit, axis=0, keepdims=True)
        sums_o[S1 : S1 + 1] += jnp.sum(grad, axis=0, keepdims=True)

    copies.send(gatt, gatt_o)
    copies.send(grad_v, gfs_o)
    for at in range(CHIPS):
        for copy in down_copies(at, at, at):
            copy.wait()
    for j in range(parts):
        for copy in up_copies(j):
            copy.wait()
    copies.finish()


def feed(slen, llen, pos, unit1, cot_s, cot_l, inv1, ub, vecs, pieces, dims):
    rows, width = unit1.shape
    inner = ub.shape[1]
    parts = RING
    block, tall, each = inner // parts, inner // SHARDS, width // SHARDS
    down, up = (CHIPS, parts, each, width), (parts, CHIPS, each, width)
    return pl.pallas_call(
        functools.partial(feed_body, dims),
        in_specs=[SCALARS] * 3 + [HBM] * 3 + [ON_CHIP] * 3 + [HBM] * 8,
        out_specs=[HBM] * 6 + [ON_CHIP] * 2,
        scratch_shapes=[
            pltpu.VMEM((parts, SHARDS, each, width), BF16), pltpu.VMEM((SHARDS, parts, each, width), BF16),
            pltpu.VMEM((rows, width), F32), pltpu.VMEM((rows, width), BF16), pltpu.VMEM((rows, width), BF16),
            pltpu.VMEM((width + 16, rows), BF16), pltpu.VMEM((parts, rows, block), BF16),
            pltpu.VMEM((parts, rows, block), BF16), pltpu.VMEM((rows, width), F32), pltpu.VMEM((rows, width), BF16),
            pltpu.VMEM((rows, width), BF16), pltpu.VMEM((rows, width), BF16), pltpu.VMEM((rows, 1), F32),
            pltpu.VMEM(down, BF16), pltpu.VMEM(down, BF16), pltpu.VMEM(up, BF16), pltpu.VMEM(up, BF16),
            pltpu.SemaphoreType.DMA((8,)), pltpu.SemaphoreType.DMA((3, SHARDS)),
            pltpu.SemaphoreType.DMA((2, CHIPS)), pltpu.SemaphoreType.DMA((2, parts)),
        ],
        out_shape=[
            *[jax.ShapeDtypeStruct((CHIPS, 2 * parts, each, width), BF16)] * 2,
            jax.ShapeDtypeStruct(cot_s.shape, BF16),
            jax.ShapeDtypeStruct(cot_l.shape, BF16),
            jax.ShapeDtypeStruct((rows, width), F32),
            jax.ShapeDtypeStruct((rows, width), BF16),
            jax.ShapeDtypeStruct((8, width), F32),
            jax.ShapeDtypeStruct((1, inner), F32),
        ],
        compiler_params=params(58),
        cost_estimate=cost(12 * rows * width * inner, 30e6),
        name="feed",
    )(slen, llen, pos, unit1, cot_s, cot_l, inv1, ub, vecs, *pieces)


def attention_back_body(dims, gatt, wo_block, q, k, v, ps, plong, dq_o, dk_o, dv_o, gc, wo_all):
    step = pl.program_id(0)
    width, cols = gatt.shape[1], q.shape[1]
    at_cols = pl.ds(pl.multiple_of(step * cols, cols), cols)

    @pl.when(step == 0)
    def _():
        wo_all[...] = wo_block[...].reshape(width, width)

    gc[...] = nt(gatt[...], wo_all[at_cols, :]).astype(BF16)
    scale = HEAD_DIM**-0.5
    for first, rows, long_at in segments(dims):
        at = slice(first, first + rows)
        for pair in range(cols // PAIR):
            lanes = slice(pair * PAIR, (pair + 1) * PAIR)
            probs = ps[pair] if long_at is None else plong[long_at, pair]
            grad = gc[at, lanes]
            dp = nt(two_heads(v[at, lanes]), grad)
            ds = []
            for h in range(2):
                half = slice(h * rows, (h + 1) * rows)
                p = probs[half].astype(F32)
                d = dp[half]
                ds.append((p * (d - jnp.sum(d * p, axis=0, keepdims=True))).astype(BF16))
            ds = jnp.concatenate(ds, axis=0)
            dv_o[at, lanes] = own_lanes(nn(probs, grad)).astype(BF16)
            dk_o[at, lanes] = (own_lanes(nn(ds, q[at, lanes])) * scale).astype(BF16)
            dq_o[at, lanes] = (tn(ds, two_heads(k[at, lanes])) * scale).astype(BF16)


def attention_back(gatt, gathered, q, k, v, ps, plong, dims):
    rows, width = gatt.shape
    short_rows, long_count, long_length, _ = dims
    step = 256
    per = step // PAIR
    cols = pl.BlockSpec((rows, step), lambda g: (0, g))
    return pl.pallas_call(
        functools.partial(attention_back_body, dims),
        grid=(width // step,),
        in_specs=[
            whole(rows, width),
            pl.BlockSpec((SHARDS, width // SHARDS, width), lambda g: (0, 3, 0)),
            cols, cols, cols,
            pl.BlockSpec((per, 2 * short_rows, short_rows), lambda g: (g, 0, 0)),
            pl.BlockSpec((long_count, per, 2 * long_length, long_length), lambda g: (0, g, 0, 0)),
        ],
        out_specs=[cols, cols, cols],
        scratch_shapes=[pltpu.VMEM((rows, step), BF16), pltpu.VMEM((width, width), BF16)],
        out_shape=[jax.ShapeDtypeStruct((rows, width), BF16)] * 3,
        compiler_params=params(BACK_MIB),
        cost_estimate=cost(8 * rows * width * width, 15e6),
        name="attention_back",
    )(gatt, gathered, q, k, v, ps, plong)


def weight_back_body(
    dims, pos, gatt_cols, c, dq, dk, dv, xs, xl, sums_f, dub,
    keep, g0, g1, g2, g3,
    x_t, c_t, sums, spare,
):
    gives = (g0, g1, g2, g3)
    step = pl.program_id(0)
    short_rows = dims[0]
    rows, width = c.shape
    cols = dq.shape[1]
    each = width // SHARDS
    at_cols = pl.ds(pl.multiple_of(step * cols, cols), cols)

    @pl.when(step == 0)
    def _():
        x_t[:width, :short_rows] = xs[...].T
        x_t[:width, short_rows:] = xl[...].T
        x_t[width:] = jnp.ones((16, rows), BF16)
        c_t[...] = c[...].T
        sums[...] = sums_f[...]

    deal_apart(keep, gives, spare, pos, nn(c_t[...], gatt_cols[...]).astype(BF16), slice(3 * each, 4 * each), each)
    for i, d in enumerate((dq, dk, dv)):
        grad = nn(x_t[...], d[...])
        deal_apart(keep, gives, spare, pos, grad[:width].astype(BF16), slice(i * each, (i + 1) * each), each)
        if i != 1:
            at = QB if i == 0 else VB
            sums[at : at + 1, at_cols] = grad[width : width + 1]
    keep[:, 4 * each :] = jnp.zeros((CHIPS, 8, cols), BF16)
    for give in gives:
        give[:, 4 * each :] = jnp.zeros((RING, 8, cols), BF16)

    @pl.when(step == pl.num_programs(0) - 1)
    def _():
        mine = spread(SHARDS, width)
        rest = column_rest(cols, width, each)
        line = jnp.zeros((SHARDS, cols), F32)
        for i in range(8):
            put = (iota(rest.shape, 0) == rest + i * each).astype(BF16)
            line += nt(jnp.where(mine, sums[i : i + 1], 0.0).astype(BF16), put)
        inner = dub.shape[1]
        put = (iota((cols, inner), 0) == column_rest(cols, inner, inner // SHARDS)).astype(BF16)
        wide = nt(jnp.where(spread(SHARDS, inner), dub[...], 0.0).astype(BF16), put)
        both = jnp.concatenate([line[:, None], wide[:, None], jnp.zeros((SHARDS, 6, cols), F32)], axis=1)
        deal_apart(keep, gives, spare, pos, both.reshape(SHARDS * 8, cols).astype(BF16), slice(4 * each, 4 * each + 8), 8)


def weight_back(pos, gatt, c, dq, dk, dv, xs, xl, sums_f, dub, dims):
    rows, width = gatt.shape
    each = width // SHARDS
    step = 256
    cols = pl.BlockSpec((rows, step), lambda g, *_: (0, g))
    dealt = pl.BlockSpec((CHIPS, 4 * each + 8, step), lambda g, *_: (0, 0, g))
    return pl.pallas_call(
        functools.partial(weight_back_body, dims),
        grid_spec=pltpu.PrefetchScalarGridSpec(
            num_scalar_prefetch=1,
            grid=(width // step,),
            in_specs=[
                cols, whole(rows, width), cols, cols, cols,
                whole(*xs.shape), whole(*xl.shape), whole(8, width), whole(*dub.shape),
            ],
            out_specs=[dealt, *[pl.BlockSpec((RING, 4 * each + 8, step), lambda g, *_: (0, 0, g))] * RING],
            scratch_shapes=[
                pltpu.VMEM((width + 16, rows), BF16), pltpu.VMEM((width, rows), BF16), pltpu.VMEM((8, width), F32),
                pltpu.VMEM((CHIPS, each, step), BF16),
            ],
        ),
        out_shape=[
            jax.ShapeDtypeStruct((CHIPS, 4 * each + 8, width), BF16),
            *[jax.ShapeDtypeStruct((RING, 4 * each + 8, width), BF16)] * RING,
        ],
        compiler_params=params(BACK_MIB),
        cost_estimate=cost(8 * rows * width * width, 12e6),
        name="weight_back",
    )(pos, gatt, c, dq, dk, dv, xs, xl, sums_f, dub)


def input_back_body(dims, gfs, dq, dk, dv, wq, wk, wv, gs_o, gl_o, total):
    step = pl.program_id(0)
    short_rows, width, cols = dims[0], gfs.shape[1], dq.shape[1]
    part = (
        nt(dq[...], wq[...].reshape(width, cols))
        + nt(dk[...], wk[...].reshape(width, cols))
        + nt(dv[...], wv[...].reshape(width, cols))
    )

    @pl.when(step == 0)
    def _():
        total[...] = gfs[...] + part

    @pl.when(step > 0)
    def _():
        total[...] += part

    @pl.when(step == pl.num_programs(0) - 1)
    def _():
        gs_o[...] = total[:short_rows]
        gl_o[...] = total[short_rows:]


def input_back(gfs, dq, dk, dv, gathered, dims):
    rows, width = gfs.shape
    each = width // SHARDS
    step = 256
    short_rows = dims[0]
    cols = pl.BlockSpec((rows, step), lambda g: (0, g))
    slab = lambda i: pl.BlockSpec((SHARDS, each, step), lambda g: (0, i, g))
    return pl.pallas_call(
        functools.partial(input_back_body, dims),
        grid=(width // step,),
        in_specs=[whole(rows, width), cols, cols, cols, slab(0), slab(1), slab(2)],
        out_specs=[whole(short_rows, width), whole(rows - short_rows, width)],
        scratch_shapes=[pltpu.VMEM((rows, width), F32)],
        out_shape=[
            jax.ShapeDtypeStruct((short_rows, width), F32),
            jax.ShapeDtypeStruct((rows - short_rows, width), F32),
        ],
        compiler_params=params(16),
        cost_estimate=cost(6 * rows * width * width, 12e6),
        name="input_back",
    )(gfs, dq, dk, dv, gathered, gathered, gathered)


def pair_sum(keep, got):
    parts = []
    for d in range(RING):
        at = slice(d * RING, (d + 1) * RING)
        parts.append((keep[at].astype(F32) + got[at].astype(F32)).astype(BF16))
    return parts


def pair_sum_apart(keep, gots):
    return [
        (keep[d * RING : (d + 1) * RING].astype(F32) + got.astype(F32)).astype(BF16) for d, got in enumerate(gots)
    ]


def four_sum(own, left, right, far):
    return (own.astype(F32) + far.astype(F32)) + (left.astype(F32) + right.astype(F32))


def turn(delta, stage):
    moves = []
    for x in range(RING):
        for z in range(RING):
            for core in range(2):
                to_x, to_z = x, z
                if (core == 0) == (stage == 0):
                    to_x = (x + delta) % RING
                else:
                    to_z = (z + delta) % RING
                moves.append(((x * RING + z) * 2 + core, (to_x * RING + to_z) * 2 + core))
    return moves


def swap_cores(v):
    return lax.ppermute(v, "shard", [(i, i ^ 1) for i in range(SHARDS)])


def around(v, stage):
    return tuple(lax.ppermute(v[d] if isinstance(v, (list, tuple)) else v, "shard", turn(d, stage)) for d in (1, 3, 2))


def both_cores(pieces):
    return (*pieces, *(swap_cores(p) for p in pieces))


def second_turn(own, left, right, far):
    parts = [four_sum(own[d], left[d], right[d], far[d]).astype(BF16) for d in range(RING)]
    return four_sum(parts[0], *around(parts, 1)).astype(BF16)


def across_replicas(own):
    return own, *(lax.ppermute(own, "rep", [(i, (i + d) % RING) for i in range(RING)]) for d in (1, 3, 2))


def replica_sum(own, left, right, far, at):
    return (own[at].astype(F32) + far[at].astype(F32)) + (left[at].astype(F32) + right[at].astype(F32))


def finish_attention_body(own, left, right, far, wqkv_o, wo_o, *vector_os):
    each, width = wo_o.shape
    for j in range(wqkv_o.shape[1] // width):
        at = slice(j * each, (j + 1) * each)
        wqkv_o[:, j * width : (j + 1) * width] = replica_sum(own, left, right, far, at)
    wo_o[...] = replica_sum(own, left, right, far, slice(3 * each, 4 * each))
    last = replica_sum(own, left, right, far, slice(4 * each, 4 * each + 8))[:, width - 256 :]
    for i, o in enumerate(vector_os[:-1]):
        o[...] = last[0:1, i * each : (i + 1) * each]
    o = vector_os[-1]
    o[...] = last[1:2, : o.shape[1]]


def finish_attention(arrays, tall):
    width = arrays[0].shape[1]
    each = width // SHARDS
    return pl.pallas_call(
        finish_attention_body,
        out_shape=[
            jax.ShapeDtypeStruct((each, 3 * width), F32),
            jax.ShapeDtypeStruct((each, width), F32),
            *[jax.ShapeDtypeStruct((1, each), F32)] * 8,
            jax.ShapeDtypeStruct((1, tall), F32),
        ],
        compiler_params=params(4),
        name="finish_attention",
    )(*arrays)


def finish_feed_body(own, left, right, far, up_o, down_o):
    parts = own.shape[0] // 2
    each, width = own.shape[1:]
    for j in range(parts):
        down_o[j * each : (j + 1) * each] = replica_sum(own, left, right, far, j)
        up_o[:, j * width : (j + 1) * width] = replica_sum(own, left, right, far, parts + j)


def finish_feed(arrays, each, inner, tall):
    width = arrays[0].shape[2]
    return pl.pallas_call(
        finish_feed_body,
        out_shape=[jax.ShapeDtypeStruct((each, inner), F32), jax.ShapeDtypeStruct((tall, width), F32)],
        compiler_params=params(4),
        name="finish_feed",
    )(*arrays)


def on_device(
    short_tokens, long_tokens, short_lengths, long_lengths, short_cotangent, long_cotangent,
    input_weight, query_bias, value_bias, output_weight, output_bias, first_gain, first_shift,
    up_weight, up_bias, down_weight, down_bias, second_gain, second_shift,
):
    short_count, short_length, width = short_tokens.shape
    long_count, long_length, _ = long_tokens.shape
    dims = (short_count * short_length, long_count, long_length, short_length)
    each, inner, tall = width // SHARDS, up_weight.shape[1], down_weight.shape[0]
    xs, xl = short_tokens.reshape(-1, width), long_tokens.reshape(-1, width)
    cs, cl = short_cotangent.reshape(-1, width), long_cotangent.reshape(-1, width)
    index = lax.axis_index("shard")
    pos = jnp.stack([index // 8, (index // 2) % 4, index % 2]).astype(jnp.int32)

    packed = pack(
        input_weight, output_weight, up_weight, down_weight,
        (query_bias, value_bias, output_bias, first_gain, first_shift, down_bias, second_gain, second_shift),
        up_bias,
    )
    near = (packed, *around(packed, 1))
    cut = 4 * each + 8
    near_a = jnp.stack([n[:cut] for n in near])
    near_f = jnp.stack([n[cut:].reshape(-1, each, width) for n in near])
    around_a = around(near_a, 0)
    far_f = around(near_f, 0)
    pieces_a = both_cores((near_a, *around_a))
    xs, near_f = lax.optimization_barrier((xs, near_f))
    q, k, v, c, ps, plong, unit1, inv1, vecs, ub, gathered_a = attention_forward(
        short_lengths, long_lengths, pos, xs, xl, pieces_a, inner, dims
    )
    unit1, *far_f = lax.optimization_barrier((unit1, *far_f))
    keep_f, give_f, out_s, out_l, gfs, gatt, sums_f, dub = feed(
        short_lengths, long_lengths, pos, unit1, cs, cl, inv1, ub, vecs, both_cores((near_f, *far_f)), dims
    )
    dq, dk, dv = attention_back(gatt, gathered_a, q, k, v, ps, plong, dims)
    parts_f = pair_sum(keep_f, swap_cores(give_f))
    dv, *parts_f = lax.optimization_barrier((dv, *parts_f))
    around_f = around(parts_f, 0)
    keep_a, *gives_a = weight_back(pos, gatt, c, dq, dk, dv, xs, xl, sums_f, dub, dims)
    keep_a, *around_f = lax.optimization_barrier((keep_a, *around_f))
    parts_a = pair_sum_apart(keep_a, [swap_cores(give) for give in gives_a])
    gfs, *parts_a = lax.optimization_barrier((gfs, *parts_a))
    around_a = around(parts_a, 0)
    grad_s, grad_l = input_back(gfs, dq, dk, dv, gathered_a, dims)
    grad_s, *around_a = lax.optimization_barrier((grad_s, *around_a))
    own_f = second_turn(parts_f[0], *around_f)
    own_f, *around_a = lax.optimization_barrier((own_f, *around_a))
    up, down = finish_feed(across_replicas(own_f), each, inner, tall)
    own_a = second_turn(parts_a[0], *around_a)
    w_in, w_out, *vectors = finish_attention(across_replicas(own_a), tall)
    vectors = [x.reshape(-1) for x in vectors]
    return (
        out_s.reshape(short_tokens.shape), out_l.reshape(long_tokens.shape),
        grad_s.reshape(short_tokens.shape), grad_l.reshape(long_tokens.shape),
        w_in, vectors[QB], vectors[VB], w_out, vectors[OB], vectors[G1], vectors[S1],
        up, vectors[8], down, vectors[DB], vectors[G2], vectors[S2],
    )


def solution(mesh):
    rows, flat = P(("rep", "shard"), None, None), P("shard")
    tall = P("shard", None)
    return jax.shard_map(
        on_device,
        mesh=mesh,
        in_specs=(
            rows, rows, P(("rep", "shard")), P(("rep", "shard")), rows, rows,
            tall, flat, flat, tall, flat, flat, flat, tall, flat, tall, flat, flat, flat,
        ),
        out_specs=(
            rows, rows, rows, rows,
            tall, flat, flat, tall, flat, flat, flat, tall, flat, tall, flat, flat, flat,
        ),
        check_vma=False,
    )
```

```python
import functools

import jax
import jax.numpy as jnp
from jax import lax
from jax.experimental import pallas as pl
from jax.experimental.pallas import tpu as pltpu
from jax.sharding import PartitionSpec as P

F32 = jnp.float32
BF16 = jnp.bfloat16
HEAD_DIM = 64
PAIR = 128
EPSILON = 1e-06
BACK_MIB = 58
QB, VB, OB, G1, S1, DB, G2, S2 = range(8)
RING = 4
CHIPS = RING * RING
SHARDS = 2 * CHIPS


def nn(a, b):
    return lax.dot_general(a, b, (((1,), (0,)), ((), ())), preferred_element_type=F32)


def nt(a, b):
    return lax.dot_general(a, b, (((1,), (1,)), ((), ())), preferred_element_type=F32)


def tn(a, b):
    return lax.dot_general(a, b, (((0,), (0,)), ((), ())), preferred_element_type=F32)


def iota(shape, dim):
    return lax.broadcasted_iota(jnp.int32, shape, dim)


def row_of(ref, i):
    return ref[i : i + 1, :].astype(F32)


def whole(*shape):
    return pl.BlockSpec(shape, lambda g, *_: (0,) * len(shape))


def params(mebibytes):
    return pltpu.CompilerParams(vmem_limit_bytes=mebibytes * 1024 * 1024)


def cost(flops, moved):
    return pl.CostEstimate(flops=int(flops), bytes_accessed=int(moved), transcendentals=0)


def places(pos, x, z):
    along_x, along_z = (x - pos[0]) & (RING - 1), (z - pos[1]) & (RING - 1)
    return along_x * RING + along_z, along_z * RING + along_x


def deal(keep, give, pos, value, at, each):
    first = pos[2] == 0
    for x in range(RING):
        for z in range(RING):
            p0, p1 = places(pos, x, z)
            low = 2 * (x * RING + z) * each
            even, odd = value[low : low + each], value[low + each : low + 2 * each]
            keep[jnp.where(first, p0, p1), at] = jnp.where(first, even, odd)
            give[jnp.where(first, p1, p0), at] = jnp.where(first, odd, even)


def deal_apart(keep, gives, spare, pos, value, at, each):
    first = pos[2] == 0
    for x in range(RING):
        for z in range(RING):
            p0, p1 = places(pos, x, z)
            low = 2 * (x * RING + z) * each
            even, odd = value[low : low + each], value[low + each : low + 2 * each]
            keep[jnp.where(first, p0, p1), at] = jnp.where(first, even, odd)
            spare[x * RING + z, :each] = jnp.where(first, odd, even)
    for a, give in enumerate(gives):
        for b in range(RING):
            xa, zb = (pos[0] + a) & (RING - 1), (pos[1] + b) & (RING - 1)
            xb, za = (pos[0] + b) & (RING - 1), (pos[1] + a) & (RING - 1)
            give[b, at] = spare[jnp.where(first, xb * RING + za, xa * RING + zb), :each]


def spread(owners, width):
    each = width // owners
    at = iota((owners, width), 1)
    low = iota((owners, width), 0) * each
    return (at >= low) & (at < low + each)


def column_rest(rows, width, each):
    at = iota((1, width), 1)
    return jnp.broadcast_to(at - (at // each) * each, (rows, width))


def two_heads(pair):
    low_half = iota(pair.shape, 1) < HEAD_DIM
    zero = jnp.zeros_like(pair)
    return jnp.concatenate([jnp.where(low_half, pair, zero), jnp.where(low_half, zero, pair)], axis=0)


def own_lanes(stack):
    half = stack.shape[0] // 2
    return jnp.where(iota((half, stack.shape[1]), 1) < HEAD_DIM, stack[:half], stack[half:])


def normalized(hidden):
    center = hidden - jnp.mean(hidden, axis=-1, keepdims=True)
    spread_of = jnp.mean(center * center, axis=-1, keepdims=True)
    inverse = lax.rsqrt(spread_of + EPSILON)
    return center * inverse, inverse


def norm_back(scaled, unit, inverse):
    return inverse * (
        scaled
        - jnp.mean(scaled, axis=-1, keepdims=True)
        - unit * jnp.mean(scaled * unit, axis=-1, keepdims=True)
    )


def segments(dims):
    short_rows, long_count, long_length, _ = dims
    return [(0, short_rows, None)] + [
        (short_rows + i * long_length, long_length, i) for i in range(long_count)
    ]


def key_bias(slen, llen, short_length, rows, long_at):
    key = iota((rows, rows), 0)
    if long_at is not None:
        return jnp.where(key < llen[long_at], 0.0, -1e9).astype(F32)
    query = iota((rows, rows), 1)
    keep = jnp.zeros((rows, rows), jnp.bool_)
    for p in range(rows // short_length):
        low, high = p * short_length, (p + 1) * short_length
        keep = keep | ((key >= low) & (key < low + slen[p]) & (query >= low) & (query < high))
    return jnp.where(keep, 0.0, -1e9).astype(F32)


def valid_rows(slen, llen, dims):
    short_rows, long_count, long_length, short_length = dims
    parts = []
    at = iota((short_length, 1), 0)
    for p in range(short_rows // short_length):
        parts.append((at < slen[p]).astype(F32))
    at = iota((long_length, 1), 0)
    for p in range(long_count):
        parts.append((at < llen[p]).astype(F32))
    return jnp.concatenate(parts, axis=0)


def slabs_of(out, base, source, each, width):
    for j in range(source.shape[1] // width):
        out[base + j * each : base + (j + 1) * each] = source[:, j * width : (j + 1) * width]
    return base + source.shape[1] // width * each


def pack_body(wqkv, wo, wup, wdown, *rest):
    vectors, out = rest[:-1], rest[-1]
    each, width = wo.shape
    base = slabs_of(out, 0, wqkv, each, width)
    base = slabs_of(out, base, wo, each, width)
    out[base : base + 8] = jnp.zeros((8, width), BF16)
    for i, v in enumerate(vectors[:-1]):
        out[base : base + 1, i * each : (i + 1) * each] = v[...]
    out[base + 1 : base + 2, : vectors[-1].shape[1]] = vectors[-1][...]
    base = slabs_of(out, base + 8, wup, each, width)
    out[base:] = wdown[...]


def pack(wqkv, wo, wup, wdown, vectors, ub):
    each, width = wo.shape
    rows = wqkv.shape[1] // width * each + each + 8 + 2 * wdown.shape[0]
    return pl.pallas_call(
        pack_body,
        out_shape=jax.ShapeDtypeStruct((rows, width), BF16),
        compiler_params=params(58),
        name="pack",
    )(wqkv, wo, wup, wdown, *[v[None] for v in vectors], ub[None])


STEPS = (0, -1, 1, 2)


def gathered_at(pos, other, k, i):
    core = pos[2] ^ other
    x0, z0 = (pos[0] + STEPS[k]) & (RING - 1), (pos[1] + STEPS[i]) & (RING - 1)
    x1, z1 = (pos[0] + STEPS[i]) & (RING - 1), (pos[1] + STEPS[k]) & (RING - 1)
    return jnp.where(core == 0, (x0 * RING + z0) * 2, (x1 * RING + z1) * 2 + 1)


def arrivals(pos, pieces, target, sems, at):
    copies = []
    for other in range(2):
        for k in range(RING):
            for i in range(RING):
                n = (other * RING + k) * RING + i
                copies.append(
                    pltpu.make_async_copy(
                        pieces[other * RING + k].at[i, at], target.at[gathered_at(pos, other, k, i), at], sems.at[n]
                    )
                )
    return copies


def attention_forward_body(
    dims, slen, llen, pos, xs, xl, p0, p1, p2, p3, p4, p5, p6, p7,
    q_o, k_o, v_o, c_o, ps_o, pl_o, n_o, r_o, vecs_o, ub_o, gathered_o,
    x_all, total, wo_all, gathered, sems, out_sem,
):
    step = pl.program_id(0)
    short_rows, width = dims[0], x_all.shape[1]
    cols = q_o.shape[1]
    each = width // SHARDS
    keep_all = pltpu.make_async_copy(gathered, gathered_o, out_sem)

    @pl.when(step == 0)
    def _():
        copies = arrivals(pos, (p0, p1, p2, p3, p4, p5, p6, p7), gathered, sems, slice(None))
        for copy in copies:
            copy.start()
        x_all[:short_rows, :] = xs[...]
        x_all[short_rows:, :] = xl[...]
        total[...] = jnp.zeros_like(total)
        for copy in copies:
            copy.wait()
        keep_all.start()
        wo_all[...] = gathered[:, 3 * each : 4 * each].reshape(width, width)
        packed = gathered[:, 4 * each :]
        line = packed[:, 0, : 8 * each + 64]
        rest = column_rest(line.shape[1], width, each)
        mine = spread(SHARDS, width)
        for i in range(8):
            pick = (iota(rest.shape, 0) == rest + i * each).astype(BF16)
            row = jnp.sum(jnp.where(mine, nn(line, pick), 0.0), axis=0, keepdims=True)
            vecs_o[i : i + 1] = row.astype(BF16)
        inner = ub_o.shape[1]
        line = packed[:, 1, :128]
        pick = (iota((128, inner), 0) == column_rest(128, inner, inner // SHARDS)).astype(BF16)
        row = jnp.sum(jnp.where(spread(SHARDS, inner), nn(line, pick), 0.0), axis=0, keepdims=True)
        ub_o[...] = row.astype(BF16)

    x = x_all[...]
    at_cols = pl.ds(pl.multiple_of(step * cols, cols), cols)
    wq, wk, wv = (gathered[:, i * each : (i + 1) * each, at_cols].reshape(width, cols) for i in range(3))
    q_o[...] = (nn(x, wq) + vecs_o[QB : QB + 1, at_cols].astype(F32)).astype(BF16)
    k_o[...] = nn(x, wk).astype(BF16)
    v_o[...] = (nn(x, wv) + vecs_o[VB : VB + 1, at_cols].astype(F32)).astype(BF16)
    for first, rows, long_at in segments(dims):
        bias = key_bias(slen, llen, dims[3], rows, long_at)
        at = slice(first, first + rows)
        for pair in range(cols // PAIR):
            lanes = slice(pair * PAIR, (pair + 1) * PAIR)
            q = q_o[at, lanes] * jnp.asarray(HEAD_DIM**-0.5, BF16)
            scores = nt(two_heads(k_o[at, lanes]), q)
            probs = []
            for h in range(2):
                s = scores[h * rows : (h + 1) * rows] + bias
                e = jnp.exp(s - jnp.max(s, axis=0, keepdims=True))
                probs.append((e * (1.0 / jnp.sum(e, axis=0, keepdims=True))).astype(BF16))
            probs = jnp.concatenate(probs, axis=0)
            if long_at is None:
                ps_o[pair] = probs
            else:
                pl_o[long_at, pair] = probs
            c_o[at, lanes] = tn(probs, two_heads(v_o[at, lanes])).astype(BF16)
    total[...] += nn(c_o[...], wo_all[at_cols, :])

    @pl.when(step == pl.num_programs(0) - 1)
    def _():
        h = x_all[...].astype(F32) + (total[...] + row_of(vecs_o, OB))
        unit, inverse = normalized(h)
        n_o[...] = unit
        r_o[...] = inverse
        keep_all.wait()


def attention_forward(slen, llen, pos, xs, xl, pieces, inner, dims):
    rows, width = xs.shape[0] + xl.shape[0], xs.shape[1]
    short_rows, long_count, long_length, _ = dims
    step = 256
    steps, pairs = width // step, width // PAIR
    per = step // PAIR
    each_all = pieces[0].shape[1]
    cols = pl.BlockSpec((rows, step), lambda g, *_: (0, g))
    return pl.pallas_call(
        functools.partial(attention_forward_body, dims),
        grid_spec=pltpu.PrefetchScalarGridSpec(
            num_scalar_prefetch=3,
            grid=(steps,),
            in_specs=[
                whole(*xs.shape), whole(*xl.shape), *[pl.BlockSpec(memory_space=pl.ANY)] * 8,
            ],
            out_specs=[
                cols, cols, cols, cols,
                pl.BlockSpec((per, 2 * short_rows, short_rows), lambda g, *_: (g, 0, 0)),
                pl.BlockSpec((long_count, per, 2 * long_length, long_length), lambda g, *_: (0, g, 0, 0)),
                whole(rows, width), whole(rows, 1), whole(8, width), whole(1, inner),
                pl.BlockSpec(memory_space=pl.ANY),
            ],
            scratch_shapes=[
                pltpu.VMEM((rows, width), BF16), pltpu.VMEM((rows, width), F32), pltpu.VMEM((width, width), BF16),
                pltpu.VMEM((SHARDS, each_all, width), BF16), pltpu.SemaphoreType.DMA((SHARDS,)),
                pltpu.SemaphoreType.DMA(()),
            ],
        ),
        out_shape=[
            *[jax.ShapeDtypeStruct((rows, width), BF16)] * 4,
            jax.ShapeDtypeStruct((pairs, 2 * short_rows, short_rows), BF16),
            jax.ShapeDtypeStruct((long_count, pairs, 2 * long_length, long_length), BF16),
            jax.ShapeDtypeStruct((rows, width), F32),
            jax.ShapeDtypeStruct((rows, 1), F32),
            jax.ShapeDtypeStruct((8, width), BF16),
            jax.ShapeDtypeStruct((1, inner), BF16),
            jax.ShapeDtypeStruct((SHARDS, each_all, width), BF16),
        ],
        compiler_params=params(58),
        cost_estimate=cost(8 * rows * width * width, 20e6),
        name="attention_forward",
    )(slen, llen, pos, xs, xl, *pieces)


HBM = pl.BlockSpec(memory_space=pl.ANY)
ON_CHIP = pl.BlockSpec(memory_space=pltpu.VMEM)
SCALARS = pl.BlockSpec(memory_space=pltpu.SMEM)


class Copies:
    def __init__(self, sems):
        self.sems, self.used, self.open = sems, 0, []

    def start(self, source, target):
        copy = pltpu.make_async_copy(source, target, self.sems.at[self.used])
        self.used += 1
        copy.start()
        return copy

    def send(self, source, target):
        self.open.append(self.start(source, target))

    def finish(self):
        for copy in self.open:
            copy.wait()


def feed_body(
    dims, slen, llen, pos, unit1, cot_s, cot_l, inv1, ub, vecs, p0, p1, p2, p3, p4, p5, p6, p7,
    keep, give, outs_o, outl_o, gfs_o, gatt_o, sums_o, dub_o,
    wup, wdown, unit_v, cot_v, low_v, low_t, hidden, gelu_v, grad_v, gffn, out_v, gatt, valid_v,
    keep_dv, give_dv, keep_uv, give_uv, sems, piece_sems, down_sems, up_sems,
):
    short_rows = dims[0]
    rows, width = low_v.shape
    parts, block = hidden.shape[0], hidden.shape[2]
    each, tall = width // SHARDS, block * parts // SHARDS
    owners, lanes, tile = SHARDS // parts, 256, 128
    copies = Copies(sems)
    pieces = (p0, p1, p2, p3, p4, p5, p6, p7)
    unit_here = copies.start(unit1, unit_v)
    groups = [[], [], []]
    for other in range(2):
        for k in range(RING):
            for i in range(RING):
                n = (other * RING + k) * RING + i
                at = gathered_at(pos, other, k, i)
                source = pieces[other * RING + k]
                half = parts // 2
                targets = (wup.at[:half, at], wup.at[half:, at], wdown.at[at])
                sources = (source.at[i, :half], source.at[i, half:parts], source.at[i, parts:])
                for group, sem, src, target in zip(groups, range(3), sources, targets):
                    group.append(pltpu.make_async_copy(src, target, piece_sems.at[sem, n]))
    for copy in groups[0]:
        copy.start()
    valid_v[...] = valid_rows(slen, llen, dims)
    grad_v[...] = jnp.zeros_like(grad_v)
    unit_here.wait()

    @pl.loop(0, rows // tile)
    def _(r):
        at = pl.ds(pl.multiple_of(r * tile, tile), tile)
        low_v[at] = (unit_v[at] * row_of(vecs, G1) + row_of(vecs, S1)).astype(BF16)

    @pl.loop(0, parts)
    def _(j):
        for n in range(2):

            @pl.when(j == n * (parts // 2))
            def _():
                for copy in groups[n]:
                    copy.wait()
                for copy in groups[n + 1]:
                    copy.start()

        bias = ub[:, pl.ds(pl.multiple_of(j * block, block), block)].astype(F32)
        pre = nn(low_v[...], wup[j].reshape(width, block)) + bias
        cdf = 0.5 + 0.5 * lax.erf(pre * (0.5**0.5))
        density = jnp.exp(-0.5 * pre * pre) * (0.5 / jnp.pi) ** 0.5
        hidden[j] = (pre * cdf).astype(BF16)
        gelu_v[j] = (cdf + pre * density).astype(BF16)

    for copy in groups[2]:
        copy.wait()
    cots_here = copies.start(cot_s, cot_v.at[:short_rows]), copies.start(cot_l, cot_v.at[short_rows:])

    @pl.loop(0, parts)
    def _(j):
        grad_v[...] += nn(hidden[j], wdown[pl.ds(j * owners, owners)].reshape(block, width))

    for copy in cots_here:
        copy.wait()
    sums_o[...] = jnp.zeros_like(sums_o)

    @pl.loop(0, rows // tile)
    def _(r):
        at = pl.ds(pl.multiple_of(r * tile, tile), tile)
        first = unit_v[at] * row_of(vecs, G1) + row_of(vecs, S1)
        unit, inverse = normalized(first + (grad_v[at] + row_of(vecs, DB)))
        valid = valid_v[at]
        out_v[at] = ((unit * row_of(vecs, G2) + row_of(vecs, S2)) * valid).astype(BF16)
        cot = cot_v[at].astype(F32) * valid
        back = norm_back(cot * row_of(vecs, G2), unit, inverse)
        grad_v[at] = back
        low_back = back.astype(BF16)
        gffn[at] = low_back
        sums_o[DB : DB + 1] += jnp.sum(low_back.astype(F32), axis=0, keepdims=True)
        sums_o[G2 : G2 + 1] += jnp.sum(cot * unit, axis=0, keepdims=True)
        sums_o[S2 : S2 + 1] += jnp.sum(cot, axis=0, keepdims=True)

    copies.send(out_v.at[:short_rows], outs_o)
    copies.send(out_v.at[short_rows:], outl_o)
    on_first = pos[2] == 0

    def down_copies(at, p0, p1):
        return (
            pltpu.make_async_copy(keep_dv.at[at], keep.at[jnp.where(on_first, p0, p1), :parts], down_sems.at[0, at]),
            pltpu.make_async_copy(give_dv.at[at], give.at[jnp.where(on_first, p1, p0), :parts], down_sems.at[1, at]),
        )

    @pl.loop(0, RING)
    def _(x):
        grad = tn(hidden[x], gffn[...]).astype(BF16)
        for z in range(RING):
            place = x * RING + z
            even, odd = grad[2 * z * tall : (2 * z + 1) * tall], grad[(2 * z + 1) * tall : (2 * z + 2) * tall]
            keep_dv[place] = jnp.where(on_first, even, odd).reshape(parts, each, width)
            give_dv[place] = jnp.where(on_first, odd, even).reshape(parts, each, width)
            for copy in down_copies(place, *places(pos, x, z)):
                copy.start()

    def up_copies(j):
        return (
            pltpu.make_async_copy(keep_uv.at[j], keep.at[:, parts + j], up_sems.at[0, j]),
            pltpu.make_async_copy(give_uv.at[j], give.at[:, parts + j], up_sems.at[1, j]),
        )

    low_t[:width] = low_v[...].T
    low_t[width:] = jnp.ones((16, rows), BF16)

    @pl.loop(0, parts)
    def _(j):
        weight = wdown[pl.ds(j * owners, owners)].reshape(block, width)
        up = (nt(gffn[...], weight) * gelu_v[j].astype(F32)).astype(BF16)
        hidden[j] = up
        grad = nn(low_t[...], hidden[j])
        dub_o[:, pl.ds(pl.multiple_of(j * block, block), block)] = grad[width : width + 1]
        deal(keep_uv.at[j], give_uv.at[j], pos, grad[:width].astype(BF16), slice(None), each)
        for copy in up_copies(j):
            copy.start()

    @pl.loop(0, parts)
    def _(j):
        grad_v[...] += nt(hidden[j], wup[j].reshape(width, block))

    @pl.loop(0, rows // tile)
    def _(r):
        at = pl.ds(pl.multiple_of(r * tile, tile), tile)
        grad, unit = grad_v[at], unit_v[at]
        back = norm_back(grad * row_of(vecs, G1), unit, inv1[at])
        grad_v[at] = back
        low_back = back.astype(BF16)
        gatt[at] = low_back
        sums_o[OB : OB + 1] += jnp.sum(low_back.astype(F32), axis=0, keepdims=True)
        sums_o[G1 : G1 + 1] += jnp.sum(grad * unit, axis=0, keepdims=True)
        sums_o[S1 : S1 + 1] += jnp.sum(grad, axis=0, keepdims=True)

    copies.send(gatt, gatt_o)
    copies.send(grad_v, gfs_o)
    for at in range(CHIPS):
        for copy in down_copies(at, at, at):
            copy.wait()
    for j in range(parts):
        for copy in up_copies(j):
            copy.wait()
    copies.finish()


def feed(slen, llen, pos, unit1, cot_s, cot_l, inv1, ub, vecs, pieces, dims):
    rows, width = unit1.shape
    inner = ub.shape[1]
    parts = RING
    block, tall, each = inner // parts, inner // SHARDS, width // SHARDS
    down, up = (CHIPS, parts, each, width), (parts, CHIPS, each, width)
    return pl.pallas_call(
        functools.partial(feed_body, dims),
        in_specs=[SCALARS] * 3 + [HBM] * 3 + [ON_CHIP] * 3 + [HBM] * 8,
        out_specs=[HBM] * 6 + [ON_CHIP] * 2,
        scratch_shapes=[
            pltpu.VMEM((parts, SHARDS, each, width), BF16), pltpu.VMEM((SHARDS, parts, each, width), BF16),
            pltpu.VMEM((rows, width), F32), pltpu.VMEM((rows, width), BF16), pltpu.VMEM((rows, width), BF16),
            pltpu.VMEM((width + 16, rows), BF16), pltpu.VMEM((parts, rows, block), BF16),
            pltpu.VMEM((parts, rows, block), BF16), pltpu.VMEM((rows, width), F32), pltpu.VMEM((rows, width), BF16),
            pltpu.VMEM((rows, width), BF16), pltpu.VMEM((rows, width), BF16), pltpu.VMEM((rows, 1), F32),
            pltpu.VMEM(down, BF16), pltpu.VMEM(down, BF16), pltpu.VMEM(up, BF16), pltpu.VMEM(up, BF16),
            pltpu.SemaphoreType.DMA((8,)), pltpu.SemaphoreType.DMA((3, SHARDS)),
            pltpu.SemaphoreType.DMA((2, CHIPS)), pltpu.SemaphoreType.DMA((2, parts)),
        ],
        out_shape=[
            *[jax.ShapeDtypeStruct((CHIPS, 2 * parts, each, width), BF16)] * 2,
            jax.ShapeDtypeStruct(cot_s.shape, BF16),
            jax.ShapeDtypeStruct(cot_l.shape, BF16),
            jax.ShapeDtypeStruct((rows, width), F32),
            jax.ShapeDtypeStruct((rows, width), BF16),
            jax.ShapeDtypeStruct((8, width), F32),
            jax.ShapeDtypeStruct((1, inner), F32),
        ],
        compiler_params=params(58),
        cost_estimate=cost(12 * rows * width * inner, 30e6),
        name="feed",
    )(slen, llen, pos, unit1, cot_s, cot_l, inv1, ub, vecs, *pieces)


def attention_back_body(dims, gatt, wo_block, q, k, v, ps, plong, dq_o, dk_o, dv_o, gc, wo_all):
    step = pl.program_id(0)
    width, cols = gatt.shape[1], q.shape[1]
    at_cols = pl.ds(pl.multiple_of(step * cols, cols), cols)

    @pl.when(step == 0)
    def _():
        wo_all[...] = wo_block[...].reshape(width, width)

    gc[...] = nt(gatt[...], wo_all[at_cols, :]).astype(BF16)
    scale = HEAD_DIM**-0.5
    for first, rows, long_at in segments(dims):
        at = slice(first, first + rows)
        for pair in range(cols // PAIR):
            lanes = slice(pair * PAIR, (pair + 1) * PAIR)
            probs = ps[pair] if long_at is None else plong[long_at, pair]
            grad = gc[at, lanes]
            dp = nt(two_heads(v[at, lanes]), grad)
            ds = []
            for h in range(2):
                half = slice(h * rows, (h + 1) * rows)
                p = probs[half].astype(F32)
                d = dp[half]
                ds.append((p * (d - jnp.sum(d * p, axis=0, keepdims=True))).astype(BF16))
            ds = jnp.concatenate(ds, axis=0)
            dv_o[at, lanes] = own_lanes(nn(probs, grad)).astype(BF16)
            dk_o[at, lanes] = (own_lanes(nn(ds, q[at, lanes])) * scale).astype(BF16)
            dq_o[at, lanes] = (tn(ds, two_heads(k[at, lanes])) * scale).astype(BF16)


def attention_back(gatt, gathered, q, k, v, ps, plong, dims):
    rows, width = gatt.shape
    short_rows, long_count, long_length, _ = dims
    step = 256
    per = step // PAIR
    cols = pl.BlockSpec((rows, step), lambda g: (0, g))
    return pl.pallas_call(
        functools.partial(attention_back_body, dims),
        grid=(width // step,),
        in_specs=[
            whole(rows, width),
            pl.BlockSpec((SHARDS, width // SHARDS, width), lambda g: (0, 3, 0)),
            cols, cols, cols,
            pl.BlockSpec((per, 2 * short_rows, short_rows), lambda g: (g, 0, 0)),
            pl.BlockSpec((long_count, per, 2 * long_length, long_length), lambda g: (0, g, 0, 0)),
        ],
        out_specs=[cols, cols, cols],
        scratch_shapes=[pltpu.VMEM((rows, step), BF16), pltpu.VMEM((width, width), BF16)],
        out_shape=[jax.ShapeDtypeStruct((rows, width), BF16)] * 3,
        compiler_params=params(BACK_MIB),
        cost_estimate=cost(8 * rows * width * width, 15e6),
        name="attention_back",
    )(gatt, gathered, q, k, v, ps, plong)


def weight_back_body(
    dims, pos, gatt_cols, c, dq, dk, dv, xs, xl, sums_f, dub,
    keep, g0, g1, g2, g3,
    x_t, c_t, sums, spare,
):
    gives = (g0, g1, g2, g3)
    step = pl.program_id(0)
    short_rows = dims[0]
    rows, width = c.shape
    cols = dq.shape[1]
    each = width // SHARDS
    at_cols = pl.ds(pl.multiple_of(step * cols, cols), cols)

    @pl.when(step == 0)
    def _():
        x_t[:width, :short_rows] = xs[...].T
        x_t[:width, short_rows:] = xl[...].T
        x_t[width:] = jnp.ones((16, rows), BF16)
        c_t[...] = c[...].T
        sums[...] = sums_f[...]

    deal_apart(keep, gives, spare, pos, nn(c_t[...], gatt_cols[...]).astype(BF16), slice(3 * each, 4 * each), each)
    for i, d in enumerate((dq, dk, dv)):
        grad = nn(x_t[...], d[...])
        deal_apart(keep, gives, spare, pos, grad[:width].astype(BF16), slice(i * each, (i + 1) * each), each)
        if i != 1:
            at = QB if i == 0 else VB
            sums[at : at + 1, at_cols] = grad[width : width + 1]
    keep[:, 4 * each :] = jnp.zeros((CHIPS, 8, cols), BF16)
    for give in gives:
        give[:, 4 * each :] = jnp.zeros((RING, 8, cols), BF16)

    @pl.when(step == pl.num_programs(0) - 1)
    def _():
        mine = spread(SHARDS, width)
        rest = column_rest(cols, width, each)
        line = jnp.zeros((SHARDS, cols), F32)
        for i in range(8):
            put = (iota(rest.shape, 0) == rest + i * each).astype(BF16)
            line += nt(jnp.where(mine, sums[i : i + 1], 0.0).astype(BF16), put)
        inner = dub.shape[1]
        put = (iota((cols, inner), 0) == column_rest(cols, inner, inner // SHARDS)).astype(BF16)
        wide = nt(jnp.where(spread(SHARDS, inner), dub[...], 0.0).astype(BF16), put)
        both = jnp.concatenate([line[:, None], wide[:, None], jnp.zeros((SHARDS, 6, cols), F32)], axis=1)
        deal_apart(keep, gives, spare, pos, both.reshape(SHARDS * 8, cols).astype(BF16), slice(4 * each, 4 * each + 8), 8)


def weight_back(pos, gatt, c, dq, dk, dv, xs, xl, sums_f, dub, dims):
    rows, width = gatt.shape
    each = width // SHARDS
    step = 256
    cols = pl.BlockSpec((rows, step), lambda g, *_: (0, g))
    dealt = pl.BlockSpec((CHIPS, 4 * each + 8, step), lambda g, *_: (0, 0, g))
    return pl.pallas_call(
        functools.partial(weight_back_body, dims),
        grid_spec=pltpu.PrefetchScalarGridSpec(
            num_scalar_prefetch=1,
            grid=(width // step,),
            in_specs=[
                cols, whole(rows, width), cols, cols, cols,
                whole(*xs.shape), whole(*xl.shape), whole(8, width), whole(*dub.shape),
            ],
            out_specs=[dealt, *[pl.BlockSpec((RING, 4 * each + 8, step), lambda g, *_: (0, 0, g))] * RING],
            scratch_shapes=[
                pltpu.VMEM((width + 16, rows), BF16), pltpu.VMEM((width, rows), BF16), pltpu.VMEM((8, width), F32),
                pltpu.VMEM((CHIPS, each, step), BF16),
            ],
        ),
        out_shape=[
            jax.ShapeDtypeStruct((CHIPS, 4 * each + 8, width), BF16),
            *[jax.ShapeDtypeStruct((RING, 4 * each + 8, width), BF16)] * RING,
        ],
        compiler_params=params(BACK_MIB),
        cost_estimate=cost(8 * rows * width * width, 12e6),
        name="weight_back",
    )(pos, gatt, c, dq, dk, dv, xs, xl, sums_f, dub)


def input_back_body(dims, gfs, dq, dk, dv, wq, wk, wv, gs_o, gl_o, total):
    step = pl.program_id(0)
    short_rows, width, cols = dims[0], gfs.shape[1], dq.shape[1]
    part = (
        nt(dq[...], wq[...].reshape(width, cols))
        + nt(dk[...], wk[...].reshape(width, cols))
        + nt(dv[...], wv[...].reshape(width, cols))
    )

    @pl.when(step == 0)
    def _():
        total[...] = gfs[...] + part

    @pl.when(step > 0)
    def _():
        total[...] += part

    @pl.when(step == pl.num_programs(0) - 1)
    def _():
        gs_o[...] = total[:short_rows]
        gl_o[...] = total[short_rows:]


def input_back(gfs, dq, dk, dv, gathered, dims):
    rows, width = gfs.shape
    each = width // SHARDS
    step = 256
    short_rows = dims[0]
    cols = pl.BlockSpec((rows, step), lambda g: (0, g))
    slab = lambda i: pl.BlockSpec((SHARDS, each, step), lambda g: (0, i, g))
    return pl.pallas_call(
        functools.partial(input_back_body, dims),
        grid=(width // step,),
        in_specs=[whole(rows, width), cols, cols, cols, slab(0), slab(1), slab(2)],
        out_specs=[whole(short_rows, width), whole(rows - short_rows, width)],
        scratch_shapes=[pltpu.VMEM((rows, width), F32)],
        out_shape=[
            jax.ShapeDtypeStruct((short_rows, width), F32),
            jax.ShapeDtypeStruct((rows - short_rows, width), F32),
        ],
        compiler_params=params(16),
        cost_estimate=cost(6 * rows * width * width, 12e6),
        name="input_back",
    )(gfs, dq, dk, dv, gathered, gathered, gathered)


def pair_sum(keep, got):
    parts = []
    for d in range(RING):
        at = slice(d * RING, (d + 1) * RING)
        parts.append((keep[at].astype(F32) + got[at].astype(F32)).astype(BF16))
    return parts


def pair_sum_apart(keep, gots):
    return [
        (keep[d * RING : (d + 1) * RING].astype(F32) + got.astype(F32)).astype(BF16) for d, got in enumerate(gots)
    ]


def four_sum(own, left, right, far):
    return (own.astype(F32) + far.astype(F32)) + (left.astype(F32) + right.astype(F32))


def turn(delta, stage):
    moves = []
    for x in range(RING):
        for z in range(RING):
            for core in range(2):
                to_x, to_z = x, z
                if (core == 0) == (stage == 0):
                    to_x = (x + delta) % RING
                else:
                    to_z = (z + delta) % RING
                moves.append(((x * RING + z) * 2 + core, (to_x * RING + to_z) * 2 + core))
    return moves


def swap_cores(v):
    return lax.ppermute(v, "shard", [(i, i ^ 1) for i in range(SHARDS)])


def around(v, stage):
    return tuple(lax.ppermute(v[d] if isinstance(v, (list, tuple)) else v, "shard", turn(d, stage)) for d in (1, 3, 2))


def both_cores(pieces):
    return (*pieces, *(swap_cores(p) for p in pieces))


def second_turn(own, left, right, far):
    parts = [four_sum(own[d], left[d], right[d], far[d]).astype(BF16) for d in range(RING)]
    return parts[0], *around(parts, 1)


def across_replicas(own):
    return own, *(lax.ppermute(own, "rep", [(i, (i + d) % RING) for i in range(RING)]) for d in (1, 3, 2))


def replica_sum(own, left, right, far, at):
    return (own[at].astype(F32) + far[at].astype(F32)) + (left[at].astype(F32) + right[at].astype(F32))


def finish_attention_body(own, left, right, far, wqkv_o, wo_o, *vector_os):
    each, width = wo_o.shape
    for j in range(wqkv_o.shape[1] // width):
        at = slice(j * each, (j + 1) * each)
        wqkv_o[:, j * width : (j + 1) * width] = replica_sum(own, left, right, far, at)
    wo_o[...] = replica_sum(own, left, right, far, slice(3 * each, 4 * each))
    last = replica_sum(own, left, right, far, slice(4 * each, 4 * each + 8))[:, width - 256 :]
    for i, o in enumerate(vector_os[:-1]):
        o[...] = last[0:1, i * each : (i + 1) * each]
    o = vector_os[-1]
    o[...] = last[1:2, : o.shape[1]]


def finish_attention(arrays, tall):
    width = arrays[0].shape[1]
    each = width // SHARDS
    return pl.pallas_call(
        finish_attention_body,
        out_shape=[
            jax.ShapeDtypeStruct((each, 3 * width), F32),
            jax.ShapeDtypeStruct((each, width), F32),
            *[jax.ShapeDtypeStruct((1, each), F32)] * 8,
            jax.ShapeDtypeStruct((1, tall), F32),
        ],
        compiler_params=params(4),
        name="finish_attention",
    )(*arrays)


def finish_feed_body(own, left, right, far, up_o, down_o):
    parts = own.shape[0] // 2
    each, width = own.shape[1:]
    for j in range(parts):
        down_o[j * each : (j + 1) * each] = replica_sum(own, left, right, far, j)
        up_o[:, j * width : (j + 1) * width] = replica_sum(own, left, right, far, parts + j)


def finish_feed(arrays, each, inner, tall):
    width = arrays[0].shape[2]
    return pl.pallas_call(
        finish_feed_body,
        out_shape=[jax.ShapeDtypeStruct((each, inner), F32), jax.ShapeDtypeStruct((tall, width), F32)],
        compiler_params=params(4),
        name="finish_feed",
    )(*arrays)


def on_device(
    short_tokens, long_tokens, short_lengths, long_lengths, short_cotangent, long_cotangent,
    input_weight, query_bias, value_bias, output_weight, output_bias, first_gain, first_shift,
    up_weight, up_bias, down_weight, down_bias, second_gain, second_shift,
):
    short_count, short_length, width = short_tokens.shape
    long_count, long_length, _ = long_tokens.shape
    dims = (short_count * short_length, long_count, long_length, short_length)
    each, inner, tall = width // SHARDS, up_weight.shape[1], down_weight.shape[0]
    xs, xl = short_tokens.reshape(-1, width), long_tokens.reshape(-1, width)
    cs, cl = short_cotangent.reshape(-1, width), long_cotangent.reshape(-1, width)
    index = lax.axis_index("shard")
    pos = jnp.stack([index // 8, (index // 2) % 4, index % 2]).astype(jnp.int32)

    packed = pack(
        input_weight, output_weight, up_weight, down_weight,
        (query_bias, value_bias, output_bias, first_gain, first_shift, down_bias, second_gain, second_shift),
        up_bias,
    )
    near = (packed, *around(packed, 1))
    cut = 4 * each + 8
    near_a = jnp.stack([n[:cut] for n in near])
    near_f = jnp.stack([n[cut:].reshape(-1, each, width) for n in near])
    around_a = around(near_a, 0)
    far_f = around(near_f, 0)
    pieces_a = both_cores((near_a, *around_a))
    xs, near_f = lax.optimization_barrier((xs, near_f))
    q, k, v, c, ps, plong, unit1, inv1, vecs, ub, gathered_a = attention_forward(
        short_lengths, long_lengths, pos, xs, xl, pieces_a, inner, dims
    )
    unit1, *far_f = lax.optimization_barrier((unit1, *far_f))
    keep_f, give_f, out_s, out_l, gfs, gatt, sums_f, dub = feed(
        short_lengths, long_lengths, pos, unit1, cs, cl, inv1, ub, vecs, both_cores((near_f, *far_f)), dims
    )
    dq, dk, dv = attention_back(gatt, gathered_a, q, k, v, ps, plong, dims)
    parts_f = pair_sum(keep_f, swap_cores(give_f))
    dv, *parts_f = lax.optimization_barrier((dv, *parts_f))
    around_f = around(parts_f, 0)
    keep_a, *gives_a = weight_back(pos, gatt, c, dq, dk, dv, xs, xl, sums_f, dub, dims)
    keep_a, *around_f = lax.optimization_barrier((keep_a, *around_f))
    parts_a = pair_sum_apart(keep_a, [swap_cores(give) for give in gives_a])
    gfs, *parts_a = lax.optimization_barrier((gfs, *parts_a))
    around_a = around(parts_a, 0)
    grad_s, grad_l = input_back(gfs, dq, dk, dv, gathered_a, dims)
    grad_s, *around_a = lax.optimization_barrier((grad_s, *around_a))
    own_f = four_sum(*second_turn(parts_f[0], *around_f)).astype(BF16)
    own_f, *around_a = lax.optimization_barrier((own_f, *around_a))
    own_f, *others_f = across_replicas(own_f)
    last_a = second_turn(parts_a[0], *around_a)
    *last_a, left_f, right_f = lax.optimization_barrier((*last_a, *others_f[:2]))
    up, down = finish_feed((own_f, left_f, right_f, others_f[2]), each, inner, tall)
    own_a = four_sum(*last_a).astype(BF16)
    w_in, w_out, *vectors = finish_attention(across_replicas(own_a), tall)
    vectors = [x.reshape(-1) for x in vectors]
    return (
        out_s.reshape(short_tokens.shape), out_l.reshape(long_tokens.shape),
        grad_s.reshape(short_tokens.shape), grad_l.reshape(long_tokens.shape),
        w_in, vectors[QB], vectors[VB], w_out, vectors[OB], vectors[G1], vectors[S1],
        up, vectors[8], down, vectors[DB], vectors[G2], vectors[S2],
    )


def solution(mesh):
    rows, flat = P(("rep", "shard"), None, None), P("shard")
    tall = P("shard", None)
    return jax.shard_map(
        on_device,
        mesh=mesh,
        in_specs=(
            rows, rows, P(("rep", "shard")), P(("rep", "shard")), rows, rows,
            tall, flat, flat, tall, flat, flat, flat, tall, flat, tall, flat, flat, flat,
        ),
        out_specs=(
            rows, rows, rows, rows,
            tall, flat, flat, tall, flat, flat, flat, tall, flat, tall, flat, flat, flat,
        ),
        check_vma=False,
    )
```

```python
import functools

import jax
import jax.numpy as jnp
from jax import lax
from jax.experimental import pallas as pl
from jax.experimental.pallas import tpu as pltpu
from jax.sharding import PartitionSpec as P

F32 = jnp.float32
BF16 = jnp.bfloat16
HEAD_DIM = 64
PAIR = 128
EPSILON = 1e-06
BACK_MIB = 58
QB, VB, OB, G1, S1, DB, G2, S2 = range(8)
RING = 4
CHIPS = RING * RING
SHARDS = 2 * CHIPS


def nn(a, b):
    return lax.dot_general(a, b, (((1,), (0,)), ((), ())), preferred_element_type=F32)


def nt(a, b):
    return lax.dot_general(a, b, (((1,), (1,)), ((), ())), preferred_element_type=F32)


def tn(a, b):
    return lax.dot_general(a, b, (((0,), (0,)), ((), ())), preferred_element_type=F32)


def iota(shape, dim):
    return lax.broadcasted_iota(jnp.int32, shape, dim)


def row_of(ref, i):
    return ref[i : i + 1, :].astype(F32)


def whole(*shape):
    return pl.BlockSpec(shape, lambda g, *_: (0,) * len(shape))


def params(mebibytes):
    return pltpu.CompilerParams(vmem_limit_bytes=mebibytes * 1024 * 1024)


def cost(flops, moved):
    return pl.CostEstimate(flops=int(flops), bytes_accessed=int(moved), transcendentals=0)


def places(pos, x, z):
    along_x, along_z = (x - pos[0]) & (RING - 1), (z - pos[1]) & (RING - 1)
    return along_x * RING + along_z, along_z * RING + along_x


def deal(keep, give, pos, value, at, each):
    first = pos[2] == 0
    for x in range(RING):
        for z in range(RING):
            p0, p1 = places(pos, x, z)
            low = 2 * (x * RING + z) * each
            even, odd = value[low : low + each], value[low + each : low + 2 * each]
            keep[jnp.where(first, p0, p1), at] = jnp.where(first, even, odd)
            give[jnp.where(first, p1, p0), at] = jnp.where(first, odd, even)


def deal_apart(keep, gives, spare, pos, value, at, each):
    first = pos[2] == 0
    for x in range(RING):
        for z in range(RING):
            p0, p1 = places(pos, x, z)
            low = 2 * (x * RING + z) * each
            even, odd = value[low : low + each], value[low + each : low + 2 * each]
            keep[jnp.where(first, p0, p1), at] = jnp.where(first, even, odd)
            spare[x * RING + z, :each] = jnp.where(first, odd, even)
    for a, give in enumerate(gives):
        for b in range(RING):
            xa, zb = (pos[0] + a) & (RING - 1), (pos[1] + b) & (RING - 1)
            xb, za = (pos[0] + b) & (RING - 1), (pos[1] + a) & (RING - 1)
            give[b, at] = spare[jnp.where(first, xb * RING + za, xa * RING + zb), :each]


def spread(owners, width):
    each = width // owners
    at = iota((owners, width), 1)
    low = iota((owners, width), 0) * each
    return (at >= low) & (at < low + each)


def column_rest(rows, width, each):
    at = iota((1, width), 1)
    return jnp.broadcast_to(at - (at // each) * each, (rows, width))


def two_heads(pair):
    low_half = iota(pair.shape, 1) < HEAD_DIM
    zero = jnp.zeros_like(pair)
    return jnp.concatenate([jnp.where(low_half, pair, zero), jnp.where(low_half, zero, pair)], axis=0)


def own_lanes(stack):
    half = stack.shape[0] // 2
    return jnp.where(iota((half, stack.shape[1]), 1) < HEAD_DIM, stack[:half], stack[half:])


def normalized(hidden):
    center = hidden - jnp.mean(hidden, axis=-1, keepdims=True)
    spread_of = jnp.mean(center * center, axis=-1, keepdims=True)
    inverse = lax.rsqrt(spread_of + EPSILON)
    return center * inverse, inverse


def norm_back(scaled, unit, inverse):
    return inverse * (
        scaled
        - jnp.mean(scaled, axis=-1, keepdims=True)
        - unit * jnp.mean(scaled * unit, axis=-1, keepdims=True)
    )


def segments(dims):
    short_rows, long_count, long_length, _ = dims
    return [(0, short_rows, None)] + [
        (short_rows + i * long_length, long_length, i) for i in range(long_count)
    ]


def key_bias(slen, llen, short_length, rows, long_at):
    key = iota((rows, rows), 0)
    if long_at is not None:
        return jnp.where(key < llen[long_at], 0.0, -1e9).astype(F32)
    query = iota((rows, rows), 1)
    keep = jnp.zeros((rows, rows), jnp.bool_)
    for p in range(rows // short_length):
        low, high = p * short_length, (p + 1) * short_length
        keep = keep | ((key >= low) & (key < low + slen[p]) & (query >= low) & (query < high))
    return jnp.where(keep, 0.0, -1e9).astype(F32)


def valid_rows(slen, llen, dims):
    short_rows, long_count, long_length, short_length = dims
    parts = []
    at = iota((short_length, 1), 0)
    for p in range(short_rows // short_length):
        parts.append((at < slen[p]).astype(F32))
    at = iota((long_length, 1), 0)
    for p in range(long_count):
        parts.append((at < llen[p]).astype(F32))
    return jnp.concatenate(parts, axis=0)


def slabs_of(out, base, source, each, width):
    for j in range(source.shape[1] // width):
        out[base + j * each : base + (j + 1) * each] = source[:, j * width : (j + 1) * width]
    return base + source.shape[1] // width * each


def pack_body(wqkv, wo, wup, wdown, *rest):
    vectors, out = rest[:-1], rest[-1]
    each, width = wo.shape
    base = slabs_of(out, 0, wqkv, each, width)
    base = slabs_of(out, base, wo, each, width)
    out[base : base + 8] = jnp.zeros((8, width), BF16)
    for i, v in enumerate(vectors[:-1]):
        out[base : base + 1, i * each : (i + 1) * each] = v[...]
    out[base + 1 : base + 2, : vectors[-1].shape[1]] = vectors[-1][...]
    base = slabs_of(out, base + 8, wup, each, width)
    out[base:] = wdown[...]


def pack(wqkv, wo, wup, wdown, vectors, ub):
    each, width = wo.shape
    rows = wqkv.shape[1] // width * each + each + 8 + 2 * wdown.shape[0]
    return pl.pallas_call(
        pack_body,
        out_shape=jax.ShapeDtypeStruct((rows, width), BF16),
        compiler_params=params(58),
        name="pack",
    )(wqkv, wo, wup, wdown, *[v[None] for v in vectors], ub[None])


STEPS = (0, -1, 1, 2)


def gathered_at(pos, other, k, i):
    core = pos[2] ^ other
    x0, z0 = (pos[0] + STEPS[k]) & (RING - 1), (pos[1] + STEPS[i]) & (RING - 1)
    x1, z1 = (pos[0] + STEPS[i]) & (RING - 1), (pos[1] + STEPS[k]) & (RING - 1)
    return jnp.where(core == 0, (x0 * RING + z0) * 2, (x1 * RING + z1) * 2 + 1)


def arrivals(pos, pieces, target, sems, at):
    copies = []
    for other in range(2):
        for k in range(RING):
            for i in range(RING):
                n = (other * RING + k) * RING + i
                copies.append(
                    pltpu.make_async_copy(
                        pieces[other * RING + k].at[i, at], target.at[gathered_at(pos, other, k, i), at], sems.at[n]
                    )
                )
    return copies


def attention_forward_body(
    dims, slen, llen, pos, xs, xl, p0, p1, p2, p3, p4, p5, p6, p7,
    q_o, k_o, v_o, c_o, ps_o, pl_o, n_o, r_o, vecs_o, ub_o, gathered_o,
    x_all, total, wo_all, gathered, sems, out_sem,
):
    step = pl.program_id(0)
    short_rows, width = dims[0], x_all.shape[1]
    cols = q_o.shape[1]
    each = width // SHARDS
    keep_all = pltpu.make_async_copy(gathered, gathered_o, out_sem)

    @pl.when(step == 0)
    def _():
        copies = arrivals(pos, (p0, p1, p2, p3, p4, p5, p6, p7), gathered, sems, slice(None))
        for copy in copies:
            copy.start()
        x_all[:short_rows, :] = xs[...]
        x_all[short_rows:, :] = xl[...]
        total[...] = jnp.zeros_like(total)
        for copy in copies:
            copy.wait()
        keep_all.start()
        wo_all[...] = gathered[:, 3 * each : 4 * each].reshape(width, width)
        packed = gathered[:, 4 * each :]
        line = packed[:, 0, : 8 * each + 64]
        rest = column_rest(line.shape[1], width, each)
        mine = spread(SHARDS, width)
        for i in range(8):
            pick = (iota(rest.shape, 0) == rest + i * each).astype(BF16)
            row = jnp.sum(jnp.where(mine, nn(line, pick), 0.0), axis=0, keepdims=True)
            vecs_o[i : i + 1] = row.astype(BF16)
        inner = ub_o.shape[1]
        line = packed[:, 1, :128]
        pick = (iota((128, inner), 0) == column_rest(128, inner, inner // SHARDS)).astype(BF16)
        row = jnp.sum(jnp.where(spread(SHARDS, inner), nn(line, pick), 0.0), axis=0, keepdims=True)
        ub_o[...] = row.astype(BF16)

    x = x_all[...]
    at_cols = pl.ds(pl.multiple_of(step * cols, cols), cols)
    wq, wk, wv = (gathered[:, i * each : (i + 1) * each, at_cols].reshape(width, cols) for i in range(3))
    q_o[...] = (nn(x, wq) + vecs_o[QB : QB + 1, at_cols].astype(F32)).astype(BF16)
    k_o[...] = nn(x, wk).astype(BF16)
    v_o[...] = (nn(x, wv) + vecs_o[VB : VB + 1, at_cols].astype(F32)).astype(BF16)
    for first, rows, long_at in segments(dims):
        bias = key_bias(slen, llen, dims[3], rows, long_at)
        at = slice(first, first + rows)
        for pair in range(cols // PAIR):
            lanes = slice(pair * PAIR, (pair + 1) * PAIR)
            q = q_o[at, lanes] * jnp.asarray(HEAD_DIM**-0.5, BF16)
            scores = nt(two_heads(k_o[at, lanes]), q)
            probs = []
            for h in range(2):
                s = scores[h * rows : (h + 1) * rows] + bias
                e = jnp.exp(s - jnp.max(s, axis=0, keepdims=True))
                probs.append((e * (1.0 / jnp.sum(e, axis=0, keepdims=True))).astype(BF16))
            probs = jnp.concatenate(probs, axis=0)
            if long_at is None:
                ps_o[pair] = probs
            else:
                pl_o[long_at, pair] = probs
            c_o[at, lanes] = tn(probs, two_heads(v_o[at, lanes])).astype(BF16)
    total[...] += nn(c_o[...], wo_all[at_cols, :])

    @pl.when(step == pl.num_programs(0) - 1)
    def _():
        h = x_all[...].astype(F32) + (total[...] + row_of(vecs_o, OB))
        unit, inverse = normalized(h)
        n_o[...] = unit
        r_o[...] = inverse
        keep_all.wait()


def attention_forward(slen, llen, pos, xs, xl, pieces, inner, dims):
    rows, width = xs.shape[0] + xl.shape[0], xs.shape[1]
    short_rows, long_count, long_length, _ = dims
    step = 256
    steps, pairs = width // step, width // PAIR
    per = step // PAIR
    each_all = pieces[0].shape[1]
    cols = pl.BlockSpec((rows, step), lambda g, *_: (0, g))
    return pl.pallas_call(
        functools.partial(attention_forward_body, dims),
        grid_spec=pltpu.PrefetchScalarGridSpec(
            num_scalar_prefetch=3,
            grid=(steps,),
            in_specs=[
                whole(*xs.shape), whole(*xl.shape), *[pl.BlockSpec(memory_space=pl.ANY)] * 8,
            ],
            out_specs=[
                cols, cols, cols, cols,
                pl.BlockSpec((per, 2 * short_rows, short_rows), lambda g, *_: (g, 0, 0)),
                pl.BlockSpec((long_count, per, 2 * long_length, long_length), lambda g, *_: (0, g, 0, 0)),
                whole(rows, width), whole(rows, 1), whole(8, width), whole(1, inner),
                pl.BlockSpec(memory_space=pl.ANY),
            ],
            scratch_shapes=[
                pltpu.VMEM((rows, width), BF16), pltpu.VMEM((rows, width), F32), pltpu.VMEM((width, width), BF16),
                pltpu.VMEM((SHARDS, each_all, width), BF16), pltpu.SemaphoreType.DMA((SHARDS,)),
                pltpu.SemaphoreType.DMA(()),
            ],
        ),
        out_shape=[
            *[jax.ShapeDtypeStruct((rows, width), BF16)] * 4,
            jax.ShapeDtypeStruct((pairs, 2 * short_rows, short_rows), BF16),
            jax.ShapeDtypeStruct((long_count, pairs, 2 * long_length, long_length), BF16),
            jax.ShapeDtypeStruct((rows, width), F32),
            jax.ShapeDtypeStruct((rows, 1), F32),
            jax.ShapeDtypeStruct((8, width), BF16),
            jax.ShapeDtypeStruct((1, inner), BF16),
            jax.ShapeDtypeStruct((SHARDS, each_all, width), BF16),
        ],
        compiler_params=params(58),
        cost_estimate=cost(8 * rows * width * width, 20e6),
        name="attention_forward",
    )(slen, llen, pos, xs, xl, *pieces)


HBM = pl.BlockSpec(memory_space=pl.ANY)
ON_CHIP = pl.BlockSpec(memory_space=pltpu.VMEM)
SCALARS = pl.BlockSpec(memory_space=pltpu.SMEM)


class Copies:
    def __init__(self, sems):
        self.sems, self.used, self.open = sems, 0, []

    def start(self, source, target):
        copy = pltpu.make_async_copy(source, target, self.sems.at[self.used])
        self.used += 1
        copy.start()
        return copy

    def send(self, source, target):
        self.open.append(self.start(source, target))

    def finish(self):
        for copy in self.open:
            copy.wait()


def feed_body(
    dims, slen, llen, pos, unit1, cot_s, cot_l, inv1, ub, vecs, p0, p1, p2, p3, p4, p5, p6, p7,
    keep, give, outs_o, outl_o, gfs_o, gatt_o, sums_o, dub_o,
    wup, wdown, unit_v, cot_v, low_v, low_t, hidden, gelu_v, grad_v, gffn, out_v, gatt, valid_v,
    keep_dv, give_dv, keep_uv, give_uv, sems, piece_sems, down_sems, up_sems,
):
    short_rows = dims[0]
    rows, width = low_v.shape
    parts, block = hidden.shape[0], hidden.shape[2]
    each, tall = width // SHARDS, block * parts // SHARDS
    owners, lanes, tile = SHARDS // parts, 256, 128
    copies = Copies(sems)
    pieces = (p0, p1, p2, p3, p4, p5, p6, p7)
    unit_here = copies.start(unit1, unit_v)
    groups = [[], [], []]
    for other in range(2):
        for k in range(RING):
            for i in range(RING):
                n = (other * RING + k) * RING + i
                at = gathered_at(pos, other, k, i)
                source = pieces[other * RING + k]
                half = parts // 2
                targets = (wup.at[:half, at], wup.at[half:, at], wdown.at[at])
                sources = (source.at[i, :half], source.at[i, half:parts], source.at[i, parts:])
                for group, sem, src, target in zip(groups, range(3), sources, targets):
                    group.append(pltpu.make_async_copy(src, target, piece_sems.at[sem, n]))
    for copy in groups[0]:
        copy.start()
    valid_v[...] = valid_rows(slen, llen, dims)
    grad_v[...] = jnp.zeros_like(grad_v)
    unit_here.wait()

    @pl.loop(0, rows // tile)
    def _(r):
        at = pl.ds(pl.multiple_of(r * tile, tile), tile)
        low_v[at] = (unit_v[at] * row_of(vecs, G1) + row_of(vecs, S1)).astype(BF16)

    @pl.loop(0, parts)
    def _(j):
        for n in range(2):

            @pl.when(j == n * (parts // 2))
            def _():
                for copy in groups[n]:
                    copy.wait()
                for copy in groups[n + 1]:
                    copy.start()

        bias = ub[:, pl.ds(pl.multiple_of(j * block, block), block)].astype(F32)
        pre = nn(low_v[...], wup[j].reshape(width, block)) + bias
        cdf = 0.5 + 0.5 * lax.erf(pre * (0.5**0.5))
        density = jnp.exp(-0.5 * pre * pre) * (0.5 / jnp.pi) ** 0.5
        hidden[j] = (pre * cdf).astype(BF16)
        gelu_v[j] = (cdf + pre * density).astype(BF16)

    for copy in groups[2]:
        copy.wait()
    cots_here = copies.start(cot_s, cot_v.at[:short_rows]), copies.start(cot_l, cot_v.at[short_rows:])

    @pl.loop(0, parts)
    def _(j):
        grad_v[...] += nn(hidden[j], wdown[pl.ds(j * owners, owners)].reshape(block, width))

    for copy in cots_here:
        copy.wait()
    sums_o[...] = jnp.zeros_like(sums_o)

    @pl.loop(0, rows // tile)
    def _(r):
        at = pl.ds(pl.multiple_of(r * tile, tile), tile)
        first = unit_v[at] * row_of(vecs, G1) + row_of(vecs, S1)
        unit, inverse = normalized(first + (grad_v[at] + row_of(vecs, DB)))
        valid = valid_v[at]
        out_v[at] = ((unit * row_of(vecs, G2) + row_of(vecs, S2)) * valid).astype(BF16)
        cot = cot_v[at].astype(F32) * valid
        back = norm_back(cot * row_of(vecs, G2), unit, inverse)
        grad_v[at] = back
        low_back = back.astype(BF16)
        gffn[at] = low_back
        sums_o[DB : DB + 1] += jnp.sum(low_back.astype(F32), axis=0, keepdims=True)
        sums_o[G2 : G2 + 1] += jnp.sum(cot * unit, axis=0, keepdims=True)
        sums_o[S2 : S2 + 1] += jnp.sum(cot, axis=0, keepdims=True)

    copies.send(out_v.at[:short_rows], outs_o)
    copies.send(out_v.at[short_rows:], outl_o)
    on_first = pos[2] == 0

    def down_copies(at, p0, p1):
        return (
            pltpu.make_async_copy(keep_dv.at[at], keep.at[jnp.where(on_first, p0, p1), :parts], down_sems.at[0, at]),
            pltpu.make_async_copy(give_dv.at[at], give.at[jnp.where(on_first, p1, p0), :parts], down_sems.at[1, at]),
        )

    @pl.loop(0, RING)
    def _(x):
        grad = tn(hidden[x], gffn[...]).astype(BF16)
        for z in range(RING):
            place = x * RING + z
            even, odd = grad[2 * z * tall : (2 * z + 1) * tall], grad[(2 * z + 1) * tall : (2 * z + 2) * tall]
            keep_dv[place] = jnp.where(on_first, even, odd).reshape(parts, each, width)
            give_dv[place] = jnp.where(on_first, odd, even).reshape(parts, each, width)
            for copy in down_copies(place, *places(pos, x, z)):
                copy.start()

    def up_copies(j):
        return (
            pltpu.make_async_copy(keep_uv.at[j], keep.at[:, parts + j], up_sems.at[0, j]),
            pltpu.make_async_copy(give_uv.at[j], give.at[:, parts + j], up_sems.at[1, j]),
        )

    low_t[:width] = low_v[...].T
    low_t[width:] = jnp.ones((16, rows), BF16)

    @pl.loop(0, parts)
    def _(j):
        weight = wdown[pl.ds(j * owners, owners)].reshape(block, width)
        up = (nt(gffn[...], weight) * gelu_v[j].astype(F32)).astype(BF16)
        hidden[j] = up
        grad = nn(low_t[...], hidden[j])
        dub_o[:, pl.ds(pl.multiple_of(j * block, block), block)] = grad[width : width + 1]
        deal(keep_uv.at[j], give_uv.at[j], pos, grad[:width].astype(BF16), slice(None), each)
        for copy in up_copies(j):
            copy.start()

    @pl.loop(0, parts)
    def _(j):
        grad_v[...] += nt(hidden[j], wup[j].reshape(width, block))

    @pl.loop(0, rows // tile)
    def _(r):
        at = pl.ds(pl.multiple_of(r * tile, tile), tile)
        grad, unit = grad_v[at], unit_v[at]
        back = norm_back(grad * row_of(vecs, G1), unit, inv1[at])
        grad_v[at] = back
        low_back = back.astype(BF16)
        gatt[at] = low_back
        sums_o[OB : OB + 1] += jnp.sum(low_back.astype(F32), axis=0, keepdims=True)
        sums_o[G1 : G1 + 1] += jnp.sum(grad * unit, axis=0, keepdims=True)
        sums_o[S1 : S1 + 1] += jnp.sum(grad, axis=0, keepdims=True)

    copies.send(gatt, gatt_o)
    copies.send(grad_v, gfs_o)
    for at in range(CHIPS):
        for copy in down_copies(at, at, at):
            copy.wait()
    for j in range(parts):
        for copy in up_copies(j):
            copy.wait()
    copies.finish()


def feed(slen, llen, pos, unit1, cot_s, cot_l, inv1, ub, vecs, pieces, dims):
    rows, width = unit1.shape
    inner = ub.shape[1]
    parts = RING
    block, tall, each = inner // parts, inner // SHARDS, width // SHARDS
    down, up = (CHIPS, parts, each, width), (parts, CHIPS, each, width)
    return pl.pallas_call(
        functools.partial(feed_body, dims),
        in_specs=[SCALARS] * 3 + [HBM] * 3 + [ON_CHIP] * 3 + [HBM] * 8,
        out_specs=[HBM] * 6 + [ON_CHIP] * 2,
        scratch_shapes=[
            pltpu.VMEM((parts, SHARDS, each, width), BF16), pltpu.VMEM((SHARDS, parts, each, width), BF16),
            pltpu.VMEM((rows, width), F32), pltpu.VMEM((rows, width), BF16), pltpu.VMEM((rows, width), BF16),
            pltpu.VMEM((width + 16, rows), BF16), pltpu.VMEM((parts, rows, block), BF16),
            pltpu.VMEM((parts, rows, block), BF16), pltpu.VMEM((rows, width), F32), pltpu.VMEM((rows, width), BF16),
            pltpu.VMEM((rows, width), BF16), pltpu.VMEM((rows, width), BF16), pltpu.VMEM((rows, 1), F32),
            pltpu.VMEM(down, BF16), pltpu.VMEM(down, BF16), pltpu.VMEM(up, BF16), pltpu.VMEM(up, BF16),
            pltpu.SemaphoreType.DMA((8,)), pltpu.SemaphoreType.DMA((3, SHARDS)),
            pltpu.SemaphoreType.DMA((2, CHIPS)), pltpu.SemaphoreType.DMA((2, parts)),
        ],
        out_shape=[
            *[jax.ShapeDtypeStruct((CHIPS, 2 * parts, each, width), BF16)] * 2,
            jax.ShapeDtypeStruct(cot_s.shape, BF16),
            jax.ShapeDtypeStruct(cot_l.shape, BF16),
            jax.ShapeDtypeStruct((rows, width), F32),
            jax.ShapeDtypeStruct((rows, width), BF16),
            jax.ShapeDtypeStruct((8, width), F32),
            jax.ShapeDtypeStruct((1, inner), F32),
        ],
        compiler_params=params(58),
        cost_estimate=cost(12 * rows * width * inner, 30e6),
        name="feed",
    )(slen, llen, pos, unit1, cot_s, cot_l, inv1, ub, vecs, *pieces)


def attention_back_body(dims, gatt, wo_block, q, k, v, ps, plong, dq_o, dk_o, dv_o, gc, wo_all):
    step = pl.program_id(0)
    width, cols = gatt.shape[1], q.shape[1]
    at_cols = pl.ds(pl.multiple_of(step * cols, cols), cols)

    @pl.when(step == 0)
    def _():
        wo_all[...] = wo_block[...].reshape(width, width)

    gc[...] = nt(gatt[...], wo_all[at_cols, :]).astype(BF16)
    scale = HEAD_DIM**-0.5
    for first, rows, long_at in segments(dims):
        at = slice(first, first + rows)
        for pair in range(cols // PAIR):
            lanes = slice(pair * PAIR, (pair + 1) * PAIR)
            probs = ps[pair] if long_at is None else plong[long_at, pair]
            grad = gc[at, lanes]
            dp = nt(two_heads(v[at, lanes]), grad)
            ds = []
            for h in range(2):
                half = slice(h * rows, (h + 1) * rows)
                p = probs[half].astype(F32)
                d = dp[half]
                ds.append((p * (d - jnp.sum(d * p, axis=0, keepdims=True))).astype(BF16))
            ds = jnp.concatenate(ds, axis=0)
            dv_o[at, lanes] = own_lanes(nn(probs, grad)).astype(BF16)
            dk_o[at, lanes] = (own_lanes(nn(ds, q[at, lanes])) * scale).astype(BF16)
            dq_o[at, lanes] = (tn(ds, two_heads(k[at, lanes])) * scale).astype(BF16)


def attention_back(gatt, gathered, q, k, v, ps, plong, dims):
    rows, width = gatt.shape
    short_rows, long_count, long_length, _ = dims
    step = 256
    per = step // PAIR
    cols = pl.BlockSpec((rows, step), lambda g: (0, g))
    return pl.pallas_call(
        functools.partial(attention_back_body, dims),
        grid=(width // step,),
        in_specs=[
            whole(rows, width),
            pl.BlockSpec((SHARDS, width // SHARDS, width), lambda g: (0, 3, 0)),
            cols, cols, cols,
            pl.BlockSpec((per, 2 * short_rows, short_rows), lambda g: (g, 0, 0)),
            pl.BlockSpec((long_count, per, 2 * long_length, long_length), lambda g: (0, g, 0, 0)),
        ],
        out_specs=[cols, cols, cols],
        scratch_shapes=[pltpu.VMEM((rows, step), BF16), pltpu.VMEM((width, width), BF16)],
        out_shape=[jax.ShapeDtypeStruct((rows, width), BF16)] * 3,
        compiler_params=params(BACK_MIB),
        cost_estimate=cost(8 * rows * width * width, 15e6),
        name="attention_back",
    )(gatt, gathered, q, k, v, ps, plong)


def weight_back_body(
    dims, pos, gatt_cols, c, dq, dk, dv, xs, xl, sums_f, dub,
    keep, g0, g1, g2, g3,
    x_t, c_t, sums, spare,
):
    gives = (g0, g1, g2, g3)
    step = pl.program_id(0)
    short_rows = dims[0]
    rows, width = c.shape
    cols = dq.shape[1]
    each = width // SHARDS
    at_cols = pl.ds(pl.multiple_of(step * cols, cols), cols)

    @pl.when(step == 0)
    def _():
        x_t[:width, :short_rows] = xs[...].T
        x_t[:width, short_rows:] = xl[...].T
        x_t[width:] = jnp.ones((16, rows), BF16)
        c_t[...] = c[...].T
        sums[...] = sums_f[...]

    deal_apart(keep, gives, spare, pos, nn(c_t[...], gatt_cols[...]).astype(BF16), slice(3 * each, 4 * each), each)
    for i, d in enumerate((dq, dk, dv)):
        grad = nn(x_t[...], d[...])
        deal_apart(keep, gives, spare, pos, grad[:width].astype(BF16), slice(i * each, (i + 1) * each), each)
        if i != 1:
            at = QB if i == 0 else VB
            sums[at : at + 1, at_cols] = grad[width : width + 1]
    keep[:, 4 * each :] = jnp.zeros((CHIPS, 8, cols), BF16)
    for give in gives:
        give[:, 4 * each :] = jnp.zeros((RING, 8, cols), BF16)

    @pl.when(step == pl.num_programs(0) - 1)
    def _():
        mine = spread(SHARDS, width)
        rest = column_rest(cols, width, each)
        line = jnp.zeros((SHARDS, cols), F32)
        for i in range(8):
            put = (iota(rest.shape, 0) == rest + i * each).astype(BF16)
            line += nt(jnp.where(mine, sums[i : i + 1], 0.0).astype(BF16), put)
        inner = dub.shape[1]
        put = (iota((cols, inner), 0) == column_rest(cols, inner, inner // SHARDS)).astype(BF16)
        wide = nt(jnp.where(spread(SHARDS, inner), dub[...], 0.0).astype(BF16), put)
        both = jnp.concatenate([line[:, None], wide[:, None], jnp.zeros((SHARDS, 6, cols), F32)], axis=1)
        deal_apart(keep, gives, spare, pos, both.reshape(SHARDS * 8, cols).astype(BF16), slice(4 * each, 4 * each + 8), 8)


def weight_back(pos, gatt, c, dq, dk, dv, xs, xl, sums_f, dub, dims):
    rows, width = gatt.shape
    each = width // SHARDS
    step = 256
    cols = pl.BlockSpec((rows, step), lambda g, *_: (0, g))
    dealt = pl.BlockSpec((CHIPS, 4 * each + 8, step), lambda g, *_: (0, 0, g))
    return pl.pallas_call(
        functools.partial(weight_back_body, dims),
        grid_spec=pltpu.PrefetchScalarGridSpec(
            num_scalar_prefetch=1,
            grid=(width // step,),
            in_specs=[
                cols, whole(rows, width), cols, cols, cols,
                whole(*xs.shape), whole(*xl.shape), whole(8, width), whole(*dub.shape),
            ],
            out_specs=[dealt, *[pl.BlockSpec((RING, 4 * each + 8, step), lambda g, *_: (0, 0, g))] * RING],
            scratch_shapes=[
                pltpu.VMEM((width + 16, rows), BF16), pltpu.VMEM((width, rows), BF16), pltpu.VMEM((8, width), F32),
                pltpu.VMEM((CHIPS, each, step), BF16),
            ],
        ),
        out_shape=[
            jax.ShapeDtypeStruct((CHIPS, 4 * each + 8, width), BF16),
            *[jax.ShapeDtypeStruct((RING, 4 * each + 8, width), BF16)] * RING,
        ],
        compiler_params=params(BACK_MIB),
        cost_estimate=cost(8 * rows * width * width, 12e6),
        name="weight_back",
    )(pos, gatt, c, dq, dk, dv, xs, xl, sums_f, dub)


def input_back_body(dims, gfs, dq, dk, dv, wq, wk, wv, gs_o, gl_o, total):
    step = pl.program_id(0)
    short_rows, width, cols = dims[0], gfs.shape[1], dq.shape[1]
    part = (
        nt(dq[...], wq[...].reshape(width, cols))
        + nt(dk[...], wk[...].reshape(width, cols))
        + nt(dv[...], wv[...].reshape(width, cols))
    )

    @pl.when(step == 0)
    def _():
        total[...] = gfs[...] + part

    @pl.when(step > 0)
    def _():
        total[...] += part

    @pl.when(step == pl.num_programs(0) - 1)
    def _():
        gs_o[...] = total[:short_rows]
        gl_o[...] = total[short_rows:]


def input_back(gfs, dq, dk, dv, gathered, dims):
    rows, width = gfs.shape
    each = width // SHARDS
    step = 256
    short_rows = dims[0]
    cols = pl.BlockSpec((rows, step), lambda g: (0, g))
    slab = lambda i: pl.BlockSpec((SHARDS, each, step), lambda g: (0, i, g))
    return pl.pallas_call(
        functools.partial(input_back_body, dims),
        grid=(width // step,),
        in_specs=[whole(rows, width), cols, cols, cols, slab(0), slab(1), slab(2)],
        out_specs=[whole(short_rows, width), whole(rows - short_rows, width)],
        scratch_shapes=[pltpu.VMEM((rows, width), F32)],
        out_shape=[
            jax.ShapeDtypeStruct((short_rows, width), F32),
            jax.ShapeDtypeStruct((rows - short_rows, width), F32),
        ],
        compiler_params=params(16),
        cost_estimate=cost(6 * rows * width * width, 12e6),
        name="input_back",
    )(gfs, dq, dk, dv, gathered, gathered, gathered)


def pair_sum(keep, got):
    parts = []
    for d in range(RING):
        at = slice(d * RING, (d + 1) * RING)
        parts.append((keep[at].astype(F32) + got[at].astype(F32)).astype(BF16))
    return parts


def pair_sum_apart(keep, gots):
    return [
        (keep[d * RING : (d + 1) * RING].astype(F32) + got.astype(F32)).astype(BF16) for d, got in enumerate(gots)
    ]


def four_sum(own, left, right, far):
    return (own.astype(F32) + far.astype(F32)) + (left.astype(F32) + right.astype(F32))


def turn(delta, stage):
    moves = []
    for x in range(RING):
        for z in range(RING):
            for core in range(2):
                to_x, to_z = x, z
                if (core == 0) == (stage == 0):
                    to_x = (x + delta) % RING
                else:
                    to_z = (z + delta) % RING
                moves.append(((x * RING + z) * 2 + core, (to_x * RING + to_z) * 2 + core))
    return moves


def swap_cores(v):
    return lax.ppermute(v, "shard", [(i, i ^ 1) for i in range(SHARDS)])


def around(v, stage):
    return tuple(lax.ppermute(v[d] if isinstance(v, (list, tuple)) else v, "shard", turn(d, stage)) for d in (1, 3, 2))


def both_cores(pieces):
    return (*pieces, *(swap_cores(p) for p in pieces))


def second_turn(own, left, right, far):
    parts = [four_sum(own[d], left[d], right[d], far[d]).astype(BF16) for d in range(RING)]
    return parts[0], *around(parts, 1)


def across_replicas(own):
    return own, *(lax.ppermute(own, "rep", [(i, (i + d) % RING) for i in range(RING)]) for d in (1, 3, 2))


def replica_sum(own, left, right, far, at):
    return (own[at].astype(F32) + far[at].astype(F32)) + (left[at].astype(F32) + right[at].astype(F32))


def finish_attention_body(own, left, right, far, wqkv_o, wo_o, *vector_os):
    each, width = wo_o.shape
    for j in range(wqkv_o.shape[1] // width):
        at = slice(j * each, (j + 1) * each)
        wqkv_o[:, j * width : (j + 1) * width] = replica_sum(own, left, right, far, at)
    wo_o[...] = replica_sum(own, left, right, far, slice(3 * each, 4 * each))
    last = replica_sum(own, left, right, far, slice(4 * each, 4 * each + 8))[:, width - 256 :]
    for i, o in enumerate(vector_os[:-1]):
        o[...] = last[0:1, i * each : (i + 1) * each]
    o = vector_os[-1]
    o[...] = last[1:2, : o.shape[1]]


def finish_attention(arrays, tall):
    width = arrays[0].shape[1]
    each = width // SHARDS
    return pl.pallas_call(
        finish_attention_body,
        out_shape=[
            jax.ShapeDtypeStruct((each, 3 * width), F32),
            jax.ShapeDtypeStruct((each, width), F32),
            *[jax.ShapeDtypeStruct((1, each), F32)] * 8,
            jax.ShapeDtypeStruct((1, tall), F32),
        ],
        compiler_params=params(4),
        name="finish_attention",
    )(*arrays)


def finish_feed_body(own, left, right, far, up_o, down_o):
    parts = own.shape[0] // 2
    each, width = own.shape[1:]
    for j in range(parts):
        down_o[j * each : (j + 1) * each] = replica_sum(own, left, right, far, j)
        up_o[:, j * width : (j + 1) * width] = replica_sum(own, left, right, far, parts + j)


def finish_feed(arrays, each, inner, tall):
    width = arrays[0].shape[2]
    return pl.pallas_call(
        finish_feed_body,
        out_shape=[jax.ShapeDtypeStruct((each, inner), F32), jax.ShapeDtypeStruct((tall, width), F32)],
        compiler_params=params(4),
        name="finish_feed",
    )(*arrays)


def on_device(
    short_tokens, long_tokens, short_lengths, long_lengths, short_cotangent, long_cotangent,
    input_weight, query_bias, value_bias, output_weight, output_bias, first_gain, first_shift,
    up_weight, up_bias, down_weight, down_bias, second_gain, second_shift,
):
    short_count, short_length, width = short_tokens.shape
    long_count, long_length, _ = long_tokens.shape
    dims = (short_count * short_length, long_count, long_length, short_length)
    each, inner, tall = width // SHARDS, up_weight.shape[1], down_weight.shape[0]
    xs, xl = short_tokens.reshape(-1, width), long_tokens.reshape(-1, width)
    cs, cl = short_cotangent.reshape(-1, width), long_cotangent.reshape(-1, width)
    index = lax.axis_index("shard")
    pos = jnp.stack([index // 8, (index // 2) % 4, index % 2]).astype(jnp.int32)

    packed = pack(
        input_weight, output_weight, up_weight, down_weight,
        (query_bias, value_bias, output_bias, first_gain, first_shift, down_bias, second_gain, second_shift),
        up_bias,
    )
    near = (packed, *around(packed, 1))
    cut = 4 * each + 8
    near_a = jnp.stack([n[:cut] for n in near])
    near_f = jnp.stack([n[cut:].reshape(-1, each, width) for n in near])
    around_a = around(near_a, 0)
    far_f = around(near_f, 0)
    pieces_a = both_cores((near_a, *around_a))
    xs, near_f = lax.optimization_barrier((xs, near_f))
    q, k, v, c, ps, plong, unit1, inv1, vecs, ub, gathered_a = attention_forward(
        short_lengths, long_lengths, pos, xs, xl, pieces_a, inner, dims
    )
    unit1, *far_f = lax.optimization_barrier((unit1, *far_f))
    keep_f, give_f, out_s, out_l, gfs, gatt, sums_f, dub = feed(
        short_lengths, long_lengths, pos, unit1, cs, cl, inv1, ub, vecs, both_cores((near_f, *far_f)), dims
    )
    dq, dk, dv = attention_back(gatt, gathered_a, q, k, v, ps, plong, dims)
    parts_f = pair_sum(keep_f, swap_cores(give_f))
    dv, *parts_f = lax.optimization_barrier((dv, *parts_f))
    around_f = around(parts_f, 0)
    keep_a, *gives_a = weight_back(pos, gatt, c, dq, dk, dv, xs, xl, sums_f, dub, dims)
    keep_a, *around_f = lax.optimization_barrier((keep_a, *around_f))
    parts_a = pair_sum_apart(keep_a, [swap_cores(give) for give in gives_a])
    gfs, *parts_a = lax.optimization_barrier((gfs, *parts_a))
    around_a = around(parts_a, 0)
    grad_s, grad_l = input_back(gfs, dq, dk, dv, gathered_a, dims)
    grad_s, *around_a = lax.optimization_barrier((grad_s, *around_a))
    own_f = four_sum(*second_turn(parts_f[0], *around_f)).astype(BF16)
    _, *around_a = lax.optimization_barrier((own_f, *around_a))
    own_f, *others_f = across_replicas(own_f)
    last_a = second_turn(parts_a[0], *around_a)
    *last_a, far_f = lax.optimization_barrier((*last_a, others_f[2]))
    up, down = finish_feed((own_f, *others_f[:2], far_f), each, inner, tall)
    own_a = four_sum(*last_a).astype(BF16)
    w_in, w_out, *vectors = finish_attention(across_replicas(own_a), tall)
    vectors = [x.reshape(-1) for x in vectors]
    return (
        out_s.reshape(short_tokens.shape), out_l.reshape(long_tokens.shape),
        grad_s.reshape(short_tokens.shape), grad_l.reshape(long_tokens.shape),
        w_in, vectors[QB], vectors[VB], w_out, vectors[OB], vectors[G1], vectors[S1],
        up, vectors[8], down, vectors[DB], vectors[G2], vectors[S2],
    )


def solution(mesh):
    rows, flat = P(("rep", "shard"), None, None), P("shard")
    tall = P("shard", None)
    return jax.shard_map(
        on_device,
        mesh=mesh,
        in_specs=(
            rows, rows, P(("rep", "shard")), P(("rep", "shard")), rows, rows,
            tall, flat, flat, tall, flat, flat, flat, tall, flat, tall, flat, flat, flat,
        ),
        out_specs=(
            rows, rows, rows, rows,
            tall, flat, flat, tall, flat, flat, flat, tall, flat, tall, flat, flat, flat,
        ),
        check_vma=False,
    )
```
